128 devices in a mesh: tensor: 16 (over x, y_hi, core), seq: 4 (over z), dec: 2 (over y_lo).
Axes of the slice: x: 4, y: 4 (y_hi: 2, y_lo: 2; y = y_hi * 2 + y_lo), z: 4, core: 2. Of those that a mesh axis runs over, the one named last changes fastest.
Arguments:
- tokens: bfloat16 [2, 4, 1024, 2560], P('dec', 'seq', 'tensor'), may hold values from -320 to 320, as said below
- attn_gain: float32 [2560], replicated, may hold values from 0.1 to 1.9
- w_query: bfloat16 [2560, 2560], P(None, 'tensor'), may hold values from -2 to 8
- w_key: bfloat16 [2560, 640], replicated, may hold values from -2 to 8
- w_value: bfloat16 [2560, 640], replicated, may hold values from -4 to 4
- w_out: bfloat16 [2560, 2560], P('tensor'), may hold values from -0.125 to 0.125
- mlp_gain: float32 [2560], replicated, may hold values from 0.1 to 1.9
- w_gate: bfloat16 [2560, 6912], P(None, 'tensor'), may hold values from -0.125 to 0.125
- w_up: bfloat16 [2560, 6912], P(None, 'tensor'), may hold values from -0.125 to 0.125
- w_down: bfloat16 [6912, 2560], P('tensor'), may hold values from -0.078125 to 0.078125
- positions: int32 [2, 4, 1024], P('dec', 'seq'), may hold values from 0 to 4095, as said below
- window_lo: int32 [2, 4, 1024], P('dec', 'seq'), may hold values from 0 to 4095, as said below
- cache_pool: bfloat16 [320, 2, 16, 1280], P(('seq', 'dec'), None, 'tensor'), may hold values from -6 to 6
- req_len: int32 [8, 8], P(('seq', 'dec')), may hold values from 1 to 128, 512 in all within a row
- req_owner: int32 [64, 1], P(('seq', 'dec')), may hold values from 0 to 7, as said below
- block_list: int32 [8, 40], P(('seq', 'dec')), may hold values from 0 to 39, each once within a row
Outputs:
- layer_out: bfloat16 [2, 4, 1024, 2560], P('dec', 'seq', 'tensor')
- decode_cache: bfloat16 [128, 2, 16, 10240], P(('seq', 'dec'), None, 'tensor')
The draws below stay inside these ranges and needn't reach their ends.
Inputs may be any that keep to these rules, and one draw needn't show every extreme that they name: For the token at span index i: i - 4095 <= window_lo <= i; tokens of one document share their lower limit until the window binds. positions rise by one from token to token within a document. `req_len`: each source's 8 lengths sum to 512, and its longest is 128. `req_owner`: among the 8 requests of one source no owner is named more than 2 times, and one owner is named exactly 2 times by every source. Row-wise values of order one; some tokens may be far larger.
All inputs are finite; a program needn't handle non-finite values.
Results may differ from the reference program's by a relative error of at most 0.015.
Values may be sent and summed in bfloat16 or wider, within the bound.
A program may use at most 128 MiB of HBM per device.

```python
import math
import jax
import jax.numpy as jnp
import numpy as np
from jax import lax

D = 2560
QH = 32
KVH = 8
HD = 80
FF = 6912
WINDOW = 4096
TOK_BLOCK = 1024
CACHE_LAYERS = 2
BT = 16
MAXLEN = 128
RQ = 8
PAIR = 2
SEQS = 2
SEQ_BLOCKS = 4
SPAN = 4096
KVP = 16
OWNERS = 8
TOTAL = 512
NB = 40
POOL = 320
SLOTS = 128
N_TENSOR = 16


def draw_tokens(key, part):
    shape_all = (SEQS, SEQ_BLOCKS, TOK_BLOCK, D)
    key_base = jax.random.fold_in(key, 0)
    values = jax.random.normal(key_base, shape_all, jnp.float32)
    return values.astype(jnp.bfloat16)


def spiked_weight(key, columns):
    scale_in = D ** (-0.5)
    values = jnp.clip(jax.random.normal(key, (D, columns), jnp.float32), -6.0, 6.0) * scale_in
    return values.astype(jnp.bfloat16)


def draw_w_query(key, part):
    return spiked_weight(jax.random.fold_in(key, 31), QH * HD)


def draw_w_key(key, part):
    return spiked_weight(jax.random.fold_in(key, 37), KVH * HD)


def document_layout(key):
    base_key = jax.random.fold_in(key, 4711)
    key_cut = jax.random.fold_in(base_key, 0)
    index_all = jnp.broadcast_to(jnp.arange(SPAN, dtype=jnp.int32)[None, :], (SEQS, SPAN))
    cuts = jax.random.randint(key_cut, (SEQS, SPAN), 0, max(2, TOK_BLOCK // 2)) == 0
    cuts = cuts & (index_all >= 2 * TOK_BLOCK) | (index_all == 0) | (index_all == SPAN - 1)
    doc_start = lax.cummax(jnp.where(cuts, index_all, 0), axis=1)
    first_len = jnp.sum((doc_start == 0).astype(jnp.int32), axis=1, keepdims=True)
    offset = (SPAN - first_len).astype(jnp.int32)
    places = index_all - doc_start + jnp.where(doc_start == 0, offset, 0)
    lower = jnp.maximum(doc_start, index_all - WINDOW + 1)
    return (places.reshape(SEQS, SEQ_BLOCKS, TOK_BLOCK).astype(jnp.int32), lower.reshape(SEQS, SEQ_BLOCKS, TOK_BLOCK).astype(jnp.int32))


def draw_positions(key, part):
    return document_layout(key)[0]


def draw_window_lo(key, part):
    return document_layout(key)[1]


def draw_req_owner(key, part):
    hot_key, rest_key = jax.random.split(jax.random.fold_in(key, 17))
    hot_owner = jax.random.randint(hot_key, (), 0, OWNERS)

    def per_source(source_key):
        key_pick, key_order = jax.random.split(source_key)
        slot_ids = jax.random.permutation(key_pick, (OWNERS - 1) * PAIR)[:RQ - PAIR]
        others = slot_ids // PAIR
        others = others + (others >= hot_owner).astype(others.dtype)
        listed = jnp.concatenate([jnp.full((PAIR,), hot_owner, others.dtype), others])
        return listed[jax.random.permutation(key_order, RQ)]
    source_keys = jax.random.split(rest_key, OWNERS)
    return jax.vmap(per_source)(source_keys).reshape(OWNERS * RQ, 1).astype(jnp.int32)


def steps_of(own_key, shape, shards, least, high):
    def one(position, blocks):
        heights = jax.random.uniform(jax.random.fold_in(jax.random.fold_in(own_key, 6), position), (blocks,), jnp.float32, least / len(shards), high / len(shards))
        return jnp.repeat(jnp.exp(heights), shape[position] // blocks).reshape((-1,) + (1,) * (len(shape) - position - 1))

    loudness = one(*shards[0])
    for cut in shards[1:]:
        loudness = loudness * one(*cut)
    return loudness


def profile(amount, total, bound, lean):
    weights = [(1 << 20) // math.isqrt(grade ** lean) + 1 for grade in range(2, amount + 1)]
    rest, given = total - bound - (amount - 1), [1] * (amount - 1)
    while rest > 0:
        candidates = [i for i in range(amount - 1) if given[i] < bound]
        mass, left = sum([weights[i] for i in candidates]), rest
        for i in candidates:
            extra = min(bound - given[i], max(1, left * weights[i] // mass), rest)
            given[i] = given[i] + extra
            rest = rest - extra
    return np.array([bound] + given)


def uneven_parts(rng, count, total, reach, slope):
    if count == 2:
        one = jax.random.randint(rng, (), max(1, total - reach), min(reach, total - 1) + 1)
        return jnp.stack([one, total - one])
    sizes = jnp.asarray(profile(count, total, reach, slope), jnp.int32)
    pairs = (count - 1) // 2
    source_of, sink = sizes[1:1 + 2 * pairs:2], sizes[2:2 + 2 * pairs:2]
    room = jnp.minimum(source_of - 1, reach - sink)
    shifted = jax.random.randint(jax.random.fold_in(rng, 1), (pairs,), 0, 1 << 20) % (room + 1)
    sizes = sizes.at[1:1 + 2 * pairs:2].set(source_of - shifted).at[2:2 + 2 * pairs:2].set(sink + shifted)
    return sizes[jax.random.permutation(jax.random.fold_in(rng, 2), count)]


def scatter_about(own_key, shape, deviation, bound, cuts=(), kind=jnp.bfloat16):
    drawn = deviation * jax.random.normal(own_key, shape, jnp.float32)
    if cuts:
        drawn = drawn * steps_of(own_key, shape, cuts, -0.22, 0.18)
    return jnp.clip(drawn, -bound, bound).astype(kind)


def setup_inputs(seed: int = 0) -> dict:
    seeds = jax.random.split(jax.random.key(seed), 17)
    return {
        "tokens": draw_tokens(jax.random.fold_in(seeds[16], 71), 0),
        "attn_gain": jnp.clip(1.0 + 0.18 * jax.random.normal(seeds[1], (D,), jnp.float32), 0.1, 1.9),
        "w_query": draw_w_query(jax.random.fold_in(seeds[16], 71), 0),
        "w_key": draw_w_key(jax.random.fold_in(seeds[16], 71), 0),
        "w_value": scatter_about(seeds[4], (D, KVH * HD), 0.3, 4.0),
        "w_out": scatter_about(seeds[5], (QH * HD, D), (QH * HD) ** -0.5, 0.125, ((0, 16),)),
        "mlp_gain": jnp.clip(1.0 + 0.18 * jax.random.normal(seeds[6], (D,), jnp.float32), 0.1, 1.9),
        "w_gate": scatter_about(seeds[7], (D, FF), D ** -0.5, 0.125, ((1, 16),)),
        "w_up": scatter_about(seeds[8], (D, FF), D ** -0.5, 0.125, ((1, 16),)),
        "w_down": scatter_about(seeds[9], (FF, D), FF ** -0.5, 0.078125, ((0, 16),)),
        "positions": draw_positions(jax.random.fold_in(seeds[16], 71), 0),
        "window_lo": draw_window_lo(jax.random.fold_in(seeds[16], 71), 0),
        "cache_pool": scatter_about(seeds[12], (POOL, CACHE_LAYERS, KVP, BT * HD), 1.0, 6.0, ((0, 8), (2, 16))),
        "req_len": jax.vmap(lambda own: uneven_parts(own, RQ, TOTAL, MAXLEN, 2))(jax.random.split(seeds[13], OWNERS)).reshape((OWNERS, RQ)).astype(jnp.int32),
        "req_owner": draw_req_owner(jax.random.fold_in(seeds[16], 71), 0),
        "block_list": jax.vmap(lambda own: jax.random.permutation(own, NB))(jax.random.split(seeds[15], OWNERS)).reshape((OWNERS, NB)).astype(jnp.int32),
    }


norm_eps = 1e-05
rope_base = 10000.0

def rms_scale(row_block, gain_vec):
    values = row_block.astype(jnp.float32)
    mean_square = lax.optimization_barrier(jnp.mean(values * values, axis=-1, keepdims=True))
    return values * lax.rsqrt(mean_square + norm_eps) * gain_vec.astype(jnp.float32)

def rotate(values, places):
    half_dim = values.shape[-1] // 2
    inverse_rate = jnp.power(jnp.float32(rope_base), -(2.0 * jnp.arange(half_dim, dtype=jnp.float32)) / values.shape[-1])
    angles = places.astype(jnp.float32)[:, None] * inverse_rate[None, :]
    cosine = jnp.cos(angles)[:, None, :]
    sine_vals = jnp.sin(angles)[:, None, :]
    first_half = values[..., :half_dim]
    second = values[..., half_dim:]
    return jnp.concatenate([first_half * cosine - second * sine_vals, second * cosine + first_half * sine_vals], axis=-1)

def shard_sum(left, right, width):
    accum = jnp.zeros((left.shape[0], right.shape[1]), jnp.float32)
    for shard_num in range(left.shape[1] // width):
        part_sum = jnp.dot(left[:, shard_num * width:(shard_num + 1) * width], right[shard_num * width:(shard_num + 1) * width], preferred_element_type=jnp.float32)
        rounded = lax.optimization_barrier(part_sum.astype(jnp.bfloat16))
        accum = accum + rounded.astype(jnp.float32)
    return accum

def attend(queries, keys_rot, values_in, lower):
    qblock = min(512, TOK_BLOCK)
    group_size = QH // KVH
    padded_keys = jnp.concatenate([jnp.zeros((WINDOW, KVH, HD), jnp.bfloat16), keys_rot], axis=0)
    padded_values = jnp.concatenate([jnp.zeros((WINDOW, KVH, HD), jnp.bfloat16), values_in], axis=0)

    def one_block(block_begin):
        q_part = lax.dynamic_slice_in_dim(queries, block_begin, qblock, 0).reshape(qblock, KVH, group_size, HD)
        k_part = lax.dynamic_slice_in_dim(padded_keys, block_begin, WINDOW + qblock, 0)
        v_part = lax.dynamic_slice_in_dim(padded_values, block_begin, WINDOW + qblock, 0)
        scores = jnp.einsum('qcgd,kcd->cgqk', q_part.astype(jnp.float32), k_part.astype(jnp.float32)) * HD ** (-0.5)
        query_pos = block_begin + jnp.arange(qblock, dtype=jnp.int32)
        key_pos = block_begin - WINDOW + jnp.arange(WINDOW + qblock, dtype=jnp.int32)
        low_bound = lax.dynamic_slice_in_dim(lower, block_begin, qblock, 0)
        visible = (key_pos[None, :] >= low_bound[:, None]) & (key_pos[None, :] <= query_pos[:, None])
        scores = jnp.where(visible[None, None], scores, -jnp.inf)
        row_top = lax.optimization_barrier(jnp.max(scores, axis=-1, keepdims=True))
        exp_scores = jnp.exp(scores - row_top)
        row_total = lax.optimization_barrier(jnp.sum(exp_scores, axis=-1, keepdims=True))
        weights = (exp_scores / row_total).astype(jnp.bfloat16)
        mixed_vals = jnp.einsum('cgqk,kcd->qcgd', weights.astype(jnp.float32), v_part.astype(jnp.float32))
        return mixed_vals.reshape(qblock, QH * HD).astype(jnp.bfloat16)
    block_starts = jnp.arange(SPAN // qblock, dtype=jnp.int32) * qblock
    return lax.map(one_block, block_starts).reshape(SPAN, QH * HD)

def layer_span(row_block, attn_gain, w_query, w_key, w_value, w_out, mlp_gain, w_gate, w_up, w_down, places, lower):
    normed_in = rms_scale(row_block, attn_gain).astype(jnp.bfloat16)
    queries = rotate(jnp.dot(normed_in, w_query, preferred_element_type=jnp.float32).reshape(SPAN, QH, HD), places).astype(jnp.bfloat16)
    keys_rot = rotate(jnp.dot(normed_in, w_key, preferred_element_type=jnp.float32).reshape(SPAN, KVH, HD), places).astype(jnp.bfloat16)
    values_in = jnp.dot(normed_in, w_value, preferred_element_type=jnp.float32).reshape(SPAN, KVH, HD).astype(jnp.bfloat16)
    heads = attend(queries, keys_rot, values_in, lower)
    attn = shard_sum(heads, w_out, QH * HD // N_TENSOR)
    residual = row_block.astype(jnp.float32) + attn
    mixed_in = rms_scale(residual, mlp_gain).astype(jnp.bfloat16)
    gate_vals = jnp.dot(mixed_in, w_gate, preferred_element_type=jnp.float32)
    up_vals = jnp.dot(mixed_in, w_up, preferred_element_type=jnp.float32)
    hidden = (jax.nn.silu(gate_vals) * up_vals).astype(jnp.bfloat16)
    return (residual + shard_sum(hidden, w_down, FF // N_TENSOR)).astype(jnp.bfloat16)

def hand_over(cache_pool, req_len, req_owner, block_list):
    max_blocks = MAXLEN // BT
    result = jnp.zeros((SLOTS, CACHE_LAYERS, KVP, MAXLEN * HD), jnp.bfloat16)
    req_order = jnp.arange(RQ, dtype=jnp.int32)
    token_idx = jnp.arange(max_blocks, dtype=jnp.int32)[:, None] * BT + jnp.arange(BT, dtype=jnp.int32)[None, :]
    for source in range(OWNERS):
        lengths = req_len[source].astype(jnp.int32)
        owner_ids = req_owner[source * RQ:(source + 1) * RQ, 0].astype(jnp.int32)
        listing = block_list[source].astype(jnp.int32)
        counts = (lengths + BT - 1) // BT
        first_block = (jnp.cumsum(counts) - counts).astype(jnp.int32)
        same_owner = (owner_ids[:, None] == owner_ids[None, :]) & (req_order[None, :] < req_order[:, None])
        arrival = lax.optimization_barrier(jnp.sum(same_owner.astype(jnp.int32), axis=1)).astype(jnp.int32)
        block_idx = jnp.minimum(first_block[:, None] + jnp.arange(max_blocks, dtype=jnp.int32)[None, :], NB - 1)
        pool_rows = (source * NB + listing[block_idx]).astype(jnp.int32)
        picked = cache_pool[pool_rows].reshape(RQ, max_blocks, CACHE_LAYERS, KVP, BT, HD)
        keep_mask = token_idx[None] < lengths[:, None, None]
        picked = jnp.where(keep_mask[:, :, None, None, :, None], picked, jnp.zeros((), jnp.bfloat16))
        arranged = jnp.transpose(picked, (0, 2, 3, 1, 4, 5)).reshape(RQ, CACHE_LAYERS, KVP, MAXLEN * HD)
        dest_rows = (owner_ids * (OWNERS * PAIR) + source * PAIR + arrival).astype(jnp.int32)
        result = result.at[dest_rows].set(arranged)
    return result

def reference(tokens, attn_gain, w_query, w_key, w_value, w_out, mlp_gain, w_gate, w_up, w_down, positions, window_lo, cache_pool, req_len, req_owner, block_list):
    outputs = []
    for seq_num in range(SEQS):
        outputs.append(layer_span(tokens[seq_num].reshape(SPAN, D), attn_gain, w_query, w_key, w_value, w_out, mlp_gain, w_gate, w_up, w_down, positions[seq_num].reshape(SPAN), window_lo[seq_num].reshape(SPAN)))
    layer_out = jnp.stack(outputs).reshape(SEQS, SEQ_BLOCKS, TOK_BLOCK, D)
    return (layer_out, hand_over(cache_pool, req_len, req_owner, block_list))
```

```python
import functools

import jax
import jax.numpy as jnp
from jax import lax
from jax.experimental import pallas as pl
from jax.experimental.pallas import tpu as pltpu
from jax.sharding import PartitionSpec as P

HD = 80
D = 2560
BT = 16
MAXLEN = 128
PAIR = 2
RQ = 8
NB = 40
UN = 432
ROWS = 64
NP = 2
PIECE = ROWS // NP
LANES = 128
KT = 512
OWNERS = 8

MESH = pl.DeviceIdType.MESH
VM = pltpu.VMEM
norm_eps = 1e-05
rope_base = 10000.0
F32 = jnp.float32
BF = jnp.bfloat16


def place():
    t = lax.axis_index("tensor")
    return lax.div(t, 4), lax.rem(lax.div(t, 2), 2), lax.rem(t, 2)


def at_chip(x, yh, c):
    return {"tensor": (lax.rem(x + 4, 4) * 2 + yh) * 2 + c}


def col4(x):
    return lax.rem(x + 4, 4)


def normed(values, gain):
    mean_square = jnp.mean(values * values, axis=-1, keepdims=True)
    return (values * lax.rsqrt(mean_square + norm_eps) * gain).astype(BF)


class Gather:
    def __init__(self, buf, send, recv):
        self.x, self.yh, self.c = place()
        self.buf, self.send, self.recv = buf, send, recv
        self.p = 1 - self.yh
        x, yh, c, p = self.x, self.yh, self.c, self.p
        self.a = at_chip(x + 1, yh, c)
        self.b = at_chip(x - 1, yh, c)
        self.o = at_chip(x, p, c)
        own, ca, cb, co = col4(x), col4(x + 1), col4(x - 1), col4(x + 2)
        self.plan = [
            (own * 2 + yh, self.o, own * 2 + p),
            (own * 2 + yh, self.a, cb * 2 + yh),
            (own * 2 + yh, self.b, ca * 2 + yh),
            (own * 2 + p, self.a, cb * 2 + p),
            (own * 2 + p, self.b, ca * 2 + p),
            (cb * 2 + yh, self.a, co * 2 + yh),
            (ca * 2 + p, self.b, co * 2 + p),
        ]

    def copy(self, k, i, slot):
        part = self.buf.at[slot, pl.ds(i * PIECE, PIECE)]
        return pltpu.make_async_remote_copy(
            src_ref=part,
            dst_ref=part,
            send_sem=self.send.at[k, i],
            recv_sem=self.recv.at[k, i],
            device_id=self.plan[k][1],
            device_id_type=MESH,
        )

    def start(self, k, i):
        self.copy(k, i, self.plan[k][0]).start()

    def got(self, k, i):
        self.copy(k, i, self.plan[k][2]).wait_recv()

    def first(self):
        for i in range(NP):
            for k in (0, 1, 2):
                self.start(k, i)

    def second(self):
        for i in range(NP):
            self.got(0, i)
            self.start(3, i)
            self.start(4, i)

    def third(self):
        for i in range(NP):
            self.got(1, i)
            self.start(5, i)

    def fourth(self):
        for i in range(NP):
            self.got(4, i)
            self.start(6, i)

    def finish(self):
        for k in range(7):
            for i in range(NP):
                self.copy(k, i, self.plan[k][0]).wait_send()


def signal(where):
    pl.semaphore_signal(
        pltpu.get_barrier_semaphore(), inc=1, device_id=where, device_id_type=MESH
    )


def first_kernel(
    tok, gain, rc, rs1, rs2, pool, lens, owners, listing, wq, wk, wv, wo, wg, wu, wd,
    q_out, kv, wo_s, wg_s, wu_s, wd_s, dc,
    buf, wq_o, wq_s, wkw, wvw, wall, outg, kvs,
    ag_send, ag_recv, lsem, wsend, wrecv, hsend, hrecv, hlocal,
    zsend, zrecv, ssend, srecv, rsend, rrecv, kvl,
):
    x, yh, c = place()
    s, d = lax.axis_index("seq"), lax.axis_index("dec")
    chip = x * 2 + yh
    sib = at_chip(x, yh, 1 - c)
    start = jnp.minimum(lax.div(chip * HD, LANES), 3) * LANES
    off = chip * HD - start
    cols = pl.ds(pl.multiple_of(start, LANES), 2 * LANES)
    local = [
        pltpu.make_async_copy(wq, wq_o, lsem.at[0]),
        pltpu.make_async_copy(wk.at[:, cols], wkw, lsem.at[1]),
        pltpu.make_async_copy(wv.at[:, cols], wvw, lsem.at[2]),
    ]
    for copy in local:
        copy.start()
    ag = Gather(buf, ag_send, ag_recv)
    for where in (ag.a, ag.b, ag.o, sib):
        signal(where)
    others = []
    for k in range(1, OWNERS):
        ds, dd = k // 2, k % 2
        others.append({"seq": lax.rem(s + ds, 4), "dec": lax.rem(d + dd, 2)})
    for where in others:
        signal(where)
    buf[chip] = normed(tok[...].astype(F32), gain[...])
    pl.semaphore_wait(pltpu.get_barrier_semaphore(), 4 + len(others))
    ag.first()
    shared = [
        pltpu.make_async_remote_copy(
            src_ref=a, dst_ref=b, send_sem=wsend.at[k], recv_sem=wrecv.at[k],
            device_id=sib, device_id_type=MESH,
        )
        for k, (a, b) in enumerate(((wq, wq_s), (wo, wo_s), (wg, wg_s), (wu, wu_s), (wd, wd_s)))
    ]
    for copy in shared:
        copy.start()

    counts = [lax.div(lens[k] + (BT - 1), BT) for k in range(RQ)]
    firsts, so_far = [], jnp.int32(0)
    for k in range(RQ):
        firsts.append(so_far)
        so_far = so_far + counts[k]
    ranks = []
    for k in range(RQ):
        rank = jnp.int32(0)
        for e in range(k):
            rank = rank + (owners[e] == owners[k]).astype(jnp.int32)
        ranks.append(rank)
    feature = lax.broadcasted_iota(jnp.int32, (2, BT * HD), 1)

    def cut(o, _):
        for r in range(PAIR):
            at, length = jnp.int32(0), jnp.int32(0)
            for k in range(RQ):
                hit = (owners[k] == o) & (ranks[k] == r)
                at = jnp.where(hit, firsts[k], at)
                length = jnp.where(hit, lens[k], length)
            for b in range(MAXLEN // BT):
                block = pool[listing[jnp.minimum(at + b, NB - 1)]].astype(F32)
                kept = jnp.where(feature < (length - BT * b) * HD, block, 0.0)
                outg[o * PAIR + r, :, BT * HD * b : BT * HD * (b + 1)] = kept.astype(BF)
        return 0

    lax.fori_loop(0, OWNERS, cut, 0)
    me = s * 2 + d
    handed = []
    for k, where in enumerate(others):
        there = where["seq"] * 2 + where["dec"]
        handed.append(
            pltpu.make_async_remote_copy(
                src_ref=outg.at[pl.ds(there * PAIR, PAIR)],
                dst_ref=dc.at[pl.ds(me * PAIR, PAIR)],
                send_sem=hsend.at[k],
                recv_sem=hrecv.at[k],
                device_id=where,
                device_id_type=MESH,
            )
        )
    keep = pltpu.make_async_copy(
        outg.at[pl.ds(me * PAIR, PAIR)], dc.at[pl.ds(me * PAIR, PAIR)], hlocal
    )
    for copy in handed:
        copy.start()
    keep.start()

    row = lax.broadcasted_iota(jnp.int32, (2 * HD, 2 * LANES), 0)
    col = lax.broadcasted_iota(jnp.int32, (2 * HD, 2 * LANES), 1)
    head = lax.div(col, LANES)
    lane = col - head * LANES
    spread = ((row == lane + head * HD) & (lane < HD)).astype(F32).astype(BF)
    row2 = lax.broadcasted_iota(jnp.int32, (2 * LANES, LANES), 0)
    col2 = lax.broadcasted_iota(jnp.int32, (2 * LANES, LANES), 1)
    pick = ((row2 == col2 + off) & (col2 < HD)).astype(F32).astype(BF)
    chunk = 512

    def laid(src, select, begin, width):
        def one(i, _):
            rows = pl.ds(pl.multiple_of(i * chunk, chunk), chunk)
            wall[rows, begin : begin + width] = jnp.dot(
                src[rows, :], select, preferred_element_type=F32
            ).astype(BF)
            return 0

        lax.fori_loop(0, D // chunk, one, 0)

    for copy in local:
        copy.wait()
    laid(wq_o, spread, 0, 256)
    laid(wkw, pick, 512, 128)
    laid(wvw, pick, 640, 128)
    ag.second()
    shared[0].wait_recv()
    laid(wq_s, spread, 256, 256)

    def rotated(v, cs, s1, s2):
        return v * cs + pltpu.roll(v, LANES - HD // 2, 1) * s1 + pltpu.roll(v, HD // 2, 1) * s2

    def sends(k, cx):
        dst = kv.at[s, pl.ds(2 * cx, 2), c]
        src = kvs.at[cx]
        z = [
            pltpu.make_async_remote_copy(
                src_ref=src, dst_ref=dst, send_sem=zsend.at[e - 1, k], recv_sem=zrecv.at[e - 1, k],
                device_id={"seq": lax.rem(s + e, 4)}, device_id_type=MESH,
            )
            for e in (1, 2, 3)
        ]
        near = pltpu.make_async_remote_copy(
            src_ref=src, dst_ref=dst, send_sem=ssend.at[k], recv_sem=srecv.at[k],
            device_id=sib, device_id_type=MESH,
        )
        return z, near, pltpu.make_async_copy(src, dst, kvl.at[k])

    def project(k, cx):
        both = buf[pl.ds(2 * cx, 2)].reshape(2 * ROWS, D)
        out = jnp.dot(both, wall[...], preferred_element_type=F32)
        here = pl.ds(pl.multiple_of(cx * 2 * ROWS, 2 * ROWS), 2 * ROWS)
        cs, s1, s2 = rc[here, :], rs1[here, :], rs2[here, :]
        for h in range(4):
            v = rotated(out[:, h * LANES : (h + 1) * LANES], cs, s1, s2).astype(BF)
            q_out[pl.ds(2 * cx, 2), :, h * LANES : (h + 1) * LANES] = v.reshape(2, ROWS, LANES)
        kr = rotated(out[:, 512:640], cs, s1, s2).astype(BF)
        kvs[cx, :, :, 0:LANES] = kr.reshape(2, ROWS, LANES)
        kvs[cx, :, :, LANES:] = out[:, 640:768].astype(BF).reshape(2, ROWS, LANES)
        z, near, mine = sends(k, cx)
        for e in (1, 2, 3):

            @pl.when(s + e < 4)
            def _():
                z[e - 1].start()

        near.start()
        mine.start()

    columns = [x, col4(x - 1), col4(x + 1), col4(x + 2)]
    project(0, columns[0])
    ag.third()
    ag.fourth()
    for i in range(NP):
        ag.got(3, i)
    project(1, columns[1])
    for i in range(NP):
        ag.got(2, i)
    project(2, columns[2])
    for i in range(NP):
        ag.got(5, i)
        ag.got(6, i)
    project(3, columns[3])
    ag.finish()

    def relay(e, k, sq, core):
        part = kv.at[sq, pl.ds(2 * columns[k], 2), core]
        return pltpu.make_async_remote_copy(
            src_ref=part, dst_ref=part, send_sem=rsend.at[e - 1, k], recv_sem=rrecv.at[e - 1, k],
            device_id=sib, device_id_type=MESH,
        )

    for k in range(4):
        for e in (1, 2, 3):

            @pl.when(s >= e)
            def _():
                sq = lax.rem(s - e + 4, 4)
                part = kv.at[sq, pl.ds(2 * columns[k], 2), c]
                pltpu.make_async_remote_copy(
                    src_ref=part, dst_ref=part, send_sem=zsend.at[e - 1, k], recv_sem=zrecv.at[e - 1, k],
                    device_id=sib, device_id_type=MESH,
                ).wait_recv()
                relay(e, k, sq, c).start()

    for k in range(4):
        z, near, mine = sends(k, columns[k])
        near.wait_send()
        mine.wait()
        part = kv.at[s, pl.ds(2 * columns[k], 2), 1 - c]
        pltpu.make_async_remote_copy(
            src_ref=part, dst_ref=part, send_sem=ssend.at[k], recv_sem=srecv.at[k],
            device_id=sib, device_id_type=MESH,
        ).wait_recv()
        for e in (1, 2, 3):

            @pl.when(s + e < 4)
            def _():
                z[e - 1].wait_send()

            @pl.when(s >= e)
            def _():
                sq = lax.rem(s - e + 4, 4)
                relay(e, k, sq, c).wait_send()
                relay(e, k, sq, 1 - c).wait_recv()

    for k, where in enumerate(others):
        handed[k].wait_send()
        back = lax.rem(s - (k + 1) // 2 + 4, 4) * 2 + lax.rem(d - (k + 1) % 2 + 2, 2)
        pltpu.make_async_remote_copy(
            src_ref=outg.at[pl.ds(back * PAIR, PAIR)],
            dst_ref=dc.at[pl.ds(back * PAIR, PAIR)],
            send_sem=hsend.at[k],
            recv_sem=hrecv.at[k],
            device_id=where,
            device_id_type=MESH,
        ).wait_recv()
    keep.wait()
    for k, copy in enumerate(shared):
        copy.wait_send()
        if k:
            copy.wait_recv()


def attend_kernel(lo_ref, info, q_ref, kv_ref, o_ref, sc, mx, den, acc):
    j = pl.program_id(0)
    s, c = info[0], info[1]
    base = s * 1024 + j * 2 * ROWS + c * ROWS
    lo_row = lo_ref[pl.ds(j, 1), :].astype(F32)
    eye = lax.broadcasted_iota(jnp.int32, (ROWS, ROWS), 0) == lax.broadcasted_iota(
        jnp.int32, (ROWS, ROWS), 1
    )
    lo_col = jnp.sum(jnp.where(eye, lo_row, 0.0), axis=1, keepdims=True).astype(jnp.int32)
    low = jnp.concatenate([lo_col] * 4, axis=0)
    qpos = base + lax.rem(lax.broadcasted_iota(jnp.int32, (4 * ROWS, 1), 0), ROWS)
    least = jnp.min(lo_row).astype(jnp.int32)
    begin = lax.div(jnp.maximum(least, 0), KT)
    end = lax.div(base + ROWS - 1, KT) + 1
    q = q_ref[0]
    q4 = jnp.concatenate([q[:, h * LANES : (h + 1) * LANES] for h in range(4)], axis=0)
    mx[...] = jnp.full_like(mx, -jnp.inf)
    key_lane = lax.broadcasted_iota(jnp.int32, (4 * ROWS, KT), 1)

    def score(t, _):
        k_part = kv_ref[pl.ds(pl.multiple_of(t * KT, KT), KT), 0:LANES]
        sco = lax.dot_general(q4, k_part, (((1,), (1,)), ((), ())), preferred_element_type=F32)
        key = key_lane + t * KT
        sco = jnp.where((key >= low) & (key <= qpos), sco, -jnp.inf)
        sc[t] = sco
        top = mx[...]
        for i in range(KT // LANES):
            top = jnp.maximum(top, sco[:, i * LANES : (i + 1) * LANES])
        mx[...] = top
        return 0

    lax.fori_loop(begin, end, score, 0)
    m = jnp.max(mx[...], axis=1, keepdims=True)
    den[...] = jnp.zeros_like(den)
    acc[...] = jnp.zeros_like(acc)
    rate = HD**-0.5 * 1.4426950408889634

    def mix(t, _):
        p = jnp.exp2((sc[t] - m) * rate)
        total = den[...]
        for i in range(KT // LANES):
            total = total + p[:, i * LANES : (i + 1) * LANES]
        den[...] = total
        v_part = kv_ref[pl.ds(pl.multiple_of(t * KT, KT), KT), LANES:]
        acc[...] += jnp.dot(p.astype(BF), v_part, preferred_element_type=F32)
        return 0

    lax.fori_loop(begin, end, mix, 0)
    out = acc[...] / jnp.sum(den[...], axis=1, keepdims=True)
    for h in range(4):
        o_ref[0, :, h * LANES : (h + 1) * LANES] = out[h * ROWS : (h + 1) * ROWS, :].astype(BF)


class Scatter:
    def __init__(self, out, inb, send, recv):
        x, yh, c = place()
        self.out, self.inb, self.send, self.recv = out, inb, send, recv
        step = 2 * yh - 1
        self.m, self.p = yh, 1 - yh
        self.ca, self.cb, self.co, self.own = col4(x + step), col4(x - step), col4(x + 2), x
        a, b, o = at_chip(x + step, yh, c), at_chip(x - step, yh, c), at_chip(x, 1 - yh, c)
        self.to = [a, b, b, a, a, b, o]

    def copy(self, k, i):
        rows = pl.ds(i * PIECE, PIECE)
        return pltpu.make_async_remote_copy(
            src_ref=self.out.at[k, rows],
            dst_ref=self.inb.at[k, rows],
            send_sem=self.send.at[k, i],
            recv_sem=self.recv.at[k, i],
            device_id=self.to[k],
            device_id_type=MESH,
        )

    def put(self, k, part, row, i, adds=()):
        rows = pl.ds(i * PIECE, PIECE)
        total = part[row, rows, :]
        for e in adds:
            self.copy(e, i).wait_recv()
            total = total + self.inb[e, rows, :].astype(F32)
        self.out[k, rows, :] = total.astype(BF)
        self.copy(k, i).start()

    def run(self, far, cb, ca, own):
        part = far()
        for i in range(NP):
            self.put(0, part, self.p, i)
        part_b = cb()
        for i in range(NP):
            self.put(1, part_b, self.p, i)
        for i in range(NP):
            self.put(2, part, self.m, i)
        part_a = ca()
        for i in range(NP):
            self.put(3, part_a, self.p, i, (0,))
        for i in range(NP):
            self.put(4, part_a, self.m, i)
        mine = own()
        for i in range(NP):
            self.put(5, part_b, self.m, i, (2,))
        for i in range(NP):
            self.put(6, mine, self.p, i, (1, 3))
        pieces = []
        for i in range(NP):
            rows = pl.ds(i * PIECE, PIECE)
            total = mine[self.m, rows, :]
            for e in (4, 5, 6):
                self.copy(e, i).wait_recv()
                total = total + self.inb[e, rows, :].astype(F32)
            pieces.append(total)
        return pieces

    def finish(self):
        for k in range(7):
            for i in range(NP):
                self.copy(k, i).wait_send()


def last_kernel(
    heads, tok, gain, wo, wo_s, wg, wg_s, wu, wu_s, wd, wd_s,
    out,
    buf, res, part, hid, wov, g0, g1, u0, u1, d0, d1, o1, i1, o2, i2,
    lsem, ag_send, ag_recv, s1, r1, s2, r2,
):
    ag = Gather(buf, ag_send, ag_recv)
    for where in (ag.a, ag.b, ag.o):
        signal(where)
    loads = []
    for e, src in enumerate((wo, wo_s)):
        for h in range(2):
            loads.append((src.at[pl.ds(h * HD, HD)], wov.at[pl.ds((2 * e + h) * LANES, HD)]))
    loads += [(wg, g0), (wg_s, g1), (wu, u0), (wu_s, u1), (wd, d0), (wd_s, d1)]
    copies = [pltpu.make_async_copy(a, b, lsem.at[k]) for k, (a, b) in enumerate(loads)]
    for copy in copies:
        copy.start()
    for h in range(4):
        wov[h * LANES + HD : (h + 1) * LANES, :] = jnp.zeros((LANES - HD, D), BF)
    for copy in copies[:4]:
        copy.wait()
    pl.semaphore_wait(pltpu.get_barrier_semaphore(), 3)
    chunk = 512

    def wide(slot, terms):
        def one(n, _):
            cols = pl.ds(pl.multiple_of(n * chunk, chunk), chunk)
            total = None
            for left, right in terms:
                this = jnp.dot(left, right[:, cols], preferred_element_type=F32)
                total = this if total is None else total + this
            part[slot, :, :, cols] = total.reshape(2, ROWS, chunk)
            return 0

        lax.fori_loop(0, D // chunk, one, 0)
        return part.at[slot]

    rs = Scatter(o1, i1, s1, r1)

    def project(slot, cx):
        return wide(slot, [(heads[pl.ds(2 * cx, 2)].reshape(2 * ROWS, 4 * LANES), wov)])

    pieces = rs.run(
        lambda: project(0, rs.co),
        lambda: project(1, rs.cb),
        lambda: project(2, rs.ca),
        lambda: project(3, rs.own),
    )
    chip = ag.x * 2 + ag.yh
    for i in range(NP):
        rows = pl.ds(i * PIECE, PIECE)
        total = tok[rows, :].astype(F32) + pieces[i]
        res[rows, :] = total
        buf[chip, rows, :] = normed(total, gain[...])
        for k in (0, 1, 2):
            ag.start(k, i)
    for copy in copies[4:]:
        copy.wait()

    def hidden(slot, cx):
        both = buf[pl.ds(2 * cx, 2)].reshape(2 * ROWS, D)
        for e, (g, u) in enumerate(((g0, u0), (g1, u1))):
            gate = jnp.dot(both, g[...], preferred_element_type=F32)
            up = jnp.dot(both, u[...], preferred_element_type=F32)
            hid[e] = (gate / (1.0 + jnp.exp(-gate)) * up).astype(BF)
        return wide(slot, [(hid[0], d0), (hid[1], d1)])

    rs2 = Scatter(o2, i2, s2, r2)
    ag.second()
    own = hidden(3, rs2.own)
    ag.third()
    ag.fourth()
    for i in range(NP):
        ag.got(3, i)
        ag.got(2, i)
    near_b = hidden(1, rs2.cb)
    near_a = hidden(2, rs2.ca)
    for i in range(NP):
        ag.got(5, i)
        ag.got(6, i)
    pieces = rs2.run(
        lambda: hidden(0, rs2.co), lambda: near_b, lambda: near_a, lambda: own
    )
    for i in range(NP):
        rows = pl.ds(i * PIECE, PIECE)
        out[rows, :] = (res[rows, :] + pieces[i]).astype(BF)
    ag.finish()
    rs.finish()
    rs2.finish()


VMEM_SPEC = pl.BlockSpec(memory_space=pltpu.VMEM)
SMEM_SPEC = pl.BlockSpec(memory_space=pltpu.SMEM)
ANY_SPEC = pl.BlockSpec(memory_space=pl.ANY)
DMA = pltpu.SemaphoreType.DMA


def shape(*dims, dtype=BF):
    return jax.ShapeDtypeStruct(dims, dtype)


def shards(
    tokens, attn_gain, w_query, w_key, w_value, w_out, mlp_gain, w_gate, w_up, w_down,
    positions, window_lo, cache_pool, req_len, req_owner, block_list,
):
    own_rows = tokens[0, 0]
    core = lax.rem(lax.axis_index("tensor"), 2)
    seq = lax.axis_index("seq")
    places = lax.dynamic_index_in_dim(
        positions.reshape(8, 2, ROWS), core, 1, keepdims=False
    ).reshape(8 * ROWS)
    lower = lax.dynamic_index_in_dim(window_lo.reshape(8, 2, ROWS), core, 1, keepdims=False)
    lane = jnp.arange(LANES, dtype=jnp.int32)
    half = HD // 2
    rate = jnp.power(F32(rope_base), -(2.0 * lax.rem(lane, half).astype(F32)) / HD)
    angles = places.astype(F32)[:, None] * rate[None, :]
    cosine, sine = jnp.cos(angles), jnp.sin(angles)
    lane = lane[None, :]
    rc = jnp.where(lane < HD, cosine, 0.0)
    rs1 = jnp.where(lane < half, -sine, 0.0)
    rs2 = jnp.where((lane >= half) & (lane < HD), sine, 0.0)

    q, kv, wo_s, wg_s, wu_s, wd_s, dc = pl.pallas_call(
        first_kernel,
        out_shape=(
            shape(8, ROWS, 4 * LANES),
            shape(4, 8, 2, ROWS, 2 * LANES),
            shape(*w_out.shape),
            shape(*w_gate.shape),
            shape(*w_up.shape),
            shape(*w_down.shape),
            shape(OWNERS * PAIR, 2, MAXLEN * HD),
        ),
        in_specs=[VMEM_SPEC] * 6 + [SMEM_SPEC] * 3 + [ANY_SPEC] * 7,
        out_specs=(VMEM_SPEC,) + (ANY_SPEC,) * 6,
        scratch_shapes=[
            VM((8, ROWS, D), BF),
            VM((D, 2 * HD), BF),
            VM((D, 2 * HD), BF),
            VM((D, 2 * LANES), BF),
            VM((D, 2 * LANES), BF),
            VM((D, 6 * LANES), BF),
            VM((OWNERS * PAIR, 2, MAXLEN * HD), BF),
            VM((4, 2, ROWS, 2 * LANES), BF),
            DMA((7, NP)),
            DMA((7, NP)),
            DMA((3,)),
            DMA((5,)),
            DMA((5,)),
            DMA((7,)),
            DMA((7,)),
            DMA,
            DMA((3, 4)),
            DMA((3, 4)),
            DMA((4,)),
            DMA((4,)),
            DMA((3, 4)),
            DMA((3, 4)),
            DMA((4,)),
        ],
        compiler_params=pltpu.CompilerParams(
            collective_id=0, has_side_effects=True, vmem_limit_bytes=48 << 20
        ),
        name="gather_project",
    )(
        own_rows, attn_gain.reshape(1, D), rc, rs1, rs2, cache_pool.reshape(NB, 2, BT * HD),
        req_len.reshape(RQ), req_owner.reshape(RQ), block_list.reshape(NB),
        w_query, w_key, w_value, w_out, w_gate, w_up, w_down,
    )

    info = jnp.stack([seq, core]).astype(jnp.int32)
    heads = pl.pallas_call(
        attend_kernel,
        out_shape=shape(8, ROWS, 4 * LANES),
        grid=(8,),
        in_specs=[
            pl.BlockSpec((8, ROWS), lambda j: (0, 0)),
            SMEM_SPEC,
            pl.BlockSpec((1, ROWS, 4 * LANES), lambda j: (j, 0, 0)),
            pl.BlockSpec((4096, 2 * LANES), lambda j: (0, 0)),
        ],
        out_specs=pl.BlockSpec((1, ROWS, 4 * LANES), lambda j: (j, 0, 0)),
        scratch_shapes=[
            VM((4096 // KT, 4 * ROWS, KT), F32),
            VM((4 * ROWS, LANES), F32),
            VM((4 * ROWS, LANES), F32),
            VM((4 * ROWS, LANES), F32),
        ],
        compiler_params=pltpu.CompilerParams(vmem_limit_bytes=32 << 20),
        name="attend",
    )(lower, info, q, kv.reshape(4096, 2 * LANES))

    layer_out = pl.pallas_call(
        last_kernel,
        out_shape=shape(ROWS, D),
        in_specs=[VMEM_SPEC] * 3 + [ANY_SPEC] * 8,
        out_specs=VMEM_SPEC,
        scratch_shapes=[
            VM((8, ROWS, D), BF),
            VM((ROWS, D), F32),
            VM((4, 2, ROWS, D), F32),
            VM((2, 2 * ROWS, UN), BF),
            VM((4 * LANES, D), BF),
            VM((D, UN), BF),
            VM((D, UN), BF),
            VM((D, UN), BF),
            VM((D, UN), BF),
            VM((UN, D), BF),
            VM((UN, D), BF),
            VM((7, ROWS, D), BF),
            VM((7, ROWS, D), BF),
            VM((7, ROWS, D), BF),
            VM((7, ROWS, D), BF),
            DMA((10,)),
        ]
        + [DMA((7, NP))] * 6,
        compiler_params=pltpu.CompilerParams(
            collective_id=1, has_side_effects=True, vmem_limit_bytes=56 << 20
        ),
        name="mix_feed_forward",
    )(
        heads, own_rows, mlp_gain.reshape(1, D), w_out, wo_s, w_gate, wg_s, w_up, wu_s, w_down, wd_s,
    )
    return (
        layer_out.reshape(1, 1, ROWS, D),
        dc.reshape(OWNERS * PAIR, 2, 1, MAXLEN * HD),
    )


def solution(mesh):
    in_specs = (
        P("dec", "seq", "tensor", None),
        P(),
        P(None, "tensor"),
        P(),
        P(),
        P("tensor", None),
        P(),
        P(None, "tensor"),
        P(None, "tensor"),
        P("tensor", None),
        P("dec", "seq", None),
        P("dec", "seq", None),
        P(("seq", "dec"), None, "tensor", None),
        P(("seq", "dec"), None),
        P(("seq", "dec"), None),
        P(("seq", "dec"), None),
    )
    out_specs = (P("dec", "seq", "tensor", None), P(("seq", "dec"), None, "tensor", None))
    return jax.shard_map(shards, mesh=mesh, in_specs=in_specs, out_specs=out_specs, check_vma=False)
```

```python
import functools

import jax
import jax.numpy as jnp
from jax import lax
from jax.experimental import pallas as pl
from jax.experimental.pallas import tpu as pltpu
from jax.sharding import PartitionSpec as P

HD = 80
D = 2560
BT = 16
MAXLEN = 128
PAIR = 2
RQ = 8
NB = 40
UN = 432
ROWS = 64
NP = 2
PIECE = ROWS // NP
LANES = 128
KT = 512
TILES = 8
OWNERS = 8

MESH = pl.DeviceIdType.MESH
VM = pltpu.VMEM
norm_eps = 1e-05
LOG_BASE = 9.210340371976184
SCALE = HD**-0.5 * 1.4426950408889634
F32 = jnp.float32
BF = jnp.bfloat16


def place():
    t = lax.axis_index("tensor")
    return lax.div(t, 4), lax.rem(lax.div(t, 2), 2), lax.rem(t, 2)


def at_chip(x, yh, c):
    return {"tensor": (lax.rem(x + 4, 4) * 2 + yh) * 2 + c}


def col4(x):
    return lax.rem(x + 4, 4)


def normed(values, gain):
    mean_square = jnp.mean(values * values, axis=-1, keepdims=True)
    return (values * lax.rsqrt(mean_square + norm_eps) * gain).astype(BF)


class Gather:
    def __init__(self, buf, send, recv):
        self.x, self.yh, self.c = place()
        self.buf, self.send, self.recv = buf, send, recv
        x, m, c, p = self.x, self.yh, self.c, 1 - self.yh
        self.a, self.b, self.o = at_chip(x + 1, m, c), at_chip(x - 1, m, c), at_chip(x, p, c)
        own, ca, cb, co = col4(x), col4(x + 1), col4(x - 1), col4(x + 2)
        self.plan = [
            (own * 2 + m, self.o, own * 2 + p),
            (own * 2 + m, self.a, cb * 2 + m),
            (own * 2 + m, self.b, ca * 2 + m),
            (own * 2 + p, self.a, cb * 2 + p),
            (own * 2 + p, self.b, ca * 2 + p),
            (cb * 2 + m, self.a, co * 2 + m),
            (co * 2 + m, self.o, co * 2 + p),
            (ca * 2 + m, self.b, co * 2 + m),
        ]

    def copy(self, k, i, got):
        plan = self.plan[7 if k == 5 and i >= NP // 2 else k]
        part = self.buf.at[plan[2] if got else plan[0], pl.ds(i * PIECE, PIECE)]
        return pltpu.make_async_remote_copy(
            src_ref=part,
            dst_ref=part,
            send_sem=self.send.at[k, i],
            recv_sem=self.recv.at[k, i],
            device_id=plan[1],
            device_id_type=MESH,
        )

    def start(self, k, i):
        self.copy(k, i, False).start()

    def got(self, k, i):
        self.copy(k, i, True).wait_recv()

    def first(self, i):
        self.start(1, i)
        self.start(2, i)
        self.start(0, i)

    def second(self):
        for i in range(NP // 2):
            self.got(1, i)
            self.start(5, i)
            self.got(2, NP - 1 - i)
            self.start(5, NP - 1 - i)

    def third(self):
        for i in range(NP):
            self.got(0, i)
            self.start(3, i)
            self.start(4, i)

    def fourth(self):
        for i in range(NP // 2):
            for e in (i, NP - 1 - i):
                self.got(5, e)
                self.start(6, e)

    def near(self, side):
        for i in range(NP):
            if (i >= NP // 2) == (side == 1):
                self.got(side, i)
        for i in range(NP):
            self.got(side + 2, i)

    def far(self):
        for i in range(NP):
            self.got(6, i)

    def finish(self):
        for k in range(7):
            for i in range(NP):
                self.copy(k, i, False).wait_send()


class Scatter:
    def __init__(self, out, inb, send, recv):
        x, yh, c = place()
        self.out, self.inb, self.send, self.recv = out, inb, send, recv
        self.m, self.p = yh, 1 - yh
        self.ca, self.cb, self.co, self.own = col4(x + 1), col4(x - 1), col4(x + 2), x
        self.a, self.b = at_chip(x + 1, yh, c), at_chip(x - 1, yh, c)
        o = at_chip(x, 1 - yh, c)
        self.to = [o, self.a, self.b, None, self.a, self.b, o]

    def copy(self, k, i):
        rows = pl.ds(i * PIECE, PIECE)
        to = self.to[k] if k != 3 else (self.a if i < NP // 2 else self.b)
        return pltpu.make_async_remote_copy(
            src_ref=self.out.at[k, rows],
            dst_ref=self.inb.at[k, rows],
            send_sem=self.send.at[k, i],
            recv_sem=self.recv.at[k, i],
            device_id=to,
            device_id_type=MESH,
        )

    def summed(self, part, row, i, adds):
        rows = pl.ds(i * PIECE, PIECE)
        total = part[row, rows, :]
        for e in adds:
            self.copy(e, i).wait_recv()
            total = total + self.inb[e, rows, :].astype(F32)
        return total

    def put(self, k, part, row, i, adds=()):
        self.out[k, pl.ds(i * PIECE, PIECE), :] = self.summed(part, row, i, adds).astype(BF)
        self.copy(k, i).start()

    def sides(self, part_a, part_b):
        for i in range(NP):
            self.put(1, part_a, self.p, i)
            self.put(2, part_b, self.p, i)

    def across(self, far):
        for i in range(NP // 2):
            self.put(0, far, self.p, i)
            self.put(0, far, self.p, NP - 1 - i)

    def rest(self, far, part_a, part_b, mine):
        for i in range(NP // 2):
            self.put(3, far, self.m, i, (0,))
            self.put(3, far, self.m, NP - 1 - i, (0,))
        for i in range(NP):
            self.put(6, mine, self.p, i, (1, 2))
        for i in range(NP // 2):
            self.put(4, part_a, self.m, NP - 1 - i)
            self.put(5, part_b, self.m, i)
        for i in range(NP // 2):
            self.put(4, part_a, self.m, i, (3,))
            self.put(5, part_b, self.m, NP - 1 - i, (3,))

    def final(self, mine, i):
        return self.summed(mine, self.m, i, (6, 4, 5))

    def finish(self):
        for k in range(7):
            for i in range(NP):
                self.copy(k, i).wait_send()


def signal(where):
    pl.semaphore_signal(
        pltpu.get_barrier_semaphore(), inc=1, device_id=where, device_id_type=MESH
    )


def dot_nt(left, right):
    return lax.dot_general(left, right, (((1,), (1,)), ((), ())), preferred_element_type=F32)


def first_kernel(
    tok, gain, pos, pool, lens, owners, listing, wq, wk, wv, wo, wg, wu, wd,
    q_out, k_out, v_out, wo_s, wg_s, wu_s, wd_s, dc,
    buf, wall, wkw, wvw, outg, qst, kst, vst,
    ag_send, ag_recv, lsem, wsend, wrecv, hsend, hrecv, hlocal,
    zsend, zrecv, ssend, srecv, rsend, rrecv, kvl, qsem,
):
    x, yh, c = place()
    s, d = lax.axis_index("seq"), lax.axis_index("dec")
    chip = x * 2 + yh
    sib = at_chip(x, yh, 1 - c)
    start = jnp.minimum(lax.div(chip * HD, LANES), 3) * LANES
    off = chip * HD - start
    cols = pl.ds(pl.multiple_of(start, LANES), 2 * LANES)
    local = [
        pltpu.make_async_copy(wq, wall.at[pl.ds(0, 2 * HD)], lsem.at[0]),
        pltpu.make_async_copy(wk.at[:, cols], wkw, lsem.at[1]),
        pltpu.make_async_copy(wv.at[:, cols], wvw, lsem.at[2]),
    ]
    for copy in local:
        copy.start()
    ag = Gather(buf, ag_send, ag_recv)
    for where in (ag.a, ag.b, ag.o, sib):
        signal(where)
    others = []
    for k in range(1, OWNERS):
        ds, dd = k // 2, k % 2
        others.append({"seq": lax.rem(s + ds, 4), "dec": lax.rem(d + dd, 2)})
    for where in others:
        signal(where)
    buf[chip] = normed(tok[...].astype(F32), gain[...])
    pl.semaphore_wait(pltpu.get_barrier_semaphore(), 4 + len(others))
    for i in range(NP):
        ag.first(i)
    shared = [
        pltpu.make_async_remote_copy(
            src_ref=a, dst_ref=b, send_sem=wsend.at[k], recv_sem=wrecv.at[k],
            device_id=sib, device_id_type=MESH,
        )
        for k, (a, b) in enumerate(
            ((wq, wall.at[pl.ds(2 * HD, 2 * HD)]), (wo, wo_s), (wg, wg_s), (wu, wu_s), (wd, wd_s))
        )
    ]
    for copy in shared:
        copy.start()

    counts = [lax.div(lens[k] + (BT - 1), BT) for k in range(RQ)]
    firsts, so_far = [], jnp.int32(0)
    for k in range(RQ):
        firsts.append(so_far)
        so_far = so_far + counts[k]
    ranks = []
    for k in range(RQ):
        rank = jnp.int32(0)
        for e in range(k):
            rank = rank + (owners[e] == owners[k]).astype(jnp.int32)
        ranks.append(rank)
    feature = lax.broadcasted_iota(jnp.int32, (2, BT * HD), 1)

    def cut(o, _):
        for r in range(PAIR):
            at, length = jnp.int32(0), jnp.int32(0)
            for k in range(RQ):
                hit = (owners[k] == o) & (ranks[k] == r)
                at = jnp.where(hit, firsts[k], at)
                length = jnp.where(hit, lens[k], length)
            for b in range(MAXLEN // BT):
                block = pool[listing[jnp.minimum(at + b, NB - 1)]].astype(F32)
                kept = jnp.where(feature < (length - BT * b) * HD, block, 0.0)
                outg[o * PAIR + r, :, BT * HD * b : BT * HD * (b + 1)] = kept.astype(BF)
        return 0

    lax.fori_loop(0, OWNERS, cut, 0)
    me = s * 2 + d
    handed = []
    for k, where in enumerate(others):
        there = where["seq"] * 2 + where["dec"]
        handed.append(
            pltpu.make_async_remote_copy(
                src_ref=outg.at[pl.ds(there * PAIR, PAIR)],
                dst_ref=dc.at[pl.ds(me * PAIR, PAIR)],
                send_sem=hsend.at[k],
                recv_sem=hrecv.at[k],
                device_id=where,
                device_id_type=MESH,
            )
        )
    keep = pltpu.make_async_copy(
        outg.at[pl.ds(me * PAIR, PAIR)], dc.at[pl.ds(me * PAIR, PAIR)], hlocal
    )
    ag.second()
    for copy in handed:
        copy.start()
    keep.start()

    row = lax.broadcasted_iota(jnp.int32, (HD, 2 * LANES), 0)
    col = lax.broadcasted_iota(jnp.int32, (HD, 2 * LANES), 1)
    pick = (col == row + off).astype(F32).astype(BF)
    chunk = 512

    def laid(src, begin):
        def one(i, _):
            rows = pl.ds(pl.multiple_of(i * chunk, chunk), chunk)
            wall[begin : begin + HD, rows] = dot_nt(pick, src[rows, :]).astype(BF)
            return 0

        lax.fori_loop(0, D // chunk, one, 0)

    for copy in local:
        copy.wait()
    laid(wkw, 4 * HD)
    laid(wvw, 5 * HD)
    half = HD // 2
    rate = jnp.exp(
        lax.broadcasted_iota(jnp.int32, (half, 1), 0).astype(F32) * (-2.0 / HD * LOG_BASE)
    )
    low_lanes = lax.broadcasted_iota(jnp.int32, (1, LANES), 1) < ROWS
    kst[:, :, HD:] = jnp.zeros((4, LANES, LANES - HD), BF)
    qst[:, :, HD:, :] = jnp.zeros((4, 2, LANES - HD, 2 * LANES), BF)
    ag.third()
    shared[0].wait_recv()

    def own_half(two, one_more):
        low = jnp.where(c == 0, two, pltpu.roll(two, ROWS, 1))
        high = jnp.where(c == 0, pltpu.roll(one_more, ROWS, 1), one_more)
        return jnp.where(low_lanes, low, high)

    def sends(k, cx):
        t, begin = s * 2 + lax.div(cx, 2), c * 256 + lax.rem(cx, 2) * LANES
        rows = pl.ds(pl.multiple_of(begin, LANES), LANES)
        pairs = ((kst.at[cx], k_out.at[t, rows]), (vst.at[cx], v_out.at[t, :, rows]))
        z, near, mine = [], [], []
        for n, (src, dst) in enumerate(pairs):
            z.append([
                pltpu.make_async_remote_copy(
                    src_ref=src, dst_ref=dst, send_sem=zsend.at[e - 1, k, n], recv_sem=zrecv.at[e - 1, k, n],
                    device_id={"seq": lax.rem(s + e, 4)}, device_id_type=MESH,
                )
                for e in (1, 2, 3)
            ])
            near.append(pltpu.make_async_remote_copy(
                src_ref=src, dst_ref=dst, send_sem=ssend.at[k, n], recv_sem=srecv.at[k, n],
                device_id=sib, device_id_type=MESH,
            ))
            mine.append(pltpu.make_async_copy(src, dst, kvl.at[k, n]))
        return z, near, mine

    def rotated(v, cosine, sine):
        a, b = v[:half], v[half:]
        return jnp.concatenate([a * cosine - b * sine, b * cosine + a * sine], axis=0)

    def q_copy(k, cx):
        return pltpu.make_async_copy(qst.at[cx], q_out.at[cx], qsem.at[k])

    def project(k, cx):
        both = buf[pl.ds(2 * cx, 2)].reshape(2 * ROWS, D)
        out = dot_nt(wall[...], both)
        lanes = pl.multiple_of(cx * 2 * LANES, 2 * LANES)
        where = pos[:, pl.ds(lanes, 2 * LANES)].astype(F32)
        angles = rate * own_half(where[:, :LANES], where[:, LANES:])
        cosine, sine = jnp.cos(angles), jnp.sin(angles)
        for h in range(4):
            v = rotated(out[h * HD : (h + 1) * HD], cosine, sine) * SCALE
            qst[cx, h // 2, 0:HD, (h % 2) * LANES : (h % 2 + 1) * LANES] = v.astype(BF)
        kr = rotated(out[4 * HD : 5 * HD], cosine, sine)
        kr = jnp.concatenate([kr, jnp.zeros((LANES - HD, LANES), F32)], axis=0)
        kst[cx] = kr.T.astype(BF)
        vst[cx] = out[5 * HD :].astype(BF)
        z, near, mine = sends(k, cx)
        for n in range(2):
            for e in (1, 2, 3):

                @pl.when(s + e < 4)
                def _():
                    z[n][e - 1].start()

            near[n].start()
            mine[n].start()
        q_copy(k, cx).start()

    columns = [x, col4(x - 1), col4(x + 1), col4(x + 2)]
    project(0, columns[0])
    ag.fourth()
    ag.near(1)
    project(1, columns[1])
    ag.near(2)
    project(2, columns[2])
    ag.far()
    project(3, columns[3])

    def arrived(k, sq, core, n):
        cx = columns[k]
        t, begin = sq * 2 + lax.div(cx, 2), core * 256 + lax.rem(cx, 2) * LANES
        rows = pl.ds(pl.multiple_of(begin, LANES), LANES)
        return k_out.at[t, rows] if n == 0 else v_out.at[t, :, rows]

    def moved(part, send, recv):
        return pltpu.make_async_remote_copy(
            src_ref=part, dst_ref=part, send_sem=send, recv_sem=recv,
            device_id=sib, device_id_type=MESH,
        )

    def relay(e, k, core, n):
        part = arrived(k, lax.rem(s - e + 4, 4), core, n)
        return moved(part, rsend.at[e - 1, k, n], rrecv.at[e - 1, k, n])

    for k in range(4):
        for e in (1, 2, 3):

            @pl.when(s >= e)
            def _():
                for n in range(2):
                    part = arrived(k, lax.rem(s - e + 4, 4), c, n)
                    moved(part, zsend.at[e - 1, k, n], zrecv.at[e - 1, k, n]).wait_recv()
                    relay(e, k, c, n).start()

    ag.finish()
    for k in range(4):
        z, near, mine = sends(k, columns[k])
        q_copy(k, columns[k]).wait()
        for n in range(2):
            near[n].wait_send()
            mine[n].wait()
            part = arrived(k, s, 1 - c, n)
            moved(part, ssend.at[k, n], srecv.at[k, n]).wait_recv()
            for e in (1, 2, 3):

                @pl.when(s + e < 4)
                def _():
                    z[n][e - 1].wait_send()

                @pl.when(s >= e)
                def _():
                    relay(e, k, c, n).wait_send()
                    relay(e, k, 1 - c, n).wait_recv()

    for k, where in enumerate(others):
        handed[k].wait_send()
        back = lax.rem(s - (k + 1) // 2 + 4, 4) * 2 + lax.rem(d - (k + 1) % 2 + 2, 2)
        pltpu.make_async_remote_copy(
            src_ref=outg.at[pl.ds(back * PAIR, PAIR)],
            dst_ref=dc.at[pl.ds(back * PAIR, PAIR)],
            send_sem=hsend.at[k],
            recv_sem=hrecv.at[k],
            device_id=where,
            device_id_type=MESH,
        ).wait_recv()
    keep.wait()
    for k, copy in enumerate(shared):
        copy.wait_send()
        if k:
            copy.wait_recv()


def attend_kernel(
    lo_ref, q_hbm, k_hbm, v_hbm, dc_in, o_ref, dc_out, q_ref, k_ref, v_ref, kpos, sc, mx, den, acc, sems
):
    loads = [
        pltpu.make_async_copy(a, b, sems.at[k])
        for k, (a, b) in enumerate(((q_hbm, q_ref), (k_hbm, k_ref), (v_hbm, v_ref)))
    ]
    for copy in loads:
        copy.start()
    passed = pltpu.make_async_copy(dc_in, dc_out, sems.at[3])
    passed.start()
    s, c = lax.axis_index("seq"), lax.rem(lax.axis_index("tensor"), 2)
    row = lax.broadcasted_iota(jnp.int32, (KT, 2 * LANES), 0)
    chips, local = lax.div(lax.rem(row, 256), ROWS), lax.rem(row, ROWS)
    kpos[...] = chips * LANES + lax.div(row, 256) * ROWS + local
    lane = lax.broadcasted_iota(jnp.int32, (1, LANES), 1)
    low_lanes = lane < ROWS
    for copy in loads:
        copy.wait()

    def tile(j, _):
        cx = lax.div(j, 2)
        pair = lax.rem(j, 2)
        lo2 = lo_ref[:, pl.ds(pl.multiple_of(cx * 2 * LANES, 2 * LANES), 2 * LANES)].astype(F32)
        one, two = lo2[:, :LANES], lo2[:, LANES:]
        low = jnp.where(c == 0, one, pltpu.roll(one, ROWS, 1))
        high = jnp.where(c == 0, pltpu.roll(two, ROWS, 1), two)
        lows = jnp.where(low_lanes, low, high)
        base = s * 1024 + cx * 2 * LANES + c * ROWS
        places = base + lane + jnp.where(low_lanes, 0, ROWS)
        least, most = jnp.min(lows).astype(jnp.int32), jnp.max(lows).astype(jnp.int32)
        lo_row = jnp.concatenate([lows, lows], axis=1).astype(jnp.int32)
        at_row = jnp.concatenate([places, places], axis=1)
        begin = lax.div(jnp.maximum(least, 0), KT)
        end = lax.div(base + LANES + ROWS - 1, KT) + 1
        mx[...] = jnp.full_like(mx, -jnp.inf)
        den[...] = jnp.zeros_like(den)
        acc[...] = jnp.zeros_like(acc)

        def score(t, _):
            sco = jnp.dot(k_ref[t], q_ref[cx, pair], preferred_element_type=F32)
            clear = (t * KT >= most) & (t * KT + KT - 1 <= base)

            @pl.when(clear)
            def _():
                sc[t] = sco
                mx[...] = jnp.maximum(mx[...], jnp.max(sco.reshape(KT // 8, 8, 2 * LANES), axis=0))

            @pl.when(jnp.logical_not(clear))
            def _():
                keys = kpos[...]
                seen = (keys >= lo_row - t * KT) & (keys <= at_row - t * KT)
                kept = jnp.where(seen, sco, -jnp.inf)
                sc[t] = kept
                mx[...] = jnp.maximum(mx[...], jnp.max(kept.reshape(KT // 8, 8, 2 * LANES), axis=0))

            return 0

        lax.fori_loop(begin, end, score, 0)
        top = jnp.max(mx[...], axis=0, keepdims=True)

        def mix(t, _):
            p = jnp.exp2(sc[t] - top)
            den[...] += jnp.sum(p.reshape(KT // 8, 8, 2 * LANES), axis=0)
            acc[0:HD, :] += jnp.dot(v_ref[t], p.astype(BF), preferred_element_type=F32)
            return 0

        lax.fori_loop(begin, end, mix, 0)
        out = acc[...] / jnp.sum(den[...], axis=0, keepdims=True)
        o_ref[cx, pair, 0] = out[:, :LANES].T.astype(BF)
        o_ref[cx, pair, 1] = out[:, LANES:].T.astype(BF)
        return 0

    lax.fori_loop(0, 8, tile, 0)
    passed.wait()


def last_kernel(
    heads, tok, gain, wo, wo_s, wg, wg_s, wu, wu_s, wd, wd_s,
    out,
    buf, res, part, hid, hv, wov, g0, g1, u0, u1, d0, d1, o1, i1, o2, i2,
    lsem, ag_send, ag_recv, s1, r1, s2, r2,
):
    ag = Gather(buf, ag_send, ag_recv)
    for where in (ag.a, ag.b, ag.o):
        signal(where)
    loads = [(heads, hv)]
    for e, src in enumerate((wo, wo_s)):
        for h in range(2):
            loads.append((src.at[pl.ds(h * HD, HD)], wov.at[pl.ds((2 * e + h) * LANES, HD)]))
    loads += [(wg, g0), (wg_s, g1), (wu, u0), (wu_s, u1), (wd, d0), (wd_s, d1)]
    copies = [pltpu.make_async_copy(a, b, lsem.at[k]) for k, (a, b) in enumerate(loads)]
    for copy in copies:
        copy.start()
    for h in range(4):
        wov[h * LANES + HD : (h + 1) * LANES, :] = jnp.zeros((LANES - HD, D), BF)
    for copy in copies[:5]:
        copy.wait()
    chunk = 512

    def wide(slot, terms):
        def one(n, _):
            cols = pl.ds(pl.multiple_of(n * chunk, chunk), chunk)
            total = None
            for left, right in terms:
                this = jnp.dot(left, right[:, cols], preferred_element_type=F32)
                total = this if total is None else total + this
            part[slot, :, :, cols] = total.reshape(2, ROWS, chunk)
            return 0

        lax.fori_loop(0, D // chunk, one, 0)
        return part.at[slot]

    rs = Scatter(o1, i1, s1, r1)

    def project(slot, cx):
        side = jnp.concatenate([hv[cx, h // 2, h % 2] for h in range(4)], axis=1)
        return wide(slot, [(side, wov)])

    far = project(0, rs.co)
    pl.semaphore_wait(pltpu.get_barrier_semaphore(), 3)
    rs.across(far)
    part_a = project(1, rs.ca)
    part_b = project(2, rs.cb)
    rs.sides(part_a, part_b)
    mine = project(3, rs.own)
    rs.rest(far, part_a, part_b, mine)
    chip = ag.x * 2 + ag.yh
    for i in range(NP):
        rows = pl.ds(i * PIECE, PIECE)
        total = tok[rows, :].astype(F32) + rs.final(mine, i)
        res[rows, :] = total
        buf[chip, rows, :] = normed(total, gain[...])
        ag.first(i)
    for copy in copies[5:]:
        copy.wait()

    def hidden(slot, cx):
        both = buf[pl.ds(2 * cx, 2)].reshape(2 * ROWS, D)
        for e, (g, u) in enumerate(((g0, u0), (g1, u1))):
            gate = dot_nt(both, g[...])
            up = dot_nt(both, u[...])
            hid[e] = (gate / (1.0 + jnp.exp(-gate)) * up).astype(BF)
        return wide(slot, [(hid[0], d0), (hid[1], d1)])

    rs2 = Scatter(o2, i2, s2, r2)
    ag.second()
    ag.third()
    mine = hidden(3, rs2.own)
    ag.fourth()
    ag.near(1)
    part_b = hidden(2, rs2.cb)
    ag.near(2)
    part_a = hidden(1, rs2.ca)
    rs2.sides(part_a, part_b)
    ag.far()
    far = hidden(0, rs2.co)
    rs2.across(far)
    rs2.rest(far, part_a, part_b, mine)
    for i in range(NP):
        rows = pl.ds(i * PIECE, PIECE)
        out[rows, :] = (res[rows, :] + rs2.final(mine, i)).astype(BF)
    ag.finish()
    rs.finish()
    rs2.finish()


VMEM_SPEC = pl.BlockSpec(memory_space=pltpu.VMEM)
SMEM_SPEC = pl.BlockSpec(memory_space=pltpu.SMEM)
ANY_SPEC = pl.BlockSpec(memory_space=pl.ANY)
HBM_SPEC = pl.BlockSpec(memory_space=pltpu.HBM)
DMA = pltpu.SemaphoreType.DMA


def shape(*dims, dtype=BF):
    return jax.ShapeDtypeStruct(dims, dtype)


def shards(
    tokens, attn_gain, w_query, w_key, w_value, w_out, mlp_gain, w_gate, w_up, w_down,
    positions, window_lo, cache_pool, req_len, req_owner, block_list,
):
    own_rows = tokens[0, 0]
    wq, wg, wu = w_query.T, w_gate.T, w_up.T

    q, k, v, wo_s, wg_s, wu_s, wd_s, dc = pl.pallas_call(
        first_kernel,
        out_shape=(
            shape(4, 2, LANES, 2 * LANES),
            shape(TILES, KT, LANES),
            shape(TILES, HD, KT),
            shape(*w_out.shape),
            shape(*wg.shape),
            shape(*wu.shape),
            shape(*w_down.shape),
            shape(OWNERS * PAIR, 2, MAXLEN * HD),
        ),
        in_specs=[VMEM_SPEC] * 4 + [SMEM_SPEC] * 3 + [ANY_SPEC] * 7,
        out_specs=(HBM_SPEC,) * 8,
        scratch_shapes=[
            VM((8, ROWS, D), BF),
            VM((6 * HD, D), BF),
            VM((D, 2 * LANES), BF),
            VM((D, 2 * LANES), BF),
            VM((OWNERS * PAIR, 2, MAXLEN * HD), BF),
            VM((4, 2, LANES, 2 * LANES), BF),
            VM((4, LANES, LANES), BF),
            VM((4, HD, LANES), BF),
            DMA((7, NP)),
            DMA((7, NP)),
            DMA((3,)),
            DMA((5,)),
            DMA((5,)),
            DMA((7,)),
            DMA((7,)),
            DMA,
            DMA((3, 4, 2)),
            DMA((3, 4, 2)),
            DMA((4, 2)),
            DMA((4, 2)),
            DMA((3, 4, 2)),
            DMA((3, 4, 2)),
            DMA((4, 2)),
            DMA((4,)),
        ],
        compiler_params=pltpu.CompilerParams(
            collective_id=0, has_side_effects=True, vmem_limit_bytes=32 << 20
        ),
        name="gather_project",
    )(
        own_rows, attn_gain.reshape(1, D), positions.reshape(1, 1024), cache_pool.reshape(NB, 2, BT * HD),
        req_len.reshape(RQ), req_owner.reshape(RQ), block_list.reshape(NB),
        wq, w_key, w_value, w_out, wg, wu, w_down,
    )

    heads, dc = pl.pallas_call(
        attend_kernel,
        out_shape=(shape(4, 2, 2, LANES, LANES), shape(*dc.shape)),
        in_specs=[VMEM_SPEC] + [ANY_SPEC] * 4,
        out_specs=(VMEM_SPEC, ANY_SPEC),
        scratch_shapes=[
            VM(q.shape, BF),
            VM(k.shape, BF),
            VM(v.shape, BF),
            VM((KT, 2 * LANES), jnp.int32),
            VM((TILES, KT, 2 * LANES), F32),
            VM((8, 2 * LANES), F32),
            VM((8, 2 * LANES), F32),
            VM((LANES, 2 * LANES), F32),
            DMA((4,)),
        ],
        compiler_params=pltpu.CompilerParams(vmem_limit_bytes=24 << 20),
        name="attend",
    )(window_lo.reshape(1, 1024), q, k, v, dc)

    layer_out = pl.pallas_call(
        last_kernel,
        out_shape=shape(ROWS, D),
        in_specs=[ANY_SPEC] + [VMEM_SPEC] * 2 + [ANY_SPEC] * 8,
        out_specs=VMEM_SPEC,
        scratch_shapes=[
            VM((8, ROWS, D), BF),
            VM((ROWS, D), F32),
            VM((4, 2, ROWS, D), F32),
            VM((2, 2 * ROWS, UN), BF),
            VM((4, 2, 2, LANES, LANES), BF),
            VM((4 * LANES, D), BF),
            VM((UN, D), BF),
            VM((UN, D), BF),
            VM((UN, D), BF),
            VM((UN, D), BF),
            VM((UN, D), BF),
            VM((UN, D), BF),
            VM((7, ROWS, D), BF),
            VM((7, ROWS, D), BF),
            VM((7, ROWS, D), BF),
            VM((7, ROWS, D), BF),
            DMA((11,)),
        ]
        + [DMA((7, NP))] * 6,
        compiler_params=pltpu.CompilerParams(
            collective_id=1, has_side_effects=True, vmem_limit_bytes=48 << 20
        ),
        name="mix_feed_forward",
    )(
        heads, own_rows, mlp_gain.reshape(1, D), w_out, wo_s, wg, wg_s, wu, wu_s, w_down, wd_s,
    )
    return (
        layer_out.reshape(1, 1, ROWS, D),
        dc.reshape(OWNERS * PAIR, 2, 1, MAXLEN * HD),
    )


def solution(mesh):
    in_specs = (
        P("dec", "seq", "tensor", None),
        P(),
        P(None, "tensor"),
        P(),
        P(),
        P("tensor", None),
        P(),
        P(None, "tensor"),
        P(None, "tensor"),
        P("tensor", None),
        P("dec", "seq", None),
        P("dec", "seq", None),
        P(("seq", "dec"), None, "tensor", None),
        P(("seq", "dec"), None),
        P(("seq", "dec"), None),
        P(("seq", "dec"), None),
    )
    out_specs = (P("dec", "seq", "tensor", None), P(("seq", "dec"), None, "tensor", None))
    return jax.shard_map(shards, mesh=mesh, in_specs=in_specs, out_specs=out_specs, check_vma=False)
```

```python
import functools

import jax
import jax.numpy as jnp
from jax import lax
from jax.experimental import pallas as pl
from jax.experimental.pallas import tpu as pltpu
from jax.sharding import PartitionSpec as P

HD = 80
D = 2560
BT = 16
MAXLEN = 128
PAIR = 2
RQ = 8
NB = 40
UN = 432
WIDE = 896
ROWS = 64
NP = 2
PIECE = ROWS // NP
LANES = 128
KT = 512
TILES = 8
OWNERS = 8

MESH = pl.DeviceIdType.MESH
VM = pltpu.VMEM
norm_eps = 1e-05
LOG_BASE = 9.210340371976184
SCALE = HD**-0.5 * 1.4426950408889634
F32 = jnp.float32
BF = jnp.bfloat16


def place():
    t = lax.axis_index("tensor")
    return lax.div(t, 4), lax.rem(lax.div(t, 2), 2), lax.rem(t, 2)


def at_chip(x, yh, c):
    return {"tensor": (lax.rem(x + 4, 4) * 2 + yh) * 2 + c}


def col4(x):
    return lax.rem(x + 4, 4)


def batch(r, own, ca, cb, co, m):
    c0 = jnp.where(r == 0, own, jnp.where(r == 3, co, cb))
    c1 = jnp.where(r == 0, own, jnp.where(r == 3, co, ca))
    r0 = jnp.where(r == 2, 1 - m, m)
    r1 = jnp.where(r == 1, m, 1 - m)
    return c0 * 2 + r0, c1 * 2 + r1


def normed(values, gain):
    mean_square = jnp.mean(values * values, axis=-1, keepdims=True)
    return (values * lax.rsqrt(mean_square + norm_eps) * gain).astype(BF)


class Gather:
    def __init__(self, buf, send, recv):
        self.x, self.yh, self.c = place()
        self.buf, self.send, self.recv = buf, send, recv
        x, m, c, p = self.x, self.yh, self.c, 1 - self.yh
        self.a, self.b, self.o = at_chip(x + 1, m, c), at_chip(x - 1, m, c), at_chip(x, p, c)
        own, ca, cb, co = col4(x), col4(x + 1), col4(x - 1), col4(x + 2)
        self.plan = [
            (own * 2 + m, self.o, own * 2 + p),
            (own * 2 + m, self.a, cb * 2 + m),
            (own * 2 + m, self.b, ca * 2 + m),
            (own * 2 + p, self.a, cb * 2 + p),
            (own * 2 + p, self.b, ca * 2 + p),
            (cb * 2 + m, self.a, co * 2 + m),
            (co * 2 + m, self.o, co * 2 + p),
            (ca * 2 + m, self.b, co * 2 + m),
        ]

    def copy(self, k, i, got):
        plan = self.plan[7 if k == 5 and i >= NP // 2 else k]
        part = self.buf.at[plan[2] if got else plan[0], pl.ds(i * PIECE, PIECE)]
        return pltpu.make_async_remote_copy(
            src_ref=part,
            dst_ref=part,
            send_sem=self.send.at[k, i],
            recv_sem=self.recv.at[k, i],
            device_id=plan[1],
            device_id_type=MESH,
        )

    def start(self, k, i):
        self.copy(k, i, False).start()

    def got(self, k, i):
        self.copy(k, i, True).wait_recv()

    def first(self, i):
        self.start(1, i)
        self.start(2, i)
        self.start(0, i)

    def second(self):
        for i in range(NP // 2):
            self.got(1, i)
            self.start(5, i)
            self.got(2, NP - 1 - i)
            self.start(5, NP - 1 - i)

    def third(self):
        for i in range(NP):
            self.got(0, i)
            self.start(3, i)
            self.start(4, i)

    def fourth(self):
        for i in range(NP // 2):
            for e in (i, NP - 1 - i):
                self.got(5, e)
                self.start(6, e)

    def near_own(self):
        for i in range(NP // 2):
            self.got(1, NP - 1 - i)
            self.got(2, i)

    def near_partner(self):
        for i in range(NP):
            self.got(3, i)
            self.got(4, i)

    def far(self):
        for i in range(NP):
            self.got(6, i)

    def finish(self):
        for k in range(7):
            for i in range(NP):
                self.copy(k, i, False).wait_send()


class Scatter:
    def __init__(self, part, out, inb, send, recv):
        x, yh, c = place()
        self.part, self.out, self.inb, self.send, self.recv = part, out, inb, send, recv
        self.a, self.b = at_chip(x + 1, yh, c), at_chip(x - 1, yh, c)
        o = at_chip(x, 1 - yh, c)
        self.to = [o, self.a, self.b, None, self.a, self.b, o]

    def copy(self, k, i):
        rows = pl.ds(i * PIECE, PIECE)
        to = self.to[k] if k != 3 else (self.a if i < NP // 2 else self.b)
        return pltpu.make_async_remote_copy(
            src_ref=self.out.at[k, rows],
            dst_ref=self.inb.at[k, rows],
            send_sem=self.send.at[k, i],
            recv_sem=self.recv.at[k, i],
            device_id=to,
            device_id_type=MESH,
        )

    def summed(self, part, i, adds):
        rows = pl.ds(i * PIECE, PIECE)
        total = self.part[part[0], part[1], rows, :]
        for e in adds:
            self.copy(e, i).wait_recv()
            total = total + self.inb[e, rows, :].astype(F32)
        return total

    def put(self, k, part, i, adds=()):
        self.out[k, pl.ds(i * PIECE, PIECE), :] = self.summed(part, i, adds).astype(BF)
        self.copy(k, i).start()

    def sides(self):
        for i in range(NP):
            self.put(1, (2, 1), i)
            self.put(2, (2, 0), i)

    def across(self):
        for i in range(NP // 2):
            self.put(0, (3, 1), i)
            self.put(0, (3, 1), NP - 1 - i)

    def rest(self):
        for i in range(NP // 2):
            self.put(3, (3, 0), i, (0,))
            self.put(3, (3, 0), NP - 1 - i, (0,))
        for i in range(NP):
            self.put(6, (0, 1), i, (1, 2))
        for i in range(NP // 2):
            self.put(4, (1, 1), NP - 1 - i)
            self.put(5, (1, 0), i)
        for i in range(NP // 2):
            self.put(4, (1, 1), i, (3,))
            self.put(5, (1, 0), NP - 1 - i, (3,))

    def final(self, i):
        return self.summed((0, 0), i, (6, 4, 5))

    def finish(self):
        for k in range(7):
            for i in range(NP):
                self.copy(k, i).wait_send()


def signal(where):
    pl.semaphore_signal(
        pltpu.get_barrier_semaphore(), inc=1, device_id=where, device_id_type=MESH
    )


def dot_nt(left, right):
    return lax.dot_general(left, right, (((1,), (1,)), ((), ())), preferred_element_type=F32)


def first_kernel(
    tok, gain, pos, pool, lens, owners, listing, wq, wk, wv, wo, wg, wu, wd,
    q_out, kv_out, wo_s, wg_s, wu_s, wd_s, dc,
    buf, wall, wkw, wvw, outg, qst, kvst,
    ag_send, ag_recv, lsem, wsend, wrecv, hsend, hrecv, hlocal,
    zsend, zrecv, ssend, srecv, rsend, rrecv, kvl, qsem,
):
    x, yh, c = place()
    s, d = lax.axis_index("seq"), lax.axis_index("dec")
    chip = x * 2 + yh
    sib = at_chip(x, yh, 1 - c)
    start = jnp.minimum(lax.div(chip * HD, LANES), 3) * LANES
    off = chip * HD - start
    cols = pl.ds(pl.multiple_of(start, LANES), 2 * LANES)
    local = [
        pltpu.make_async_copy(wq, wall.at[pl.ds(0, 2 * HD)], lsem.at[0]),
        pltpu.make_async_copy(wk.at[:, cols], wkw, lsem.at[1]),
        pltpu.make_async_copy(wv.at[:, cols], wvw, lsem.at[2]),
    ]
    for copy in local:
        copy.start()
    ag = Gather(buf, ag_send, ag_recv)
    for where in (ag.a, ag.b, ag.o, sib):
        signal(where)
    others = []
    for k in range(1, OWNERS):
        ds, dd = k // 2, k % 2
        others.append({"seq": lax.rem(s + ds, 4), "dec": lax.rem(d + dd, 2)})
    for where in others:
        signal(where)
    buf[chip] = normed(tok[...].astype(F32), gain[...])
    pl.semaphore_wait(pltpu.get_barrier_semaphore(), 4 + len(others))
    for i in range(NP):
        ag.first(i)
    shared = [
        pltpu.make_async_remote_copy(
            src_ref=a, dst_ref=b, send_sem=wsend.at[k], recv_sem=wrecv.at[k],
            device_id=sib, device_id_type=MESH,
        )
        for k, (a, b) in enumerate(
            ((wq, wall.at[pl.ds(2 * HD, 2 * HD)]), (wo, wo_s), (wg, wg_s), (wu, wu_s), (wd, wd_s))
        )
    ]
    for copy in shared:
        copy.start()

    counts = [lax.div(lens[k] + (BT - 1), BT) for k in range(RQ)]
    firsts, so_far = [], jnp.int32(0)
    for k in range(RQ):
        firsts.append(so_far)
        so_far = so_far + counts[k]
    ranks = []
    for k in range(RQ):
        rank = jnp.int32(0)
        for e in range(k):
            rank = rank + (owners[e] == owners[k]).astype(jnp.int32)
        ranks.append(rank)
    feature = lax.broadcasted_iota(jnp.int32, (2, BT * HD), 1)

    def cut(o, _):
        for r in range(PAIR):
            at, length = jnp.int32(0), jnp.int32(0)
            for k in range(RQ):
                hit = (owners[k] == o) & (ranks[k] == r)
                at = jnp.where(hit, firsts[k], at)
                length = jnp.where(hit, lens[k], length)
            for b in range(MAXLEN // BT):
                block = pool[listing[jnp.minimum(at + b, NB - 1)]].astype(F32)
                kept = jnp.where(feature < (length - BT * b) * HD, block, 0.0)
                outg[o * PAIR + r, :, BT * HD * b : BT * HD * (b + 1)] = kept.astype(BF)
        return 0

    lax.fori_loop(0, OWNERS, cut, 0)
    me = s * 2 + d
    handed = []
    for k, where in enumerate(others):
        there = where["seq"] * 2 + where["dec"]
        handed.append(
            pltpu.make_async_remote_copy(
                src_ref=outg.at[pl.ds(there * PAIR, PAIR)],
                dst_ref=dc.at[pl.ds(me * PAIR, PAIR)],
                send_sem=hsend.at[k],
                recv_sem=hrecv.at[k],
                device_id=where,
                device_id_type=MESH,
            )
        )
    keep = pltpu.make_async_copy(
        outg.at[pl.ds(me * PAIR, PAIR)], dc.at[pl.ds(me * PAIR, PAIR)], hlocal
    )
    ag.second()
    for k in (1, 3, 5, 0, 2):
        handed[k].start()
    keep.start()

    row = lax.broadcasted_iota(jnp.int32, (HD, 2 * LANES), 0)
    col = lax.broadcasted_iota(jnp.int32, (HD, 2 * LANES), 1)
    pick = (col == row + off).astype(F32).astype(BF)
    chunk = 512

    def laid(src, begin):
        def one(i, _):
            rows = pl.ds(pl.multiple_of(i * chunk, chunk), chunk)
            wall[begin : begin + HD, rows] = dot_nt(pick, src[rows, :]).astype(BF)
            return 0

        lax.fori_loop(0, D // chunk, one, 0)

    for copy in local:
        copy.wait()
    laid(wkw, 4 * HD)
    laid(wvw, 5 * HD)
    half = HD // 2
    rate = jnp.exp(
        lax.broadcasted_iota(jnp.int32, (half, 1), 0).astype(F32) * (-2.0 / HD * LOG_BASE)
    )
    low_lanes = lax.broadcasted_iota(jnp.int32, (1, LANES), 1) < ROWS

    def own_half(two, one_more):
        low = jnp.where(c == 0, two, pltpu.roll(two, ROWS, 1))
        high = jnp.where(c == 0, pltpu.roll(one_more, ROWS, 1), one_more)
        return jnp.where(low_lanes, low, high)

    def lanes_of(core):
        return pl.ds(pl.multiple_of(core * 256, 256), 256)

    def moved(src, dst, send, recv, where):
        return pltpu.make_async_remote_copy(
            src_ref=src, dst_ref=dst, send_sem=send, recv_sem=recv, device_id=where, device_id_type=MESH
        )

    def to_later(e, k):
        dst = kv_out.at[s * 2 + k, :, lanes_of(c)]
        return moved(kvst.at[k], dst, zsend.at[e - 1, k], zrecv.at[e - 1, k], {"seq": lax.rem(s + e, 4)})

    def to_sibling(k):
        dst = kv_out.at[s * 2 + k, :, lanes_of(c)]
        return moved(kvst.at[k], dst, ssend.at[k], srecv.at[k], sib)

    def from_earlier(e, k, core, send, recv):
        part = kv_out.at[lax.rem(s - e + 4, 4) * 2 + k, :, lanes_of(core)]
        return moved(part, part, send.at[e - 1, k], recv.at[e - 1, k], sib)

    def own_copies(k):
        return (
            pltpu.make_async_copy(kvst.at[k], kv_out.at[s * 2 + k, :, lanes_of(c)], kvl.at[k]),
            pltpu.make_async_copy(qst.at[pl.ds(2 * k, 2)], q_out.at[pl.ds(2 * k, 2)], qsem.at[k]),
        )

    def rotated(v, cosine, sine):
        a, b = v[:half], v[half:]
        return jnp.concatenate([a * cosine - b * sine, b * cosine + a * sine], axis=0)

    def chip_lanes(ref, n):
        return ref[:, pl.ds(pl.multiple_of(n * LANES, LANES), LANES)].astype(F32)

    def project(k, _):
        @pl.when(k == 0)
        def _():
            ag.third()
            shared[0].wait_recv()
            ag.near_own()

        @pl.when(k == 1)
        def _():
            ag.fourth()
            for e in (4, 6):
                handed[e].start()
            ag.near_partner()
            ag.far()

        four = []
        for r in (2 * k, 2 * k + 1):
            four += list(batch(r, x, col4(x + 1), col4(x - 1), col4(x + 2), yh))
        shards_in = jnp.concatenate([buf[n] for n in four], axis=0)
        out = dot_nt(wall[...], shards_in)
        places = jnp.concatenate(
            [
                own_half(chip_lanes(pos, four[0]), chip_lanes(pos, four[1])),
                own_half(chip_lanes(pos, four[2]), chip_lanes(pos, four[3])),
            ],
            axis=1,
        )
        angles = rate * places
        cosine, sine = jnp.cos(angles), jnp.sin(angles)
        kvst[k, 0:HD] = rotated(out[4 * HD : 5 * HD], cosine, sine).astype(BF)
        kvst[k, HD:] = out[5 * HD :].astype(BF)
        for e in (1, 2, 3):

            @pl.when(s + e < 4)
            def _():
                to_later(e, k).start()

        to_sibling(k).start()
        for h in range(4):
            v = (rotated(out[h * HD : (h + 1) * HD], cosine, sine) * SCALE).astype(BF)
            for n in range(2):
                qst[2 * k + n, h // 2, :, (h % 2) * LANES : (h % 2 + 1) * LANES] = v[
                    :, n * LANES : (n + 1) * LANES
                ]
        for copy in own_copies(k):
            copy.start()
        return 0

    lax.fori_loop(0, 2, project, 0)
    for k in range(2):
        for e in (1, 2, 3):

            @pl.when(s >= e)
            def _():
                from_earlier(e, k, c, zsend, zrecv).wait_recv()
                from_earlier(e, k, c, rsend, rrecv).start()

    ag.finish()
    for k in range(2):
        to_sibling(k).wait_send()
        for copy in own_copies(k):
            copy.wait()
        part = kv_out.at[s * 2 + k, :, lanes_of(1 - c)]
        moved(part, part, ssend.at[k], srecv.at[k], sib).wait_recv()
        for e in (1, 2, 3):

            @pl.when(s + e < 4)
            def _():
                to_later(e, k).wait_send()

            @pl.when(s >= e)
            def _():
                from_earlier(e, k, c, rsend, rrecv).wait_send()
                from_earlier(e, k, 1 - c, rsend, rrecv).wait_recv()

    for k, where in enumerate(others):
        handed[k].wait_send()
        back = lax.rem(s - (k + 1) // 2 + 4, 4) * 2 + lax.rem(d - (k + 1) % 2 + 2, 2)
        pltpu.make_async_remote_copy(
            src_ref=outg.at[pl.ds(back * PAIR, PAIR)],
            dst_ref=dc.at[pl.ds(back * PAIR, PAIR)],
            send_sem=hsend.at[k],
            recv_sem=hrecv.at[k],
            device_id=where,
            device_id_type=MESH,
        ).wait_recv()
    keep.wait()
    for k, copy in enumerate(shared):
        copy.wait_send()
        if k:
            copy.wait_recv()


def attend_kernel(
    lo_ref, q_hbm, kv_hbm, dc_in, o_ref, dc_out, q_ref, kv_ref, o_vm, kpos, sc, mx, den, acc, sems
):
    loads = [
        pltpu.make_async_copy(q_hbm, q_ref, sems.at[0]),
        pltpu.make_async_copy(kv_hbm, kv_ref, sems.at[1]),
    ]
    for copy in loads:
        copy.start()
    passed = pltpu.make_async_copy(dc_in, dc_out, sems.at[3])
    passed.start()
    x, yh, c = place()
    s = lax.axis_index("seq")
    ring = (x, col4(x + 1), col4(x - 1), col4(x + 2), yh)
    row = lax.broadcasted_iota(jnp.int32, (2 * LANES, 2 * LANES), 0)
    quarter, local = lax.div(row, ROWS), lax.rem(row, ROWS)
    first, last = [], []
    for e in range(2):
        chips = batch(2 * e, *ring) + batch(2 * e + 1, *ring)
        chip = jnp.where(
            quarter < 2, jnp.where(quarter == 0, chips[0], chips[1]), jnp.where(quarter == 2, chips[2], chips[3])
        )
        for core in range(2):
            kpos[e, core * 256 : core * 256 + 256] = chip * LANES + core * ROWS + local
        low = jnp.minimum(jnp.minimum(chips[0], chips[1]), jnp.minimum(chips[2], chips[3]))
        high = jnp.maximum(jnp.maximum(chips[0], chips[1]), jnp.maximum(chips[2], chips[3]))
        first.append(low * LANES)
        last.append(high * LANES + LANES - 1)
    lane = lax.broadcasted_iota(jnp.int32, (1, LANES), 1)
    low_lanes = lane < ROWS
    for copy in loads:
        copy.wait()

    def tile(j, _):
        r, pair = lax.div(j, 2), lax.rem(j, 2)
        n0, n1 = batch(r, *ring)
        one = lo_ref[:, pl.ds(pl.multiple_of(n0 * LANES, LANES), LANES)].astype(F32)
        two = lo_ref[:, pl.ds(pl.multiple_of(n1 * LANES, LANES), LANES)].astype(F32)
        low = jnp.where(c == 0, one, pltpu.roll(one, ROWS, 1))
        high = jnp.where(c == 0, pltpu.roll(two, ROWS, 1), two)
        lows = jnp.where(low_lanes, low, high)
        base = s * 1024 + c * ROWS
        places = base + jnp.where(low_lanes, n0 * LANES + lane, n1 * LANES + lane - ROWS)
        q_first = base + jnp.minimum(n0, n1) * LANES
        q_last = base + jnp.maximum(n0, n1) * LANES + ROWS - 1
        least, most = jnp.min(lows).astype(jnp.int32), jnp.max(lows).astype(jnp.int32)
        lo_row = jnp.concatenate([lows, lows], axis=1).astype(jnp.int32)
        at_row = jnp.concatenate([places, places], axis=1)
        begin = lax.div(jnp.maximum(least, 0), 1024) * 2
        end = 2 * s + 2
        mx[...] = jnp.full_like(mx, -jnp.inf)
        den[...] = jnp.zeros_like(den)
        acc[...] = jnp.zeros_like(acc)

        def reach(t):
            e, block = lax.rem(t, 2), lax.div(t, 2) * 1024
            return (
                e,
                block,
                block + jnp.where(e == 0, first[0], first[1]),
                block + jnp.where(e == 0, last[0], last[1]),
            )

        def score(t, _):
            e, block, key_first, key_last = reach(t)
            clear = (key_first >= most) & (key_last <= q_first)
            touched = (key_last >= least) & (key_first <= q_last)

            def product():
                return lax.dot_general(
                    kv_ref[t, 0:HD], q_ref[r, pair], (((0,), (0,)), ((), ())), preferred_element_type=F32
                )

            @pl.when(clear)
            def _():
                sco = product()
                sc[t] = sco
                mx[...] = jnp.maximum(mx[...], jnp.max(sco.reshape(KT // 8, 8, 2 * LANES), axis=0))

            @pl.when(jnp.logical_not(clear) & touched)
            def _():
                keys = kpos[e]
                seen = (keys >= lo_row - block) & (keys <= at_row - block)
                kept = jnp.where(seen, product(), -jnp.inf)
                sc[t] = kept
                mx[...] = jnp.maximum(mx[...], jnp.max(kept.reshape(KT // 8, 8, 2 * LANES), axis=0))

            return 0

        lax.fori_loop(begin, end, score, 0)
        top = jnp.max(mx[...], axis=0, keepdims=True)

        def mix(t, _):
            e, block, key_first, key_last = reach(t)

            @pl.when((key_last >= least) & (key_first <= q_last))
            def _():
                p = jnp.exp2(sc[t] - top)
                den[...] += jnp.sum(p.reshape(KT // 8, 8, 2 * LANES), axis=0)
                acc[0:HD, :] += jnp.dot(
                    kv_ref[t, HD:], p.astype(BF), preferred_element_type=F32
                )

            return 0

        lax.fori_loop(begin, end, mix, 0)
        out = acc[...] / jnp.sum(den[...], axis=0, keepdims=True)
        o_vm[r, pair, 0] = out[:, :LANES].T.astype(BF)
        o_vm[r, pair, 1] = out[:, LANES:].T.astype(BF)
        return 0

    lax.fori_loop(0, 8, tile, 0)
    result = pltpu.make_async_copy(o_vm, o_ref, sems.at[2])
    result.start()
    passed.wait()
    result.wait()


def last_kernel(
    heads, tok, gain, wo, wo_s, wg, wg_s, wu, wu_s, wd, wd_s,
    out,
    buf, res, part, hv, wov, raw, wt, ds, o1, i1, o2, i2,
    lsem, ag_send, ag_recv, s1, r1, s2, r2,
):
    ag = Gather(buf, ag_send, ag_recv)
    for where in (ag.a, ag.b, ag.o):
        signal(where)
    loads = [(heads, hv)]
    for e, src in enumerate((wo, wo_s)):
        for h in range(2):
            loads.append((src.at[pl.ds(h * HD, HD)], wov.at[pl.ds((2 * e + h) * LANES, HD)]))
    for e, src in enumerate((wg, wg_s, wu, wu_s)):
        loads.append((src, raw.at[e // 2, pl.ds(e % 2 * UN, UN)]))
    for e, src in enumerate((wd, wd_s)):
        loads.append((src, ds.at[pl.ds(e * UN, UN)]))
    copies = [pltpu.make_async_copy(a, b, lsem.at[k]) for k, (a, b) in enumerate(loads)]
    for copy in copies:
        copy.start()
    for h in range(4):
        wov[h * LANES + HD : (h + 1) * LANES, :] = jnp.zeros((LANES - HD, D), BF)
    raw[:, 2 * UN :, :] = jnp.zeros((2, WIDE - 2 * UN, D), BF)
    ds[2 * UN :, :] = jnp.zeros((WIDE - 2 * UN, D), BF)
    for copy in copies[:5]:
        copy.wait()
    x, m = ag.x, ag.yh
    ring = (x, col4(x + 1), col4(x - 1), col4(x + 2), m)
    rs = Scatter(part, o1, i1, s1, r1)

    def project(n, _):
        r = lax.rem(n + 2, 4)
        side = jnp.concatenate([hv[r, h // 2, h % 2] for h in range(4)], axis=1)
        part[r] = jnp.dot(side, wov[...], preferred_element_type=F32).reshape(2, ROWS, D)

        @pl.when(n == 0)
        def _():
            pl.semaphore_wait(pltpu.get_barrier_semaphore(), 3)
            rs.sides()

        @pl.when(n == 1)
        def _():
            rs.across()

        return 0

    lax.fori_loop(0, 4, project, 0)
    for copy in copies[5:]:
        copy.wait()

    def turn(n, _):
        cols = pl.ds(pl.multiple_of(n * 256, 256), 256)
        for e in range(2):
            wt[cols, e * WIDE : (e + 1) * WIDE] = raw[e, :, cols].astype(F32).T.astype(BF)
        return 0

    lax.fori_loop(0, D // 256, turn, 0)
    rs.rest()
    chip = x * 2 + m
    for i in range(NP):
        rows = pl.ds(i * PIECE, PIECE)
        total = tok[rows, :].astype(F32) + rs.final(i)
        res[rows, :] = total
        buf[chip, rows, :] = normed(total, gain[...])
        ag.first(i)

    rs2 = Scatter(part, o2, i2, s2, r2)
    ag.second()
    ag.third()

    def feed(r, _):
        @pl.when(r == 1)
        def _():
            ag.near_own()

        @pl.when(r == 2)
        def _():
            ag.fourth()
            ag.near_partner()

        @pl.when(r == 3)
        def _():
            rs2.sides()
            ag.far()

        n0, n1 = batch(r, *ring)
        both = jnp.concatenate([buf[n0], buf[n1]], axis=0)
        wide = jnp.dot(both, wt[...], preferred_element_type=F32)
        gate, up = wide[:, :WIDE], wide[:, WIDE:]
        hid = (gate / (1.0 + jnp.exp(-gate)) * up).astype(BF)
        part[r] = jnp.dot(hid, ds[...], preferred_element_type=F32).reshape(2, ROWS, D)
        return 0

    lax.fori_loop(0, 4, feed, 0)
    rs2.across()
    rs2.rest()
    for i in range(NP):
        rows = pl.ds(i * PIECE, PIECE)
        out[rows, :] = (res[rows, :] + rs2.final(i)).astype(BF)
    ag.finish()
    rs.finish()
    rs2.finish()


VMEM_SPEC = pl.BlockSpec(memory_space=pltpu.VMEM)
SMEM_SPEC = pl.BlockSpec(memory_space=pltpu.SMEM)
HBM_SPEC = pl.BlockSpec(memory_space=pltpu.HBM)
DMA = pltpu.SemaphoreType.DMA


def shape(*dims, dtype=BF):
    return jax.ShapeDtypeStruct(dims, dtype)


def shards(
    tokens, attn_gain, w_query, w_key, w_value, w_out, mlp_gain, w_gate, w_up, w_down,
    positions, window_lo, cache_pool, req_len, req_owner, block_list,
):
    own_rows = tokens[0, 0]
    wq, wg, wu = w_query.T, w_gate.T, w_up.T

    q, kv, wo_s, wg_s, wu_s, wd_s, dc = pl.pallas_call(
        first_kernel,
        out_shape=(
            shape(4, 2, HD, 2 * LANES),
            shape(TILES, 2 * HD, KT),
            shape(*w_out.shape),
            shape(*wg.shape),
            shape(*wu.shape),
            shape(*w_down.shape),
            shape(OWNERS * PAIR, 2, MAXLEN * HD),
        ),
        in_specs=[VMEM_SPEC] * 4 + [SMEM_SPEC] * 3 + [HBM_SPEC] * 7,
        out_specs=(HBM_SPEC,) * 7,
        scratch_shapes=[
            VM((8, ROWS, D), BF),
            VM((6 * HD, D), BF),
            VM((D, 2 * LANES), BF),
            VM((D, 2 * LANES), BF),
            VM((OWNERS * PAIR, 2, MAXLEN * HD), BF),
            VM((4, 2, HD, 2 * LANES), BF),
            VM((2, 2 * HD, 2 * LANES), BF),
            DMA((7, NP)),
            DMA((7, NP)),
            DMA((3,)),
            DMA((5,)),
            DMA((5,)),
            DMA((7,)),
            DMA((7,)),
            DMA,
            DMA((3, 2)),
            DMA((3, 2)),
            DMA((2,)),
            DMA((2,)),
            DMA((3, 2)),
            DMA((3, 2)),
            DMA((2,)),
            DMA((2,)),
        ],
        compiler_params=pltpu.CompilerParams(
            collective_id=0, has_side_effects=True, vmem_limit_bytes=32 << 20
        ),
        name="gather_project",
    )(
        own_rows, attn_gain.reshape(1, D), positions.reshape(1, 1024), cache_pool.reshape(NB, 2, BT * HD),
        req_len.reshape(RQ), req_owner.reshape(RQ), block_list.reshape(NB),
        wq, w_key, w_value, w_out, wg, wu, w_down,
    )

    heads, dc = pl.pallas_call(
        attend_kernel,
        out_shape=(shape(4, 2, 2, LANES, LANES), shape(*dc.shape)),
        in_specs=[VMEM_SPEC] + [HBM_SPEC] * 3,
        out_specs=(HBM_SPEC, HBM_SPEC),
        scratch_shapes=[
            VM(q.shape, BF),
            VM(kv.shape, BF),
            VM((4, 2, 2, LANES, LANES), BF),
            VM((2, KT, 2 * LANES), jnp.int32),
            VM((TILES, KT, 2 * LANES), F32),
            VM((8, 2 * LANES), F32),
            VM((8, 2 * LANES), F32),
            VM((LANES, 2 * LANES), F32),
            DMA((4,)),
        ],
        compiler_params=pltpu.CompilerParams(vmem_limit_bytes=24 << 20),
        name="attend",
    )(window_lo.reshape(1, 1024), q, kv, dc)

    layer_out = pl.pallas_call(
        last_kernel,
        out_shape=shape(ROWS, D),
        in_specs=[HBM_SPEC] + [VMEM_SPEC] * 2 + [HBM_SPEC] * 8,
        out_specs=VMEM_SPEC,
        scratch_shapes=[
            VM((8, ROWS, D), BF),
            VM((ROWS, D), F32),
            VM((4, 2, ROWS, D), F32),
            VM((4, 2, 2, LANES, LANES), BF),
            VM((4 * LANES, D), BF),
            VM((2, WIDE, D), BF),
            VM((D, 2 * WIDE), BF),
            VM((WIDE, D), BF),
            VM((7, ROWS, D), BF),
            VM((7, ROWS, D), BF),
            VM((7, ROWS, D), BF),
            VM((7, ROWS, D), BF),
            DMA((11,)),
        ]
        + [DMA((7, NP))] * 6,
        compiler_params=pltpu.CompilerParams(
            collective_id=1, has_side_effects=True, vmem_limit_bytes=54 << 20
        ),
        name="mix_feed_forward",
    )(
        heads, own_rows, mlp_gain.reshape(1, D), w_out, wo_s, wg, wg_s, wu, wu_s, w_down, wd_s,
    )
    return (
        layer_out.reshape(1, 1, ROWS, D),
        dc.reshape(OWNERS * PAIR, 2, 1, MAXLEN * HD),
    )


def solution(mesh):
    in_specs = (
        P("dec", "seq", "tensor", None),
        P(),
        P(None, "tensor"),
        P(),
        P(),
        P("tensor", None),
        P(),
        P(None, "tensor"),
        P(None, "tensor"),
        P("tensor", None),
        P("dec", "seq", None),
        P("dec", "seq", None),
        P(("seq", "dec"), None, "tensor", None),
        P(("seq", "dec"), None),
        P(("seq", "dec"), None),
        P(("seq", "dec"), None),
    )
    out_specs = (P("dec", "seq", "tensor", None), P(("seq", "dec"), None, "tensor", None))
    return jax.shard_map(shards, mesh=mesh, in_specs=in_specs, out_specs=out_specs, check_vma=False)
```

```python
import functools

import jax
import jax.numpy as jnp
from jax import lax
from jax.experimental import pallas as pl
from jax.experimental.pallas import tpu as pltpu
from jax.sharding import PartitionSpec as P

HD = 80
D = 2560
BT = 16
MAXLEN = 128
PAIR = 2
RQ = 8
NB = 40
UN = 432
WIDE = 896
ROWS = 64
NP = 2
PIECE = ROWS // NP
LANES = 128
KT = 512
TILES = 8
GRANT = 60 << 20
OWNERS = 8

MESH = pl.DeviceIdType.MESH
VM = pltpu.VMEM
norm_eps = 1e-05
LOG_BASE = 9.210340371976184
SCALE = HD**-0.5 * 1.4426950408889634
F32 = jnp.float32
BF = jnp.bfloat16


def place():
    t = lax.axis_index("tensor")
    return lax.div(t, 4), lax.rem(lax.div(t, 2), 2), lax.rem(t, 2)


def at_chip(x, yh, c):
    return {"tensor": (lax.rem(x + 4, 4) * 2 + yh) * 2 + c}


def col4(x):
    return lax.rem(x + 4, 4)


def batch(r, own, ca, cb, co, m):
    c0 = jnp.where(r == 0, own, jnp.where(r == 3, co, cb))
    c1 = jnp.where(r == 0, own, jnp.where(r == 3, co, ca))
    r0 = jnp.where(r == 2, 1 - m, m)
    r1 = jnp.where(r == 1, m, 1 - m)
    return c0 * 2 + r0, c1 * 2 + r1


def normed(values, gain):
    mean_square = jnp.mean(values * values, axis=-1, keepdims=True)
    return (values * lax.rsqrt(mean_square + norm_eps) * gain).astype(BF)


class Gather:
    def __init__(self, buf, send, recv):
        self.x, self.yh, self.c = place()
        self.buf, self.send, self.recv = buf, send, recv
        x, m, c, p = self.x, self.yh, self.c, 1 - self.yh
        self.a, self.b, self.o = at_chip(x + 1, m, c), at_chip(x - 1, m, c), at_chip(x, p, c)
        own, ca, cb, co = col4(x), col4(x + 1), col4(x - 1), col4(x + 2)
        self.plan = [
            (own * 2 + m, self.o, own * 2 + p),
            (own * 2 + m, self.a, cb * 2 + m),
            (own * 2 + m, self.b, ca * 2 + m),
            (own * 2 + p, self.a, cb * 2 + p),
            (own * 2 + p, self.b, ca * 2 + p),
            (cb * 2 + m, self.a, co * 2 + m),
            (co * 2 + m, self.o, co * 2 + p),
            (ca * 2 + m, self.b, co * 2 + m),
        ]

    def copy(self, k, i, got):
        plan = self.plan[7 if k == 5 and i >= NP // 2 else k]
        part = self.buf.at[plan[2] if got else plan[0], pl.ds(i * PIECE, PIECE)]
        return pltpu.make_async_remote_copy(
            src_ref=part,
            dst_ref=part,
            send_sem=self.send.at[k, i],
            recv_sem=self.recv.at[k, i],
            device_id=plan[1],
            device_id_type=MESH,
        )

    def start(self, k, i):
        self.copy(k, i, False).start()

    def got(self, k, i):
        self.copy(k, i, True).wait_recv()

    def first(self, i):
        self.start(1, i)
        self.start(2, i)
        self.start(0, i)

    def second(self):
        for i in range(NP // 2):
            self.got(1, i)
            self.start(5, i)
            self.got(2, NP - 1 - i)
            self.start(5, NP - 1 - i)

    def third(self):
        for i in range(NP):
            self.got(0, i)
            self.start(3, i)
            self.start(4, i)

    def fourth(self):
        for i in range(NP // 2):
            for e in (i, NP - 1 - i):
                self.got(5, e)
                self.start(6, e)

    def near_own(self):
        for i in range(NP // 2):
            self.got(1, NP - 1 - i)
            self.got(2, i)

    def near_partner(self):
        for i in range(NP):
            self.got(3, i)
            self.got(4, i)

    def far(self):
        for i in range(NP):
            self.got(6, i)

    def finish(self):
        for k in range(7):
            for i in range(NP):
                self.copy(k, i, False).wait_send()


class Scatter:
    def __init__(self, part, out, inb, send, recv):
        x, yh, c = place()
        self.part, self.out, self.inb, self.send, self.recv = part, out, inb, send, recv
        self.a, self.b = at_chip(x + 1, yh, c), at_chip(x - 1, yh, c)
        o = at_chip(x, 1 - yh, c)
        self.to = [o, self.a, self.b, None, self.a, self.b, o]

    def copy(self, k, i):
        rows = pl.ds(i * PIECE, PIECE)
        to = self.to[k] if k != 3 else (self.a if i < NP // 2 else self.b)
        return pltpu.make_async_remote_copy(
            src_ref=self.out.at[k, rows],
            dst_ref=self.inb.at[k, rows],
            send_sem=self.send.at[k, i],
            recv_sem=self.recv.at[k, i],
            device_id=to,
            device_id_type=MESH,
        )

    def summed(self, part, i, adds):
        rows = pl.ds(i * PIECE, PIECE)
        total = self.part[part[0], part[1], rows, :]
        for e in adds:
            self.copy(e, i).wait_recv()
            total = total + self.inb[e, rows, :].astype(F32)
        return total

    def put(self, k, part, i, adds=()):
        self.out[k, pl.ds(i * PIECE, PIECE), :] = self.summed(part, i, adds).astype(BF)
        self.copy(k, i).start()

    def sides(self):
        for i in range(NP):
            self.put(1, (2, 1), i)
            self.put(2, (2, 0), i)

    def across(self):
        for i in range(NP // 2):
            self.put(0, (3, 1), i)
            self.put(0, (3, 1), NP - 1 - i)

    def rest(self):
        for i in range(NP // 2):
            self.put(3, (3, 0), i, (0,))
            self.put(3, (3, 0), NP - 1 - i, (0,))
        for i in range(NP):
            self.put(6, (0, 1), i, (1, 2))
        for i in range(NP // 2):
            self.put(4, (1, 1), NP - 1 - i)
            self.put(5, (1, 0), i)
        for i in range(NP // 2):
            self.put(4, (1, 1), i, (3,))
            self.put(5, (1, 0), NP - 1 - i, (3,))

    def final(self, i):
        return self.summed((0, 0), i, (6, 4, 5))

    def finish(self):
        for k in range(7):
            for i in range(NP):
                self.copy(k, i).wait_send()


def signal(where):
    pl.semaphore_signal(
        pltpu.get_barrier_semaphore(), inc=1, device_id=where, device_id_type=MESH
    )


def dot_nt(left, right):
    return lax.dot_general(left, right, (((1,), (1,)), ((), ())), preferred_element_type=F32)


def first_kernel(
    tok, gain, pos, pool, lens, owners, listing, wq, wk, wv, wo, wg, wu, wd,
    q_out, kv_out, wo_s, wg_s, wu_s, wd_s, dc,
    buf, wall, wkw, wvw, outg, qst, kvst,
    ag_send, ag_recv, lsem, wsend, wrecv, hsend, hrecv, hlocal,
    zsend, zrecv, ssend, srecv, rsend, rrecv, kvl, qsem,
):
    x, yh, c = place()
    s, d = lax.axis_index("seq"), lax.axis_index("dec")
    chip = x * 2 + yh
    sib = at_chip(x, yh, 1 - c)
    start = jnp.minimum(lax.div(chip * HD, LANES), 3) * LANES
    off = chip * HD - start
    cols = pl.ds(pl.multiple_of(start, LANES), 2 * LANES)
    local = [
        pltpu.make_async_copy(wq, wall.at[pl.ds(0, 2 * HD)], lsem.at[0]),
        pltpu.make_async_copy(wk.at[:, cols], wkw, lsem.at[1]),
        pltpu.make_async_copy(wv.at[:, cols], wvw, lsem.at[2]),
    ]
    for copy in local:
        copy.start()
    ag = Gather(buf, ag_send, ag_recv)
    for where in (ag.a, ag.b, ag.o, sib):
        signal(where)
    others = []
    for k in range(1, OWNERS):
        ds, dd = k // 2, k % 2
        others.append({"seq": lax.rem(s + ds, 4), "dec": lax.rem(d + dd, 2)})
    for where in others:
        signal(where)
    buf[chip] = normed(tok[...].astype(F32), gain[...])
    pl.semaphore_wait(pltpu.get_barrier_semaphore(), 4 + len(others))
    for i in range(NP):
        ag.first(i)
    shared = [
        pltpu.make_async_remote_copy(
            src_ref=a, dst_ref=b, send_sem=wsend.at[k], recv_sem=wrecv.at[k],
            device_id=sib, device_id_type=MESH,
        )
        for k, (a, b) in enumerate(
            ((wq, wall.at[pl.ds(2 * HD, 2 * HD)]), (wo, wo_s), (wg, wg_s), (wu, wu_s), (wd, wd_s))
        )
    ]
    for copy in shared:
        copy.start()

    counts = [lax.div(lens[k] + (BT - 1), BT) for k in range(RQ)]
    firsts, so_far = [], jnp.int32(0)
    for k in range(RQ):
        firsts.append(so_far)
        so_far = so_far + counts[k]
    ranks = []
    for k in range(RQ):
        rank = jnp.int32(0)
        for e in range(k):
            rank = rank + (owners[e] == owners[k]).astype(jnp.int32)
        ranks.append(rank)
    feature = lax.broadcasted_iota(jnp.int32, (2, BT * HD), 1)

    def cut(o, _):
        for r in range(PAIR):
            at, length = jnp.int32(0), jnp.int32(0)
            for k in range(RQ):
                hit = (owners[k] == o) & (ranks[k] == r)
                at = jnp.where(hit, firsts[k], at)
                length = jnp.where(hit, lens[k], length)
            for b in range(MAXLEN // BT):
                block = pool[listing[jnp.minimum(at + b, NB - 1)]].astype(F32)
                kept = jnp.where(feature < (length - BT * b) * HD, block, 0.0)
                outg[o * PAIR + r, :, BT * HD * b : BT * HD * (b + 1)] = kept.astype(BF)
        return 0

    lax.fori_loop(0, OWNERS, cut, 0)
    me = s * 2 + d
    handed = []
    for k, where in enumerate(others):
        there = where["seq"] * 2 + where["dec"]
        handed.append(
            pltpu.make_async_remote_copy(
                src_ref=outg.at[pl.ds(there * PAIR, PAIR)],
                dst_ref=dc.at[pl.ds(me * PAIR, PAIR)],
                send_sem=hsend.at[k],
                recv_sem=hrecv.at[k],
                device_id=where,
                device_id_type=MESH,
            )
        )
    keep = pltpu.make_async_copy(
        outg.at[pl.ds(me * PAIR, PAIR)], dc.at[pl.ds(me * PAIR, PAIR)], hlocal
    )
    ag.second()
    for k in (1, 3, 5, 0, 2):
        handed[k].start()
    keep.start()

    row = lax.broadcasted_iota(jnp.int32, (HD, 2 * LANES), 0)
    col = lax.broadcasted_iota(jnp.int32, (HD, 2 * LANES), 1)
    pick = (col == row + off).astype(F32).astype(BF)
    chunk = 512

    def laid(src, begin):
        def one(i, _):
            rows = pl.ds(pl.multiple_of(i * chunk, chunk), chunk)
            wall[begin : begin + HD, rows] = dot_nt(pick, src[rows, :]).astype(BF)
            return 0

        lax.fori_loop(0, D // chunk, one, 0)

    for copy in local:
        copy.wait()
    laid(wkw, 4 * HD)
    laid(wvw, 5 * HD)
    half = HD // 2
    rate = jnp.exp(
        lax.broadcasted_iota(jnp.int32, (half, 1), 0).astype(F32) * (-2.0 / HD * LOG_BASE)
    )
    low_lanes = lax.broadcasted_iota(jnp.int32, (1, LANES), 1) < ROWS

    def own_half(two, one_more):
        low = jnp.where(c == 0, two, pltpu.roll(two, ROWS, 1))
        high = jnp.where(c == 0, pltpu.roll(one_more, ROWS, 1), one_more)
        return jnp.where(low_lanes, low, high)

    def lanes_of(core):
        return pl.ds(pl.multiple_of(core * 256, 256), 256)

    def moved(src, dst, send, recv, where):
        return pltpu.make_async_remote_copy(
            src_ref=src, dst_ref=dst, send_sem=send, recv_sem=recv, device_id=where, device_id_type=MESH
        )

    def to_later(e, k):
        dst = kv_out.at[s * 2 + k, :, lanes_of(c)]
        return moved(kvst.at[k], dst, zsend.at[e - 1, k], zrecv.at[e - 1, k], {"seq": lax.rem(s + e, 4)})

    def to_sibling(k):
        dst = kv_out.at[s * 2 + k, :, lanes_of(c)]
        return moved(kvst.at[k], dst, ssend.at[k], srecv.at[k], sib)

    def from_earlier(e, k, core, send, recv):
        part = kv_out.at[lax.rem(s - e + 4, 4) * 2 + k, :, lanes_of(core)]
        return moved(part, part, send.at[e - 1, k], recv.at[e - 1, k], sib)

    def own_copies(k):
        return (
            pltpu.make_async_copy(kvst.at[k], kv_out.at[s * 2 + k, :, lanes_of(c)], kvl.at[k]),
            pltpu.make_async_copy(qst.at[pl.ds(2 * k, 2)], q_out.at[pl.ds(2 * k, 2)], qsem.at[k]),
        )

    def rotated(v, cosine, sine):
        a, b = v[:half], v[half:]
        return jnp.concatenate([a * cosine - b * sine, b * cosine + a * sine], axis=0)

    def chip_lanes(ref, n):
        return ref[:, pl.ds(pl.multiple_of(n * LANES, LANES), LANES)].astype(F32)

    def project(k, _):
        @pl.when(k == 0)
        def _():
            ag.third()
            shared[0].wait_recv()
            ag.near_own()

        @pl.when(k == 1)
        def _():
            ag.fourth()
            for e in (4, 6):
                handed[e].start()
            ag.near_partner()
            ag.far()

        four = []
        for r in (2 * k, 2 * k + 1):
            four += list(batch(r, x, col4(x + 1), col4(x - 1), col4(x + 2), yh))
        shards_in = jnp.concatenate([buf[n] for n in four], axis=0)
        out = dot_nt(wall[...], shards_in)
        places = jnp.concatenate(
            [
                own_half(chip_lanes(pos, four[0]), chip_lanes(pos, four[1])),
                own_half(chip_lanes(pos, four[2]), chip_lanes(pos, four[3])),
            ],
            axis=1,
        )
        angles = rate * places
        cosine, sine = jnp.cos(angles), jnp.sin(angles)
        kvst[k, 0:HD] = rotated(out[4 * HD : 5 * HD], cosine, sine).astype(BF)
        kvst[k, HD:] = out[5 * HD :].astype(BF)
        for e in (1, 2, 3):

            @pl.when(s + e < 4)
            def _():
                to_later(e, k).start()

        to_sibling(k).start()
        for h in range(4):
            v = (rotated(out[h * HD : (h + 1) * HD], cosine, sine) * SCALE).astype(BF)
            for n in range(2):
                qst[2 * k + n, :, h * LANES : (h + 1) * LANES] = v[:, n * LANES : (n + 1) * LANES]
        for copy in own_copies(k):
            copy.start()
        return 0

    lax.fori_loop(0, 2, project, 0)
    for k in range(2):
        for e in (1, 2, 3):

            @pl.when(s >= e)
            def _():
                from_earlier(e, k, c, zsend, zrecv).wait_recv()
                from_earlier(e, k, c, rsend, rrecv).start()

    ag.finish()
    for k in range(2):
        to_sibling(k).wait_send()
        for copy in own_copies(k):
            copy.wait()
        part = kv_out.at[s * 2 + k, :, lanes_of(1 - c)]
        moved(part, part, ssend.at[k], srecv.at[k], sib).wait_recv()
        for e in (1, 2, 3):

            @pl.when(s + e < 4)
            def _():
                to_later(e, k).wait_send()

            @pl.when(s >= e)
            def _():
                from_earlier(e, k, c, rsend, rrecv).wait_send()
                from_earlier(e, k, 1 - c, rsend, rrecv).wait_recv()

    for k, where in enumerate(others):
        handed[k].wait_send()
        back = lax.rem(s - (k + 1) // 2 + 4, 4) * 2 + lax.rem(d - (k + 1) % 2 + 2, 2)
        pltpu.make_async_remote_copy(
            src_ref=outg.at[pl.ds(back * PAIR, PAIR)],
            dst_ref=dc.at[pl.ds(back * PAIR, PAIR)],
            send_sem=hsend.at[k],
            recv_sem=hrecv.at[k],
            device_id=where,
            device_id_type=MESH,
        ).wait_recv()
    keep.wait()
    for k, copy in enumerate(shared):
        copy.wait_send()
        if k:
            copy.wait_recv()


def attend_kernel(
    lo_ref, q_hbm, kv_hbm, dc_in, o_ref, dc_out, q_ref, kv_ref, keys, o_vm, kpos, sc, mx, acc, sems
):
    loads = [
        pltpu.make_async_copy(q_hbm, q_ref.at[:, pl.ds(0, HD)], sems.at[0]),
        pltpu.make_async_copy(kv_hbm, kv_ref.at[:, pl.ds(0, 2 * HD)], sems.at[1]),
    ]
    for copy in loads:
        copy.start()
    passed = pltpu.make_async_copy(dc_in, dc_out, sems.at[3])
    passed.start()
    x, yh, c = place()
    s = lax.axis_index("seq")
    ring = (x, col4(x + 1), col4(x - 1), col4(x + 2), yh)
    row = lax.broadcasted_iota(jnp.int32, (2 * LANES, LANES), 0)
    quarter, local = lax.div(row, ROWS), lax.rem(row, ROWS)
    for e in range(2):
        chips = batch(2 * e, *ring) + batch(2 * e + 1, *ring)
        chip = jnp.where(
            quarter < 2, jnp.where(quarter == 0, chips[0], chips[1]), jnp.where(quarter == 2, chips[2], chips[3])
        )
        for core in range(2):
            kpos[e, core * 256 : core * 256 + 256] = chip * LANES + core * ROWS + local
    ones = lax.broadcasted_iota(jnp.int32, (TILES, 16, KT), 1) == 0
    kv_ref[:, 2 * HD :, :] = ones.astype(F32).astype(BF)
    q_ref[:, HD:, :] = jnp.zeros((4, LANES - HD, 4 * LANES), BF)
    lane = lax.broadcasted_iota(jnp.int32, (1, LANES), 1)
    low_lanes = lane < ROWS
    for copy in loads:
        copy.wait()

    def turn(t, _):
        k = kv_ref[t, 0:HD].astype(F32)
        k = jnp.concatenate([k, jnp.zeros((LANES - HD, KT), F32)], axis=0)
        keys[t] = k.T.astype(BF)
        return 0

    lax.fori_loop(0, 2 * s + 2, turn, 0)

    def tile(r, _):
        n0, n1 = batch(r, *ring)
        one = lo_ref[:, pl.ds(pl.multiple_of(n0 * LANES, LANES), LANES)].astype(F32)
        two = lo_ref[:, pl.ds(pl.multiple_of(n1 * LANES, LANES), LANES)].astype(F32)
        low = jnp.where(c == 0, one, pltpu.roll(one, ROWS, 1))
        high = jnp.where(c == 0, pltpu.roll(two, ROWS, 1), two)
        lows = jnp.where(low_lanes, low, high)
        places = c * ROWS + jnp.where(low_lanes, n0 * LANES + lane, n1 * LANES + lane - ROWS)
        least, most = jnp.min(lows).astype(jnp.int32), jnp.max(lows).astype(jnp.int32)
        lows = lows.astype(jnp.int32)
        begin = lax.div(jnp.maximum(least, 0), 1024)
        acc[...] = jnp.zeros_like(acc)

        def product(t):
            return jnp.dot(keys[t], q_ref[r], preferred_element_type=F32)

        def peak(v):
            return jnp.max(v.reshape(KT // 8, 8, 4 * LANES), axis=0)

        def masked(b, e, seen):
            v = product(2 * b + e)
            v = jnp.concatenate(
                [jnp.where(seen, v[:, h * LANES : (h + 1) * LANES], -jnp.inf) for h in range(4)], axis=1
            )
            sc[2 * b + e] = v
            return peak(v)

        tops = [masked(s, e, (kpos[e] >= lows - s * 1024) & (kpos[e] <= places)) for e in range(2)]
        mx[...] = jnp.maximum(tops[0], tops[1])

        def score(b, _):
            clear = b * 1024 >= most

            @pl.when(clear)
            def _():
                one, two = product(2 * b), product(2 * b + 1)
                sc[2 * b] = one
                sc[2 * b + 1] = two
                mx[...] = jnp.maximum(mx[...], jnp.maximum(peak(one), peak(two)))

            @pl.when(jnp.logical_not(clear))
            def _():
                tops = [masked(b, e, kpos[e] >= lows - b * 1024) for e in range(2)]
                mx[...] = jnp.maximum(mx[...], jnp.maximum(tops[0], tops[1]))

            return 0

        lax.fori_loop(begin, s, score, 0)
        top = jnp.max(mx[...], axis=0, keepdims=True)

        def mix(b, _):
            total = acc[0 : HD + 16, :]
            for e in range(2):
                p = jnp.exp2(sc[2 * b + e] - top).astype(BF)
                total = total + jnp.dot(kv_ref[2 * b + e, HD:], p, preferred_element_type=F32)
            acc[0 : HD + 16, :] = total
            return 0

        lax.fori_loop(begin, s + 1, mix, 0)
        out = acc[...] / acc[HD : HD + 1, :]
        for h in range(4):
            o_vm[r, h] = out[:, h * LANES : (h + 1) * LANES].T.astype(BF)
        return 0

    lax.fori_loop(0, 4, tile, 0)
    result = pltpu.make_async_copy(o_vm, o_ref, sems.at[2])
    result.start()
    passed.wait()
    result.wait()


def last_kernel(
    heads, tok, gain, wo, wo_s, wg, wg_s, wu, wu_s, wd, wd_s,
    out,
    buf, res, part, hv, wov, raw, wt, ds, o1, i1, o2, i2,
    lsem, ag_send, ag_recv, s1, r1, s2, r2,
):
    ag = Gather(buf, ag_send, ag_recv)
    for where in (ag.a, ag.b, ag.o):
        signal(where)
    loads = [(heads, hv)]
    for e, src in enumerate((wo, wo_s)):
        for h in range(2):
            loads.append((src.at[pl.ds(h * HD, HD)], wov.at[pl.ds((2 * e + h) * LANES, HD)]))
    for e, src in enumerate((wg, wg_s, wu, wu_s)):
        loads.append((src, raw.at[e // 2, pl.ds(e % 2 * UN, UN)]))
    for e, src in enumerate((wd, wd_s)):
        loads.append((src, ds.at[pl.ds(e * UN, UN)]))
    copies = [pltpu.make_async_copy(a, b, lsem.at[k]) for k, (a, b) in enumerate(loads)]
    for copy in copies:
        copy.start()
    for h in range(4):
        wov[h * LANES + HD : (h + 1) * LANES, :] = jnp.zeros((LANES - HD, D), BF)
    raw[:, 2 * UN :, :] = jnp.zeros((2, WIDE - 2 * UN, D), BF)
    ds[2 * UN :, :] = jnp.zeros((WIDE - 2 * UN, D), BF)
    for copy in copies[:5]:
        copy.wait()
    x, m = ag.x, ag.yh
    ring = (x, col4(x + 1), col4(x - 1), col4(x + 2), m)
    rs = Scatter(part, o1, i1, s1, r1)

    def project(n, _):
        r = lax.rem(n + 2, 4)
        side = jnp.concatenate([hv[r, h] for h in range(4)], axis=1)
        part[r] = jnp.dot(side, wov[...], preferred_element_type=F32).reshape(2, ROWS, D)

        @pl.when(n == 0)
        def _():
            pl.semaphore_wait(pltpu.get_barrier_semaphore(), 3)
            rs.sides()

        @pl.when(n == 1)
        def _():
            rs.across()

        return 0

    lax.fori_loop(0, 4, project, 0)
    for copy in copies[5:]:
        copy.wait()

    def turn(n, _):
        cols = pl.ds(pl.multiple_of(n * 256, 256), 256)
        for e in range(2):
            wt[cols, e * WIDE : (e + 1) * WIDE] = raw[e, :, cols].astype(F32).T.astype(BF)
        return 0

    lax.fori_loop(0, D // 256, turn, 0)
    rs.rest()
    chip = x * 2 + m
    for i in range(NP):
        rows = pl.ds(i * PIECE, PIECE)
        total = tok[rows, :].astype(F32) + rs.final(i)
        res[rows, :] = total
        buf[chip, rows, :] = normed(total, gain[...])
        ag.first(i)

    rs2 = Scatter(part, o2, i2, s2, r2)
    ag.second()
    ag.third()

    def feed(r, _):
        @pl.when(r == 1)
        def _():
            ag.near_own()

        @pl.when(r == 2)
        def _():
            ag.fourth()
            ag.near_partner()

        @pl.when(r == 3)
        def _():
            rs2.sides()
            ag.far()

        n0, n1 = batch(r, *ring)
        both = jnp.concatenate([buf[n0], buf[n1]], axis=0)
        wide = jnp.dot(both, wt[...], preferred_element_type=F32)
        gate, up = wide[:, :WIDE], wide[:, WIDE:]
        hid = (gate / (1.0 + jnp.exp(-gate)) * up).astype(BF)
        part[r] = jnp.dot(hid, ds[...], preferred_element_type=F32).reshape(2, ROWS, D)
        return 0

    lax.fori_loop(0, 4, feed, 0)
    rs2.across()
    rs2.rest()
    for i in range(NP):
        rows = pl.ds(i * PIECE, PIECE)
        out[rows, :] = (res[rows, :] + rs2.final(i)).astype(BF)
    ag.finish()
    rs.finish()
    rs2.finish()


VMEM_SPEC = pl.BlockSpec(memory_space=pltpu.VMEM)
SMEM_SPEC = pl.BlockSpec(memory_space=pltpu.SMEM)
HBM_SPEC = pl.BlockSpec(memory_space=pltpu.HBM)
DMA = pltpu.SemaphoreType.DMA


def shape(*dims, dtype=BF):
    return jax.ShapeDtypeStruct(dims, dtype)


def shards(
    tokens, attn_gain, w_query, w_key, w_value, w_out, mlp_gain, w_gate, w_up, w_down,
    positions, window_lo, cache_pool, req_len, req_owner, block_list,
):
    own_rows = tokens[0, 0]
    wq, wg, wu = w_query.T, w_gate.T, w_up.T

    q, kv, wo_s, wg_s, wu_s, wd_s, dc = pl.pallas_call(
        first_kernel,
        out_shape=(
            shape(4, HD, 4 * LANES),
            shape(TILES, 2 * HD, KT),
            shape(*w_out.shape),
            shape(*wg.shape),
            shape(*wu.shape),
            shape(*w_down.shape),
            shape(OWNERS * PAIR, 2, MAXLEN * HD),
        ),
        in_specs=[VMEM_SPEC] * 4 + [SMEM_SPEC] * 3 + [HBM_SPEC] * 7,
        out_specs=(HBM_SPEC,) * 7,
        scratch_shapes=[
            VM((8, ROWS, D), BF),
            VM((6 * HD, D), BF),
            VM((D, 2 * LANES), BF),
            VM((D, 2 * LANES), BF),
            VM((OWNERS * PAIR, 2, MAXLEN * HD), BF),
            VM((4, HD, 4 * LANES), BF),
            VM((2, 2 * HD, 2 * LANES), BF),
            DMA((7, NP)),
            DMA((7, NP)),
            DMA((3,)),
            DMA((5,)),
            DMA((5,)),
            DMA((7,)),
            DMA((7,)),
            DMA,
            DMA((3, 2)),
            DMA((3, 2)),
            DMA((2,)),
            DMA((2,)),
            DMA((3, 2)),
            DMA((3, 2)),
            DMA((2,)),
            DMA((2,)),
        ],
        compiler_params=pltpu.CompilerParams(
            collective_id=0, has_side_effects=True, vmem_limit_bytes=GRANT
        ),
        name="gather_project",
    )(
        own_rows, attn_gain.reshape(1, D), positions.reshape(1, 1024), cache_pool.reshape(NB, 2, BT * HD),
        req_len.reshape(RQ), req_owner.reshape(RQ), block_list.reshape(NB),
        wq, w_key, w_value, w_out, wg, wu, w_down,
    )

    heads, dc = pl.pallas_call(
        attend_kernel,
        out_shape=(shape(4, 4, LANES, LANES), shape(*dc.shape)),
        in_specs=[VMEM_SPEC] + [HBM_SPEC] * 3,
        out_specs=(HBM_SPEC, HBM_SPEC),
        scratch_shapes=[
            VM((4, LANES, 4 * LANES), BF),
            VM((TILES, 2 * HD + 16, KT), BF),
            VM((TILES, KT, LANES), BF),
            VM((4, 4, LANES, LANES), BF),
            VM((2, KT, LANES), jnp.int32),
            VM((TILES, KT, 4 * LANES), F32),
            VM((8, 4 * LANES), F32),
            VM((LANES, 4 * LANES), F32),
            DMA((4,)),
        ],
        compiler_params=pltpu.CompilerParams(vmem_limit_bytes=GRANT),
        name="attend",
    )(window_lo.reshape(1, 1024), q, kv, dc)

    layer_out = pl.pallas_call(
        last_kernel,
        out_shape=shape(ROWS, D),
        in_specs=[HBM_SPEC] + [VMEM_SPEC] * 2 + [HBM_SPEC] * 8,
        out_specs=VMEM_SPEC,
        scratch_shapes=[
            VM((8, ROWS, D), BF),
            VM((ROWS, D), F32),
            VM((4, 2, ROWS, D), F32),
            VM((4, 4, LANES, LANES), BF),
            VM((4 * LANES, D), BF),
            VM((2, WIDE, D), BF),
            VM((D, 2 * WIDE), BF),
            VM((WIDE, D), BF),
            VM((7, ROWS, D), BF),
            VM((7, ROWS, D), BF),
            VM((7, ROWS, D), BF),
            VM((7, ROWS, D), BF),
            DMA((11,)),
        ]
        + [DMA((7, NP))] * 6,
        compiler_params=pltpu.CompilerParams(
            collective_id=1, has_side_effects=True, vmem_limit_bytes=GRANT
        ),
        name="mix_feed_forward",
    )(
        heads, own_rows, mlp_gain.reshape(1, D), w_out, wo_s, wg, wg_s, wu, wu_s, w_down, wd_s,
    )
    return (
        layer_out.reshape(1, 1, ROWS, D),
        dc.reshape(OWNERS * PAIR, 2, 1, MAXLEN * HD),
    )


def solution(mesh):
    in_specs = (
        P("dec", "seq", "tensor", None),
        P(),
        P(None, "tensor"),
        P(),
        P(),
        P("tensor", None),
        P(),
        P(None, "tensor"),
        P(None, "tensor"),
        P("tensor", None),
        P("dec", "seq", None),
        P("dec", "seq", None),
        P(("seq", "dec"), None, "tensor", None),
        P(("seq", "dec"), None),
        P(("seq", "dec"), None),
        P(("seq", "dec"), None),
    )
    out_specs = (P("dec", "seq", "tensor", None), P(("seq", "dec"), None, "tensor", None))
    return jax.shard_map(shards, mesh=mesh, in_specs=in_specs, out_specs=out_specs, check_vma=False)
```

```python
import functools

import jax
import jax.numpy as jnp
from jax import lax
from jax.experimental import pallas as pl
from jax.experimental.pallas import tpu as pltpu
from jax.sharding import PartitionSpec as P

HD = 80
D = 2560
BT = 16
MAXLEN = 128
PAIR = 2
RQ = 8
NB = 40
UN = 432
WIDE = 896
ROWS = 64
NP = 2
PIECE = ROWS // NP
LANES = 128
KT = 512
TILES = 8
GRANT = 60 << 20
OWNERS = 8

MESH = pl.DeviceIdType.MESH
VM = pltpu.VMEM
norm_eps = 1e-05
LOG_BASE = 9.210340371976184
SCALE = HD**-0.5 * 1.4426950408889634
F32 = jnp.float32
BF = jnp.bfloat16


def place():
    t = lax.axis_index("tensor")
    return lax.div(t, 4), lax.rem(lax.div(t, 2), 2), lax.rem(t, 2)


def at_chip(x, yh, c):
    return {"tensor": (lax.rem(x + 4, 4) * 2 + yh) * 2 + c}


def col4(x):
    return lax.rem(x + 4, 4)


def batch(r, own, ca, cb, co, m):
    c0 = jnp.where(r == 0, own, jnp.where(r == 3, co, cb))
    c1 = jnp.where(r == 0, own, jnp.where(r == 3, co, ca))
    r0 = jnp.where(r == 2, 1 - m, m)
    r1 = jnp.where(r == 1, m, 1 - m)
    return c0 * 2 + r0, c1 * 2 + r1


def normed(values, gain):
    mean_square = jnp.mean(values * values, axis=-1, keepdims=True)
    return (values * lax.rsqrt(mean_square + norm_eps) * gain).astype(BF)


class Gather:
    def __init__(self, buf, send, recv):
        self.x, self.yh, self.c = place()
        self.buf, self.send, self.recv = buf, send, recv
        x, m, c, p = self.x, self.yh, self.c, 1 - self.yh
        self.a, self.b, self.o = at_chip(x + 1, m, c), at_chip(x - 1, m, c), at_chip(x, p, c)
        own, ca, cb, co = col4(x), col4(x + 1), col4(x - 1), col4(x + 2)
        self.plan = [
            (own * 2 + m, self.o, own * 2 + p),
            (own * 2 + m, self.a, cb * 2 + m),
            (own * 2 + m, self.b, ca * 2 + m),
            (own * 2 + p, self.a, cb * 2 + p),
            (own * 2 + p, self.b, ca * 2 + p),
            (cb * 2 + m, self.a, co * 2 + m),
            (co * 2 + m, self.o, co * 2 + p),
            (ca * 2 + m, self.b, co * 2 + m),
        ]

    def copy(self, k, i, got):
        plan = self.plan[7 if k == 5 and i >= NP // 2 else k]
        part = self.buf.at[plan[2] if got else plan[0], pl.ds(i * PIECE, PIECE)]
        return pltpu.make_async_remote_copy(
            src_ref=part,
            dst_ref=part,
            send_sem=self.send.at[k, i],
            recv_sem=self.recv.at[k, i],
            device_id=plan[1],
            device_id_type=MESH,
        )

    def start(self, k, i):
        self.copy(k, i, False).start()

    def got(self, k, i):
        self.copy(k, i, True).wait_recv()

    def first(self, i):
        self.start(1, i)
        self.start(2, i)
        self.start(0, i)

    def second(self):
        for i in range(NP // 2):
            self.got(1, i)
            self.start(5, i)
            self.got(2, NP - 1 - i)
            self.start(5, NP - 1 - i)

    def third(self):
        for i in range(NP):
            self.got(0, i)
            self.start(3, i)
            self.start(4, i)

    def fourth(self):
        for i in range(NP // 2):
            for e in (i, NP - 1 - i):
                self.got(5, e)
                self.start(6, e)

    def near_own(self):
        for i in range(NP // 2):
            self.got(1, NP - 1 - i)
            self.got(2, i)

    def near_partner(self):
        for i in range(NP):
            self.got(3, i)
            self.got(4, i)

    def far(self):
        for i in range(NP):
            self.got(6, i)

    def finish(self):
        for k in range(7):
            for i in range(NP):
                self.copy(k, i, False).wait_send()


class Scatter:
    def __init__(self, part, out, inb, send, recv):
        x, yh, c = place()
        self.part, self.out, self.inb, self.send, self.recv = part, out, inb, send, recv
        self.a, self.b = at_chip(x + 1, yh, c), at_chip(x - 1, yh, c)
        o = at_chip(x, 1 - yh, c)
        self.to = [o, self.a, self.b, None, self.a, self.b, o]

    def copy(self, k, i):
        rows = pl.ds(i * PIECE, PIECE)
        to = self.to[k] if k != 3 else (self.a if i < NP // 2 else self.b)
        return pltpu.make_async_remote_copy(
            src_ref=self.out.at[k, rows],
            dst_ref=self.inb.at[k, rows],
            send_sem=self.send.at[k, i],
            recv_sem=self.recv.at[k, i],
            device_id=to,
            device_id_type=MESH,
        )

    def summed(self, part, i, adds):
        rows = pl.ds(i * PIECE, PIECE)
        total = self.part[part[0], part[1], rows, :]
        for e in adds:
            self.copy(e, i).wait_recv()
            total = total + self.inb[e, rows, :].astype(F32)
        return total

    def put(self, k, part, i, adds=()):
        self.out[k, pl.ds(i * PIECE, PIECE), :] = self.summed(part, i, adds).astype(BF)
        self.copy(k, i).start()

    def sides(self):
        for i in range(NP):
            self.put(1, (2, 1), i)
            self.put(2, (2, 0), i)

    def across(self):
        for i in range(NP // 2):
            self.put(0, (3, 1), i)
            self.put(0, (3, 1), NP - 1 - i)

    def plain(self):
        for i in range(NP // 2):
            self.put(4, (1, 1), NP - 1 - i)
            self.put(5, (1, 0), i)

    def rest(self):
        for i in range(NP // 2):
            self.put(3, (3, 0), i, (0,))
            self.put(3, (3, 0), NP - 1 - i, (0,))
        for i in range(NP):
            self.put(6, (0, 1), i, (1, 2))
        for i in range(NP // 2):
            self.put(4, (1, 1), i, (3,))
            self.put(5, (1, 0), NP - 1 - i, (3,))

    def final(self, i):
        return self.summed((0, 0), i, (6, 4, 5))

    def finish(self):
        for k in range(7):
            for i in range(NP):
                self.copy(k, i).wait_send()


def signal(where):
    pl.semaphore_signal(
        pltpu.get_barrier_semaphore(), inc=1, device_id=where, device_id_type=MESH
    )


def dot_nt(left, right):
    return lax.dot_general(left, right, (((1,), (1,)), ((), ())), preferred_element_type=F32)


def first_kernel(
    tok, gain, pos, pool, lens, owners, listing, wq, wk, wv, wo, wg, wu, wd,
    q_out, kv_out, wo_s, wg_s, wu_s, wd_s, dc,
    buf, wall, wkw, wvw, outg, qst, kvst,
    ag_send, ag_recv, lsem, wsend, wrecv, hsend, hrecv, hlocal,
    zsend, zrecv, ssend, srecv, rsend, rrecv, kvl, qsem,
):
    x, yh, c = place()
    s, d = lax.axis_index("seq"), lax.axis_index("dec")
    chip = x * 2 + yh
    sib = at_chip(x, yh, 1 - c)
    start = jnp.minimum(lax.div(chip * HD, LANES), 3) * LANES
    off = chip * HD - start
    cols = pl.ds(pl.multiple_of(start, LANES), 2 * LANES)
    local = [
        pltpu.make_async_copy(wq, wall.at[pl.ds(0, 2 * HD)], lsem.at[0]),
        pltpu.make_async_copy(wk.at[:, cols], wkw, lsem.at[1]),
        pltpu.make_async_copy(wv.at[:, cols], wvw, lsem.at[2]),
    ]
    for copy in local:
        copy.start()
    ag = Gather(buf, ag_send, ag_recv)
    for where in (ag.a, ag.b, ag.o, sib):
        signal(where)
    others = []
    for k in range(1, OWNERS):
        ds, dd = k // 2, k % 2
        others.append({"seq": lax.rem(s + ds, 4), "dec": lax.rem(d + dd, 2)})
    for where in others:
        signal(where)
    buf[chip] = normed(tok[...].astype(F32), gain[...].reshape(1, D))
    pl.semaphore_wait(pltpu.get_barrier_semaphore(), 4 + len(others))
    for i in range(NP):
        ag.first(i)
    shared = [
        pltpu.make_async_remote_copy(
            src_ref=a, dst_ref=b, send_sem=wsend.at[k], recv_sem=wrecv.at[k],
            device_id=sib, device_id_type=MESH,
        )
        for k, (a, b) in enumerate(
            ((wq, wall.at[pl.ds(2 * HD, 2 * HD)]), (wo, wo_s), (wg, wg_s), (wu, wu_s), (wd, wd_s))
        )
    ]
    for copy in shared:
        copy.start()

    counts = [lax.div(lens[k] + (BT - 1), BT) for k in range(RQ)]
    firsts, so_far = [], jnp.int32(0)
    for k in range(RQ):
        firsts.append(so_far)
        so_far = so_far + counts[k]
    ranks = []
    for k in range(RQ):
        rank = jnp.int32(0)
        for e in range(k):
            rank = rank + (owners[e] == owners[k]).astype(jnp.int32)
        ranks.append(rank)
    feature = lax.broadcasted_iota(jnp.int32, (2, BT * HD), 1)

    def cut(o, _):
        for r in range(PAIR):
            at, length = jnp.int32(0), jnp.int32(0)
            for k in range(RQ):
                hit = (owners[k] == o) & (ranks[k] == r)
                at = jnp.where(hit, firsts[k], at)
                length = jnp.where(hit, lens[k], length)
            for b in range(MAXLEN // BT):
                block = pool[listing[jnp.minimum(at + b, NB - 1)]].astype(F32)
                kept = jnp.where(feature < (length - BT * b) * HD, block, 0.0)
                outg[o * PAIR + r, :, BT * HD * b : BT * HD * (b + 1)] = kept.astype(BF)
        return 0

    lax.fori_loop(0, OWNERS, cut, 0)
    me = s * 2 + d
    handed = []
    for k, where in enumerate(others):
        there = where["seq"] * 2 + where["dec"]
        handed.append(
            pltpu.make_async_remote_copy(
                src_ref=outg.at[pl.ds(there * PAIR, PAIR)],
                dst_ref=dc.at[pl.ds(me * PAIR, PAIR)],
                send_sem=hsend.at[k],
                recv_sem=hrecv.at[k],
                device_id=where,
                device_id_type=MESH,
            )
        )
    keep = pltpu.make_async_copy(
        outg.at[pl.ds(me * PAIR, PAIR)], dc.at[pl.ds(me * PAIR, PAIR)], hlocal
    )
    ag.second()
    for k in (1, 3, 5, 0, 2):
        handed[k].start()
    keep.start()

    row = lax.broadcasted_iota(jnp.int32, (HD, 2 * LANES), 0)
    col = lax.broadcasted_iota(jnp.int32, (HD, 2 * LANES), 1)
    pick = (col == row + off).astype(F32).astype(BF)
    chunk = 512

    def laid(src, begin):
        def one(i, _):
            rows = pl.ds(pl.multiple_of(i * chunk, chunk), chunk)
            wall[begin : begin + HD, rows] = dot_nt(pick, src[rows, :]).astype(BF)
            return 0

        lax.fori_loop(0, D // chunk, one, 0)

    for copy in local:
        copy.wait()
    laid(wkw, 4 * HD)
    laid(wvw, 5 * HD)
    half = HD // 2
    rate = jnp.exp(
        lax.broadcasted_iota(jnp.int32, (half, 1), 0).astype(F32) * (-2.0 / HD * LOG_BASE)
    )
    low_lanes = lax.broadcasted_iota(jnp.int32, (1, LANES), 1) < ROWS

    def own_half(two, one_more):
        low = jnp.where(c == 0, two, pltpu.roll(two, ROWS, 1))
        high = jnp.where(c == 0, pltpu.roll(one_more, ROWS, 1), one_more)
        return jnp.where(low_lanes, low, high)

    def lanes_of(core):
        return pl.ds(pl.multiple_of(core * 256, 256), 256)

    def moved(src, dst, send, recv, where):
        return pltpu.make_async_remote_copy(
            src_ref=src, dst_ref=dst, send_sem=send, recv_sem=recv, device_id=where, device_id_type=MESH
        )

    def to_later(e, k):
        dst = kv_out.at[s * 2 + k, :, lanes_of(c)]
        return moved(kvst.at[k], dst, zsend.at[e - 1, k], zrecv.at[e - 1, k], {"seq": lax.rem(s + e, 4)})

    def to_sibling(k):
        dst = kv_out.at[s * 2 + k, :, lanes_of(c)]
        return moved(kvst.at[k], dst, ssend.at[k], srecv.at[k], sib)

    def from_earlier(e, k, core, send, recv):
        part = kv_out.at[lax.rem(s - e + 4, 4) * 2 + k, :, lanes_of(core)]
        return moved(part, part, send.at[e - 1, k], recv.at[e - 1, k], sib)

    def own_copies(k):
        return (
            pltpu.make_async_copy(kvst.at[k], kv_out.at[s * 2 + k, :, lanes_of(c)], kvl.at[k]),
            pltpu.make_async_copy(qst.at[pl.ds(2 * k, 2)], q_out.at[pl.ds(2 * k, 2)], qsem.at[k]),
        )

    def rotated(v, cosine, sine):
        a, b = v[:half], v[half:]
        return jnp.concatenate([a * cosine - b * sine, b * cosine + a * sine], axis=0)

    def chip_lanes(ref, n):
        return ref[:, pl.ds(pl.multiple_of(n * LANES, LANES), LANES)].astype(F32)

    def project(k, _):
        @pl.when(k == 0)
        def _():
            ag.third()
            shared[0].wait_recv()
            ag.near_own()

        @pl.when(k == 1)
        def _():
            ag.fourth()
            for e in (4, 6):
                handed[e].start()
            ag.near_partner()
            ag.far()

        four = []
        for r in (2 * k, 2 * k + 1):
            four += list(batch(r, x, col4(x + 1), col4(x - 1), col4(x + 2), yh))
        shards_in = jnp.concatenate([buf[n] for n in four], axis=0)
        out = dot_nt(wall[...], shards_in)
        places = jnp.concatenate(
            [
                own_half(chip_lanes(pos, four[0]), chip_lanes(pos, four[1])),
                own_half(chip_lanes(pos, four[2]), chip_lanes(pos, four[3])),
            ],
            axis=1,
        )
        angles = rate * places
        cosine, sine = jnp.cos(angles), jnp.sin(angles)
        kvst[k, 0:HD] = rotated(out[4 * HD : 5 * HD], cosine, sine).astype(BF)
        kvst[k, HD:] = out[5 * HD :].astype(BF)
        for e in (1, 2, 3):

            @pl.when(s + e < 4)
            def _():
                to_later(e, k).start()

        to_sibling(k).start()
        for h in range(4):
            v = (rotated(out[h * HD : (h + 1) * HD], cosine, sine) * SCALE).astype(BF)
            for n in range(2):
                qst[2 * k + n, :, h * LANES : (h + 1) * LANES] = v[:, n * LANES : (n + 1) * LANES]
        for copy in own_copies(k):
            copy.start()
        return 0

    lax.fori_loop(0, 2, project, 0)
    for k in range(2):
        for e in (1, 2, 3):

            @pl.when(s >= e)
            def _():
                from_earlier(e, k, c, zsend, zrecv).wait_recv()
                from_earlier(e, k, c, rsend, rrecv).start()

    ag.finish()
    for k in range(2):
        to_sibling(k).wait_send()
        for copy in own_copies(k):
            copy.wait()
        part = kv_out.at[s * 2 + k, :, lanes_of(1 - c)]
        moved(part, part, ssend.at[k], srecv.at[k], sib).wait_recv()
        for e in (1, 2, 3):

            @pl.when(s + e < 4)
            def _():
                to_later(e, k).wait_send()

            @pl.when(s >= e)
            def _():
                from_earlier(e, k, c, rsend, rrecv).wait_send()
                from_earlier(e, k, 1 - c, rsend, rrecv).wait_recv()

    for k, where in enumerate(others):
        handed[k].wait_send()
        back = lax.rem(s - (k + 1) // 2 + 4, 4) * 2 + lax.rem(d - (k + 1) % 2 + 2, 2)
        pltpu.make_async_remote_copy(
            src_ref=outg.at[pl.ds(back * PAIR, PAIR)],
            dst_ref=dc.at[pl.ds(back * PAIR, PAIR)],
            send_sem=hsend.at[k],
            recv_sem=hrecv.at[k],
            device_id=where,
            device_id_type=MESH,
        ).wait_recv()
    keep.wait()
    for k, copy in enumerate(shared):
        copy.wait_send()
        if k:
            copy.wait_recv()


def last_kernel(
    q_hbm, kv_hbm, lo_ref, tok, gain, wo, wo_s, wg, wg_s, wu, wu_s, wd, wd_s,
    out,
    buf, res, part, hv, q_ref, kv_ref, keys, kpos, sc, mx, acc, wov, raw, wt, ds, o1, i1, i2,
    lsem, ag_send, ag_recv, s1, r1, s2, r2,
):
    ag = Gather(buf, ag_send, ag_recv)
    for where in (ag.a, ag.b, ag.o):
        signal(where)
    loads = [
        (q_hbm, q_ref.at[:, pl.ds(0, HD)]),
        (kv_hbm, kv_ref.at[:, pl.ds(0, 2 * HD)]),
    ]
    for e, src in enumerate((wo, wo_s)):
        for h in range(2):
            loads.append((src.at[pl.ds(h * HD, HD)], wov.at[pl.ds((2 * e + h) * LANES, HD)]))
    for e, src in enumerate((wg, wg_s, wu, wu_s)):
        loads.append((src, raw.at[e // 2, pl.ds(e % 2 * UN, UN)]))
    for e, src in enumerate((wd, wd_s)):
        loads.append((src, ds.at[pl.ds(e * UN, UN)]))
    copies = [pltpu.make_async_copy(a, b, lsem.at[k]) for k, (a, b) in enumerate(loads)]
    for copy in copies:
        copy.start()
    for h in range(4):
        wov[h * LANES + HD : (h + 1) * LANES, :] = jnp.zeros((LANES - HD, D), BF)
    raw[:, 2 * UN :, :] = jnp.zeros((2, WIDE - 2 * UN, D), BF)
    ds[2 * UN :, :] = jnp.zeros((WIDE - 2 * UN, D), BF)
    x, m, c = ag.x, ag.yh, ag.c
    s = lax.axis_index("seq")
    ring = (x, col4(x + 1), col4(x - 1), col4(x + 2), m)
    row = lax.broadcasted_iota(jnp.int32, (2 * LANES, LANES), 0)
    quarter, local = lax.div(row, ROWS), lax.rem(row, ROWS)
    for e in range(2):
        chips = batch(2 * e, *ring) + batch(2 * e + 1, *ring)
        chip = jnp.where(
            quarter < 2, jnp.where(quarter == 0, chips[0], chips[1]), jnp.where(quarter == 2, chips[2], chips[3])
        )
        for core in range(2):
            kpos[e, core * 256 : core * 256 + 256] = chip * LANES + core * ROWS + local
    ones = lax.broadcasted_iota(jnp.int32, (TILES, 16, KT), 1) == 0
    kv_ref[:, 2 * HD :, :] = ones.astype(F32).astype(BF)
    q_ref[:, HD:, :] = jnp.zeros((4, LANES - HD, 4 * LANES), BF)
    lane = lax.broadcasted_iota(jnp.int32, (1, LANES), 1)
    low_lanes = lane < ROWS
    for copy in copies[:2]:
        copy.wait()

    def upright(t, _):
        k = kv_ref[t, 0:HD].astype(F32)
        k = jnp.concatenate([k, jnp.zeros((LANES - HD, KT), F32)], axis=0)
        keys[t] = k.T.astype(BF)
        return 0

    lax.fori_loop(0, 2 * s + 2, upright, 0)

    def attend(r):
        n0, n1 = batch(r, *ring)
        one = lo_ref[:, pl.ds(pl.multiple_of(n0 * LANES, LANES), LANES)].astype(F32)
        two = lo_ref[:, pl.ds(pl.multiple_of(n1 * LANES, LANES), LANES)].astype(F32)
        low = jnp.where(c == 0, one, pltpu.roll(one, ROWS, 1))
        high = jnp.where(c == 0, pltpu.roll(two, ROWS, 1), two)
        lows = jnp.where(low_lanes, low, high).astype(jnp.int32)
        places = c * ROWS + jnp.where(low_lanes, n0 * LANES + lane, n1 * LANES + lane - ROWS)
        acc[...] = jnp.zeros_like(acc)

        def masked(b, e, seen):
            v = jnp.dot(keys[2 * b + e], q_ref[r], preferred_element_type=F32)
            v = jnp.concatenate(
                [jnp.where(seen, v[:, h * LANES : (h + 1) * LANES], -jnp.inf) for h in range(4)], axis=1
            )
            sc[2 * b + e] = v
            return jnp.max(v.reshape(KT // 8, 8, 4 * LANES), axis=0)

        tops = [masked(s, e, (kpos[e] >= lows - s * 1024) & (kpos[e] <= places)) for e in range(2)]
        mx[...] = jnp.maximum(tops[0], tops[1])

        def score(b, _):
            tops = [masked(b, e, kpos[e] >= lows - b * 1024) for e in range(2)]
            mx[...] = jnp.maximum(mx[...], jnp.maximum(tops[0], tops[1]))
            return 0

        lax.fori_loop(0, s, score, 0)
        top = jnp.max(mx[...], axis=0, keepdims=True)

        def mix(b, _):
            total = acc[0 : HD + 16, :]
            for e in range(2):
                p = jnp.exp2(sc[2 * b + e] - top).astype(BF)
                total = total + jnp.dot(kv_ref[2 * b + e, HD:], p, preferred_element_type=F32)
            acc[0 : HD + 16, :] = total
            return 0

        lax.fori_loop(0, s + 1, mix, 0)
        heads = acc[...] / acc[HD : HD + 1, :]
        for h in range(4):
            hv[:, h * LANES : (h + 1) * LANES] = heads[:, h * LANES : (h + 1) * LANES].T.astype(BF)

    rs = Scatter(part, o1, i1, s1, r1)

    def project(n, _):
        r = jnp.where(n < 2, n + 2, 3 - n)
        attend(r)

        @pl.when(n == 0)
        def _():
            for copy in copies[2:6]:
                copy.wait()

        part[r] = jnp.dot(hv[...], wov[...], preferred_element_type=F32).reshape(2, ROWS, D)

        @pl.when(n == 0)
        def _():
            pl.semaphore_wait(pltpu.get_barrier_semaphore(), 3)
            rs.sides()

        @pl.when(n == 1)
        def _():
            rs.across()

        @pl.when(n == 2)
        def _():
            rs.plain()

        return 0

    lax.fori_loop(0, 4, project, 0)
    rs.rest()
    chip = x * 2 + m
    for i in range(NP):
        rows = pl.ds(i * PIECE, PIECE)
        total = tok[rows, :].astype(F32) + rs.final(i)
        res[rows, :] = total
        buf[chip, rows, :] = normed(total, gain[...].reshape(1, D))
        ag.first(i)
    for copy in copies[6:]:
        copy.wait()

    def turn(n, _):
        cols = pl.ds(pl.multiple_of(n * 256, 256), 256)
        for e in range(2):
            wt[cols, e * WIDE : (e + 1) * WIDE] = raw[e, :, cols].astype(F32).T.astype(BF)
        return 0

    lax.fori_loop(0, D // 256, turn, 0)
    rs.finish()

    rs2 = Scatter(part, o1, i2, s2, r2)
    ag.second()
    ag.third()

    def feed(r, _):
        @pl.when(r == 1)
        def _():
            ag.near_own()

        @pl.when(r == 2)
        def _():
            ag.fourth()
            ag.near_partner()

        @pl.when(r == 3)
        def _():
            rs2.sides()
            ag.far()

        n0, n1 = batch(r, *ring)
        both = jnp.concatenate([buf[n0], buf[n1]], axis=0)
        wide = jnp.dot(both, wt[...], preferred_element_type=F32)
        gate, up = wide[:, :WIDE], wide[:, WIDE:]
        hid = (gate / (1.0 + jnp.exp(-gate)) * up).astype(BF)
        part[r] = jnp.dot(hid, ds[...], preferred_element_type=F32).reshape(2, ROWS, D)
        return 0

    lax.fori_loop(0, 4, feed, 0)
    rs2.across()
    rs2.plain()
    rs2.rest()
    for i in range(NP):
        rows = pl.ds(i * PIECE, PIECE)
        out[rows, :] = (res[rows, :] + rs2.final(i)).astype(BF)
    ag.finish()
    rs2.finish()


VMEM_SPEC = pl.BlockSpec(memory_space=pltpu.VMEM)
SMEM_SPEC = pl.BlockSpec(memory_space=pltpu.SMEM)
HBM_SPEC = pl.BlockSpec(memory_space=pltpu.HBM)
DMA = pltpu.SemaphoreType.DMA


def shape(*dims, dtype=BF):
    return jax.ShapeDtypeStruct(dims, dtype)


def shards(
    tokens, attn_gain, w_query, w_key, w_value, w_out, mlp_gain, w_gate, w_up, w_down,
    positions, window_lo, cache_pool, req_len, req_owner, block_list,
):
    own_rows = tokens[0, 0]
    wq, wg, wu = w_query.T, w_gate.T, w_up.T

    q, kv, wo_s, wg_s, wu_s, wd_s, dc = pl.pallas_call(
        first_kernel,
        out_shape=(
            shape(4, HD, 4 * LANES),
            shape(TILES, 2 * HD, KT),
            shape(*w_out.shape),
            shape(*wg.shape),
            shape(*wu.shape),
            shape(*w_down.shape),
            shape(OWNERS * PAIR, 2, MAXLEN * HD),
        ),
        in_specs=[VMEM_SPEC] * 4 + [SMEM_SPEC] * 3 + [HBM_SPEC] * 7,
        out_specs=(HBM_SPEC,) * 7,
        scratch_shapes=[
            VM((8, ROWS, D), BF),
            VM((6 * HD, D), BF),
            VM((D, 2 * LANES), BF),
            VM((D, 2 * LANES), BF),
            VM((OWNERS * PAIR, 2, MAXLEN * HD), BF),
            VM((4, HD, 4 * LANES), BF),
            VM((2, 2 * HD, 2 * LANES), BF),
            DMA((7, NP)),
            DMA((7, NP)),
            DMA((3,)),
            DMA((5,)),
            DMA((5,)),
            DMA((7,)),
            DMA((7,)),
            DMA,
            DMA((3, 2)),
            DMA((3, 2)),
            DMA((2,)),
            DMA((2,)),
            DMA((3, 2)),
            DMA((3, 2)),
            DMA((2,)),
            DMA((2,)),
        ],
        compiler_params=pltpu.CompilerParams(
            collective_id=0, has_side_effects=True, vmem_limit_bytes=GRANT
        ),
        name="gather_project",
    )(
        own_rows, attn_gain, positions.reshape(1, 1024), cache_pool.reshape(NB, 2, BT * HD),
        req_len.reshape(RQ), req_owner.reshape(RQ), block_list.reshape(NB),
        wq, w_key, w_value, w_out, wg, wu, w_down,
    )

    layer_out = pl.pallas_call(
        last_kernel,
        out_shape=shape(ROWS, D),
        in_specs=[HBM_SPEC] * 2 + [VMEM_SPEC] * 3 + [HBM_SPEC] * 8,
        out_specs=VMEM_SPEC,
        scratch_shapes=[
            VM((8, ROWS, D), BF),
            VM((ROWS, D), F32),
            VM((4, 2, ROWS, D), F32),
            VM((LANES, 4 * LANES), BF),
            VM((4, LANES, 4 * LANES), BF),
            VM((TILES, 2 * HD + 16, KT), BF),
            VM((TILES, KT, LANES), BF),
            VM((2, KT, LANES), jnp.int32),
            VM((TILES, KT, 4 * LANES), F32),
            VM((8, 4 * LANES), F32),
            VM((LANES, 4 * LANES), F32),
            VM((4 * LANES, D), BF),
            VM((2, WIDE, D), BF),
            VM((D, 2 * WIDE), BF),
            VM((WIDE, D), BF),
            VM((7, ROWS, D), BF),
            VM((7, ROWS, D), BF),
            VM((7, ROWS, D), BF),
            DMA((12,)),
        ]
        + [DMA((7, NP))] * 6,
        compiler_params=pltpu.CompilerParams(
            collective_id=1, has_side_effects=True, vmem_limit_bytes=GRANT
        ),
        name="mix_feed_forward",
    )(
        q, kv, window_lo.reshape(1, 1024), own_rows, mlp_gain, w_out, wo_s, wg, wg_s, wu, wu_s, w_down, wd_s,
    )
    return (
        layer_out.reshape(1, 1, ROWS, D),
        dc.reshape(OWNERS * PAIR, 2, 1, MAXLEN * HD),
    )


def solution(mesh):
    in_specs = (
        P("dec", "seq", "tensor", None),
        P(),
        P(None, "tensor"),
        P(),
        P(),
        P("tensor", None),
        P(),
        P(None, "tensor"),
        P(None, "tensor"),
        P("tensor", None),
        P("dec", "seq", None),
        P("dec", "seq", None),
        P(("seq", "dec"), None, "tensor", None),
        P(("seq", "dec"), None),
        P(("seq", "dec"), None),
        P(("seq", "dec"), None),
    )
    out_specs = (P("dec", "seq", "tensor", None), P(("seq", "dec"), None, "tensor", None))
    return jax.shard_map(shards, mesh=mesh, in_specs=in_specs, out_specs=out_specs, check_vma=False)
```

```python
import functools

import jax
import jax.numpy as jnp
from jax import lax
from jax.experimental import pallas as pl
from jax.experimental.pallas import tpu as pltpu
from jax.sharding import PartitionSpec as P

HD = 80
D = 2560
BT = 16
MAXLEN = 128
PAIR = 2
RQ = 8
NB = 40
UN = 432
WIDE = 896
ROWS = 64
NP = 4
PIECE = ROWS // NP
LANES = 128
KT = 512
TILES = 8
GRANT = 60 << 20
OWNERS = 8

MESH = pl.DeviceIdType.MESH
VM = pltpu.VMEM
norm_eps = 1e-05
LOG_BASE = 9.210340371976184
SCALE = HD**-0.5 * 1.4426950408889634
F32 = jnp.float32
BF = jnp.bfloat16


def place():
    t = lax.axis_index("tensor")
    return lax.div(t, 4), lax.rem(lax.div(t, 2), 2), lax.rem(t, 2)


def at_chip(x, yh, c):
    return {"tensor": (lax.rem(x + 4, 4) * 2 + yh) * 2 + c}


def col4(x):
    return lax.rem(x + 4, 4)


def batch(r, own, ca, cb, co, m):
    c0 = jnp.where(r == 0, own, jnp.where(r == 3, co, cb))
    c1 = jnp.where(r == 0, own, jnp.where(r == 3, co, ca))
    r0 = jnp.where(r == 2, 1 - m, m)
    r1 = jnp.where(r == 1, m, 1 - m)
    return c0 * 2 + r0, c1 * 2 + r1


def normed(values, gain):
    mean_square = jnp.mean(values * values, axis=-1, keepdims=True)
    return (values * lax.rsqrt(mean_square + norm_eps) * gain).astype(BF)


class Gather:
    def __init__(self, buf, send, recv):
        self.x, self.yh, self.c = place()
        self.buf, self.send, self.recv = buf, send, recv
        x, m, c, p = self.x, self.yh, self.c, 1 - self.yh
        self.a, self.b, self.o = at_chip(x + 1, m, c), at_chip(x - 1, m, c), at_chip(x, p, c)
        own, ca, cb, co = col4(x), col4(x + 1), col4(x - 1), col4(x + 2)
        self.plan = [
            (own * 2 + m, self.o, own * 2 + p),
            (own * 2 + m, self.a, cb * 2 + m),
            (own * 2 + m, self.b, ca * 2 + m),
            (own * 2 + p, self.a, cb * 2 + p),
            (own * 2 + p, self.b, ca * 2 + p),
            (cb * 2 + m, self.a, co * 2 + m),
            (co * 2 + m, self.o, co * 2 + p),
            (ca * 2 + m, self.b, co * 2 + m),
        ]

    def copy(self, k, i, got):
        plan = self.plan[7 if k == 5 and i >= NP // 2 else k]
        part = self.buf.at[plan[2] if got else plan[0], pl.ds(i * PIECE, PIECE)]
        return pltpu.make_async_remote_copy(
            src_ref=part,
            dst_ref=part,
            send_sem=self.send.at[k, i],
            recv_sem=self.recv.at[k, i],
            device_id=plan[1],
            device_id_type=MESH,
        )

    def start(self, k, i):
        self.copy(k, i, False).start()

    def got(self, k, i):
        self.copy(k, i, True).wait_recv()

    def first(self, i):
        self.start(1, i)
        self.start(2, i)
        self.start(0, i)

    def second(self):
        for i in range(NP // 2):
            self.got(1, i)
            self.start(5, i)
            self.got(2, NP - 1 - i)
            self.start(5, NP - 1 - i)

    def third(self):
        for i in range(NP):
            self.got(0, i)
            self.start(3, i)
            self.start(4, i)

    def fourth(self):
        for i in range(NP // 2):
            for e in (i, NP - 1 - i):
                self.got(5, e)
                self.start(6, e)

    def near_own(self):
        for i in range(NP // 2):
            self.got(1, NP - 1 - i)
            self.got(2, i)

    def near_partner(self):
        for i in range(NP):
            self.got(3, i)
            self.got(4, i)

    def far(self):
        for i in range(NP):
            self.got(6, i)

    def finish(self):
        for k in range(7):
            for i in range(NP):
                self.copy(k, i, False).wait_send()


class Scatter:
    def __init__(self, part, out, inb, send, recv):
        x, yh, c = place()
        self.part, self.out, self.inb, self.send, self.recv = part, out, inb, send, recv
        self.a, self.b = at_chip(x + 1, yh, c), at_chip(x - 1, yh, c)
        o = at_chip(x, 1 - yh, c)
        self.to = [o, self.a, self.b, None, self.a, self.b, o]

    def copy(self, k, i):
        rows = pl.ds(i * PIECE, PIECE)
        to = self.to[k] if k != 3 else (self.a if i < NP // 2 else self.b)
        return pltpu.make_async_remote_copy(
            src_ref=self.out.at[k, rows],
            dst_ref=self.inb.at[k, rows],
            send_sem=self.send.at[k, i],
            recv_sem=self.recv.at[k, i],
            device_id=to,
            device_id_type=MESH,
        )

    def summed(self, part, i, adds):
        rows = pl.ds(i * PIECE, PIECE)
        total = self.part[part[0], part[1], rows, :]
        for e in adds:
            self.copy(e, i).wait_recv()
            total = total + self.inb[e, rows, :].astype(F32)
        return total

    def put(self, k, part, i, adds=()):
        self.out[k, pl.ds(i * PIECE, PIECE), :] = self.summed(part, i, adds).astype(BF)
        self.copy(k, i).start()

    def sides(self):
        for i in range(NP):
            self.put(1, (2, 1), i)
            self.put(2, (2, 0), i)

    def across(self):
        for i in range(NP // 2):
            self.put(0, (3, 1), i)
            self.put(0, (3, 1), NP - 1 - i)

    def plain(self):
        for i in range(NP // 2):
            self.put(4, (1, 1), NP - 1 - i)
            self.put(5, (1, 0), i)

    def rest(self):
        for i in range(NP // 2):
            self.put(3, (3, 0), i, (0,))
            self.put(3, (3, 0), NP - 1 - i, (0,))
        for i in range(NP):
            self.put(6, (0, 1), i, (1, 2))
        for i in range(NP // 2):
            self.put(4, (1, 1), i, (3,))
            self.put(5, (1, 0), NP - 1 - i, (3,))

    def final(self, i):
        return self.summed((0, 0), i, (6, 4, 5))

    def finish(self):
        for k in range(7):
            for i in range(NP):
                self.copy(k, i).wait_send()


def signal(where):
    pl.semaphore_signal(
        pltpu.get_barrier_semaphore(), inc=1, device_id=where, device_id_type=MESH
    )


def dot_nt(left, right):
    return lax.dot_general(left, right, (((1,), (1,)), ((), ())), preferred_element_type=F32)


def first_kernel(
    tok, gain, pos, pool, lens, owners, listing, wq, wk, wv, wo, wg, wu, wd,
    q_out, kv_out, wo_s, wg_s, wu_s, wd_s, dc,
    buf, wall, wkw, wvw, outg, qst, kvst,
    ag_send, ag_recv, lsem, wsend, wrecv, hsend, hrecv, hlocal,
    zsend, zrecv, ssend, srecv, rsend, rrecv, kvl, qsem,
):
    x, yh, c = place()
    s, d = lax.axis_index("seq"), lax.axis_index("dec")
    chip = x * 2 + yh
    sib = at_chip(x, yh, 1 - c)
    start = jnp.minimum(lax.div(chip * HD, LANES), 3) * LANES
    off = chip * HD - start
    cols = pl.ds(pl.multiple_of(start, LANES), 2 * LANES)
    local = [
        pltpu.make_async_copy(wq, wall.at[pl.ds(0, 2 * HD)], lsem.at[0]),
        pltpu.make_async_copy(wk.at[:, cols], wkw, lsem.at[1]),
        pltpu.make_async_copy(wv.at[:, cols], wvw, lsem.at[2]),
    ]
    for copy in local:
        copy.start()
    ag = Gather(buf, ag_send, ag_recv)
    for where in (ag.a, ag.b, ag.o, sib):
        signal(where)
    others = []
    for k in range(1, OWNERS):
        ds, dd = k // 2, k % 2
        others.append({"seq": lax.rem(s + ds, 4), "dec": lax.rem(d + dd, 2)})
    for where in others:
        signal(where)
    buf[chip] = normed(tok[...].astype(F32), gain[...].reshape(1, D))
    pl.semaphore_wait(pltpu.get_barrier_semaphore(), 4 + len(others))
    for i in range(NP):
        ag.first(i)
    shared = [
        pltpu.make_async_remote_copy(
            src_ref=a, dst_ref=b, send_sem=wsend.at[k], recv_sem=wrecv.at[k],
            device_id=sib, device_id_type=MESH,
        )
        for k, (a, b) in enumerate(
            ((wq, wall.at[pl.ds(2 * HD, 2 * HD)]), (wo, wo_s), (wg, wg_s), (wu, wu_s), (wd, wd_s))
        )
    ]
    for copy in shared:
        copy.start()

    counts = [lax.div(lens[k] + (BT - 1), BT) for k in range(RQ)]
    firsts, so_far = [], jnp.int32(0)
    for k in range(RQ):
        firsts.append(so_far)
        so_far = so_far + counts[k]
    ranks = []
    for k in range(RQ):
        rank = jnp.int32(0)
        for e in range(k):
            rank = rank + (owners[e] == owners[k]).astype(jnp.int32)
        ranks.append(rank)
    feature = lax.broadcasted_iota(jnp.int32, (2, BT * HD), 1)

    def cut(o, _):
        for r in range(PAIR):
            at, length = jnp.int32(0), jnp.int32(0)
            for k in range(RQ):
                hit = (owners[k] == o) & (ranks[k] == r)
                at = jnp.where(hit, firsts[k], at)
                length = jnp.where(hit, lens[k], length)
            for b in range(MAXLEN // BT):
                block = pool[listing[jnp.minimum(at + b, NB - 1)]].astype(F32)
                kept = jnp.where(feature < (length - BT * b) * HD, block, 0.0)
                outg[o * PAIR + r, :, BT * HD * b : BT * HD * (b + 1)] = kept.astype(BF)
        return 0

    lax.fori_loop(0, OWNERS, cut, 0)
    me = s * 2 + d
    handed = []
    for k, where in enumerate(others):
        there = where["seq"] * 2 + where["dec"]
        handed.append(
            pltpu.make_async_remote_copy(
                src_ref=outg.at[pl.ds(there * PAIR, PAIR)],
                dst_ref=dc.at[pl.ds(me * PAIR, PAIR)],
                send_sem=hsend.at[k],
                recv_sem=hrecv.at[k],
                device_id=where,
                device_id_type=MESH,
            )
        )
    keep = pltpu.make_async_copy(
        outg.at[pl.ds(me * PAIR, PAIR)], dc.at[pl.ds(me * PAIR, PAIR)], hlocal
    )
    ag.second()
    for k in (1, 3, 5, 0, 2):
        handed[k].start()
    keep.start()

    row = lax.broadcasted_iota(jnp.int32, (HD, 2 * LANES), 0)
    col = lax.broadcasted_iota(jnp.int32, (HD, 2 * LANES), 1)
    pick = (col == row + off).astype(F32).astype(BF)
    chunk = 512

    def laid(src, begin):
        def one(i, _):
            rows = pl.ds(pl.multiple_of(i * chunk, chunk), chunk)
            wall[begin : begin + HD, rows] = dot_nt(pick, src[rows, :]).astype(BF)
            return 0

        lax.fori_loop(0, D // chunk, one, 0)

    for copy in local:
        copy.wait()
    laid(wkw, 4 * HD)
    laid(wvw, 5 * HD)
    half = HD // 2
    rate = jnp.exp(
        lax.broadcasted_iota(jnp.int32, (half, 1), 0).astype(F32) * (-2.0 / HD * LOG_BASE)
    )
    low_lanes = lax.broadcasted_iota(jnp.int32, (1, LANES), 1) < ROWS

    def own_half(two, one_more):
        low = jnp.where(c == 0, two, pltpu.roll(two, ROWS, 1))
        high = jnp.where(c == 0, pltpu.roll(one_more, ROWS, 1), one_more)
        return jnp.where(low_lanes, low, high)

    def lanes_of(core):
        return pl.ds(pl.multiple_of(core * 256, 256), 256)

    def moved(src, dst, send, recv, where):
        return pltpu.make_async_remote_copy(
            src_ref=src, dst_ref=dst, send_sem=send, recv_sem=recv, device_id=where, device_id_type=MESH
        )

    def to_later(e, k):
        dst = kv_out.at[s * 2 + k, :, lanes_of(c)]
        return moved(kvst.at[k], dst, zsend.at[e - 1, k], zrecv.at[e - 1, k], {"seq": lax.rem(s + e, 4)})

    def to_sibling(k):
        dst = kv_out.at[s * 2 + k, :, lanes_of(c)]
        return moved(kvst.at[k], dst, ssend.at[k], srecv.at[k], sib)

    def from_earlier(e, k, core, send, recv):
        part = kv_out.at[lax.rem(s - e + 4, 4) * 2 + k, :, lanes_of(core)]
        return moved(part, part, send.at[e - 1, k], recv.at[e - 1, k], sib)

    def own_copies(k):
        return (
            pltpu.make_async_copy(kvst.at[k], kv_out.at[s * 2 + k, :, lanes_of(c)], kvl.at[k]),
            pltpu.make_async_copy(qst.at[pl.ds(2 * k, 2)], q_out.at[pl.ds(2 * k, 2)], qsem.at[k]),
        )

    def rotated(v, cosine, sine):
        a, b = v[:half], v[half:]
        return jnp.concatenate([a * cosine - b * sine, b * cosine + a * sine], axis=0)

    def chip_lanes(ref, n):
        return ref[:, pl.ds(pl.multiple_of(n * LANES, LANES), LANES)].astype(F32)

    def project(k, _):
        @pl.when(k == 0)
        def _():
            ag.third()
            shared[0].wait_recv()
            ag.near_own()

        @pl.when(k == 1)
        def _():
            ag.fourth()
            for e in (4, 6):
                handed[e].start()
            ag.near_partner()
            ag.far()

        four = []
        for r in (2 * k, 2 * k + 1):
            four += list(batch(r, x, col4(x + 1), col4(x - 1), col4(x + 2), yh))
        shards_in = jnp.concatenate([buf[n] for n in four], axis=0)
        out = dot_nt(wall[...], shards_in)
        places = jnp.concatenate(
            [
                own_half(chip_lanes(pos, four[0]), chip_lanes(pos, four[1])),
                own_half(chip_lanes(pos, four[2]), chip_lanes(pos, four[3])),
            ],
            axis=1,
        )
        angles = rate * places
        cosine, sine = jnp.cos(angles), jnp.sin(angles)
        kvst[k, 0:HD] = rotated(out[4 * HD : 5 * HD], cosine, sine).astype(BF)
        kvst[k, HD:] = out[5 * HD :].astype(BF)
        for e in (1, 2, 3):

            @pl.when(s + e < 4)
            def _():
                to_later(e, k).start()

        to_sibling(k).start()
        for h in range(4):
            v = (rotated(out[h * HD : (h + 1) * HD], cosine, sine) * SCALE).astype(BF)
            for n in range(2):
                qst[2 * k + n, :, h * LANES : (h + 1) * LANES] = v[:, n * LANES : (n + 1) * LANES]
        for copy in own_copies(k):
            copy.start()
        return 0

    lax.fori_loop(0, 2, project, 0)
    for k in range(2):
        for e in (1, 2, 3):

            @pl.when(s >= e)
            def _():
                from_earlier(e, k, c, zsend, zrecv).wait_recv()
                from_earlier(e, k, c, rsend, rrecv).start()

    ag.finish()
    for k in range(2):
        to_sibling(k).wait_send()
        for copy in own_copies(k):
            copy.wait()
        part = kv_out.at[s * 2 + k, :, lanes_of(1 - c)]
        moved(part, part, ssend.at[k], srecv.at[k], sib).wait_recv()
        for e in (1, 2, 3):

            @pl.when(s + e < 4)
            def _():
                to_later(e, k).wait_send()

            @pl.when(s >= e)
            def _():
                from_earlier(e, k, c, rsend, rrecv).wait_send()
                from_earlier(e, k, 1 - c, rsend, rrecv).wait_recv()

    for k, where in enumerate(others):
        handed[k].wait_send()
        back = lax.rem(s - (k + 1) // 2 + 4, 4) * 2 + lax.rem(d - (k + 1) % 2 + 2, 2)
        pltpu.make_async_remote_copy(
            src_ref=outg.at[pl.ds(back * PAIR, PAIR)],
            dst_ref=dc.at[pl.ds(back * PAIR, PAIR)],
            send_sem=hsend.at[k],
            recv_sem=hrecv.at[k],
            device_id=where,
            device_id_type=MESH,
        ).wait_recv()
    keep.wait()
    for k, copy in enumerate(shared):
        copy.wait_send()
        if k:
            copy.wait_recv()


def last_kernel(
    q_hbm, kv_hbm, lo_ref, tok, gain, wo, wo_s, wg, wg_s, wu, wu_s, wd, wd_s,
    out,
    buf, res, part, hv, q_ref, kv_ref, keys, kpos, sc0, sc1, mx, acc, wov, raw, wt, ds, o1, i1, i2,
    lsem, ag_send, ag_recv, s1, r1, s2, r2,
):
    ag = Gather(buf, ag_send, ag_recv)
    for where in (ag.a, ag.b, ag.o):
        signal(where)
    loads = [
        (q_hbm, q_ref.at[:, pl.ds(0, HD)]),
        (kv_hbm, kv_ref.at[:, pl.ds(0, 2 * HD)]),
    ]
    for e, src in enumerate((wo, wo_s)):
        for h in range(2):
            loads.append((src.at[pl.ds(h * HD, HD)], wov.at[pl.ds((2 * e + h) * LANES, HD)]))
    for e, src in enumerate((wg, wg_s, wu, wu_s)):
        loads.append((src, raw.at[e // 2, pl.ds(e % 2 * UN, UN)]))
    for e, src in enumerate((wd, wd_s)):
        loads.append((src, ds.at[pl.ds(e * UN, UN)]))
    copies = [pltpu.make_async_copy(a, b, lsem.at[k]) for k, (a, b) in enumerate(loads)]
    for copy in copies:
        copy.start()
    for h in range(4):
        wov[h * LANES + HD : (h + 1) * LANES, :] = jnp.zeros((LANES - HD, D), BF)
    raw[:, 2 * UN :, :] = jnp.zeros((2, WIDE - 2 * UN, D), BF)
    ds[2 * UN :, :] = jnp.zeros((WIDE - 2 * UN, D), BF)
    sc = (sc0, sc1)
    x, m, c = ag.x, ag.yh, ag.c
    s = lax.axis_index("seq")
    ring = (x, col4(x + 1), col4(x - 1), col4(x + 2), m)
    row = lax.broadcasted_iota(jnp.int32, (2 * LANES, LANES), 0)
    quarter, local = lax.div(row, ROWS), lax.rem(row, ROWS)
    for e in range(2):
        chips = batch(2 * e, *ring) + batch(2 * e + 1, *ring)
        chip = jnp.where(
            quarter < 2, jnp.where(quarter == 0, chips[0], chips[1]), jnp.where(quarter == 2, chips[2], chips[3])
        )
        for core in range(2):
            kpos[e, core * 256 : core * 256 + 256] = chip * LANES + core * ROWS + local
    ones = lax.broadcasted_iota(jnp.int32, (TILES, 16, KT), 1) == 0
    kv_ref[:, 2 * HD :, :] = ones.astype(F32).astype(BF)
    q_ref[:, HD:, :] = jnp.zeros((4, LANES - HD, 4 * LANES), BF)
    lane = lax.broadcasted_iota(jnp.int32, (1, LANES), 1)
    low_lanes = lane < ROWS
    for copy in copies[:2]:
        copy.wait()

    def upright(t, _):
        k = kv_ref[t, 0:HD].astype(F32)
        k = jnp.concatenate([k, jnp.zeros((LANES - HD, KT), F32)], axis=0)
        keys[t] = k.T.astype(BF)
        return 0

    lax.fori_loop(0, 2 * s + 2, upright, 0)

    def attend(r):
        n0, n1 = batch(r, *ring)
        one = lo_ref[:, pl.ds(pl.multiple_of(n0 * LANES, LANES), LANES)].astype(F32)
        two = lo_ref[:, pl.ds(pl.multiple_of(n1 * LANES, LANES), LANES)].astype(F32)
        low = jnp.where(c == 0, one, pltpu.roll(one, ROWS, 1))
        high = jnp.where(c == 0, pltpu.roll(two, ROWS, 1), two)
        lows = jnp.where(low_lanes, low, high).astype(jnp.int32)
        places = c * ROWS + jnp.where(low_lanes, n0 * LANES + lane, n1 * LANES + lane - ROWS)
        acc[...] = jnp.zeros_like(acc)

        def score(b, slot, seen):
            top = None
            for e in range(2):
                v = jnp.dot(keys[2 * b + e], q_ref[r], preferred_element_type=F32)
                v = jnp.concatenate(
                    [jnp.where(seen[e], v[:, h * LANES : (h + 1) * LANES], -jnp.inf) for h in range(4)],
                    axis=1,
                )
                sc[slot][e] = v
                peak = jnp.max(v.reshape(KT // 8, 8, 4 * LANES), axis=0)
                top = peak if top is None else jnp.maximum(top, peak)
            return jnp.max(top, axis=0, keepdims=True)

        def mix(b, slot):
            now = mx[0:1, :]
            total = acc[0 : HD + 16, :] * jnp.exp2(mx[1:2, :] - now)
            for e in range(2):
                p = jnp.exp2(sc[slot][e] - now).astype(BF)
                total = total + jnp.dot(kv_ref[2 * b + e, HD:], p, preferred_element_type=F32)
            acc[0 : HD + 16, :] = total

        low = [kpos[e] for e in range(2)]
        top = score(s, 0, [(k >= lows - s * 1024) & (k <= places) for k in low])
        mx[0:1, :] = top
        mx[1:2, :] = top
        for i in range(3):

            @pl.when(s > i)
            def _():
                b = s - 1 - i
                mix(b + 1, i % 2)
                top = score(b, 1 - i % 2, [kpos[e] >= lows - b * 1024 for e in range(2)])
                now = mx[0:1, :]
                mx[1:2, :] = now
                mx[0:1, :] = jnp.maximum(now, top)

        for i in range(2):

            @pl.when(lax.rem(s, 2) == i)
            def _():
                mix(0, i)

        heads = acc[...] / acc[HD : HD + 1, :]
        for h in range(4):
            hv[:, h * LANES : (h + 1) * LANES] = heads[:, h * LANES : (h + 1) * LANES].T.astype(BF)

    rs = Scatter(part, o1, i1, s1, r1)

    def project(n, _):
        r = jnp.where(n < 2, n + 2, 3 - n)
        attend(r)

        @pl.when(n == 0)
        def _():
            for copy in copies[2:6]:
                copy.wait()

        part[r] = jnp.dot(hv[...], wov[...], preferred_element_type=F32).reshape(2, ROWS, D)

        @pl.when(n == 0)
        def _():
            pl.semaphore_wait(pltpu.get_barrier_semaphore(), 3)
            rs.sides()

        @pl.when(n == 1)
        def _():
            rs.across()

        @pl.when(n == 2)
        def _():
            rs.plain()

        return 0

    lax.fori_loop(0, 4, project, 0)
    rs.rest()
    chip = x * 2 + m
    for i in range(NP):
        rows = pl.ds(i * PIECE, PIECE)
        total = tok[rows, :].astype(F32) + rs.final(i)
        res[rows, :] = total
        buf[chip, rows, :] = normed(total, gain[...].reshape(1, D))
        ag.first(i)
    for copy in copies[6:]:
        copy.wait()

    def turn(n, _):
        cols = pl.ds(pl.multiple_of(n * 256, 256), 256)
        for e in range(2):
            wt[cols, e * WIDE : (e + 1) * WIDE] = raw[e, :, cols].astype(F32).T.astype(BF)
        return 0

    lax.fori_loop(0, D // 256, turn, 0)
    rs.finish()

    rs2 = Scatter(part, o1, i2, s2, r2)
    ag.second()
    ag.third()

    def feed(r, _):
        @pl.when(r == 1)
        def _():
            ag.near_own()

        @pl.when(r == 2)
        def _():
            ag.fourth()
            ag.near_partner()

        @pl.when(r == 3)
        def _():
            rs2.sides()
            ag.far()

        n0, n1 = batch(r, *ring)
        both = jnp.concatenate([buf[n0], buf[n1]], axis=0)
        wide = jnp.dot(both, wt[...], preferred_element_type=F32)
        gate, up = wide[:, :WIDE], wide[:, WIDE:]
        hid = (gate / (1.0 + jnp.exp(-gate)) * up).astype(BF)
        part[r] = jnp.dot(hid, ds[...], preferred_element_type=F32).reshape(2, ROWS, D)
        return 0

    lax.fori_loop(0, 4, feed, 0)
    rs2.across()
    rs2.plain()
    rs2.rest()
    for i in range(NP):
        rows = pl.ds(i * PIECE, PIECE)
        out[rows, :] = (res[rows, :] + rs2.final(i)).astype(BF)
    ag.finish()
    rs2.finish()


VMEM_SPEC = pl.BlockSpec(memory_space=pltpu.VMEM)
SMEM_SPEC = pl.BlockSpec(memory_space=pltpu.SMEM)
HBM_SPEC = pl.BlockSpec(memory_space=pltpu.HBM)
DMA = pltpu.SemaphoreType.DMA


def shape(*dims, dtype=BF):
    return jax.ShapeDtypeStruct(dims, dtype)


def shards(
    tokens, attn_gain, w_query, w_key, w_value, w_out, mlp_gain, w_gate, w_up, w_down,
    positions, window_lo, cache_pool, req_len, req_owner, block_list,
):
    own_rows = tokens[0, 0]
    wq, wg, wu = w_query.T, w_gate.T, w_up.T

    q, kv, wo_s, wg_s, wu_s, wd_s, dc = pl.pallas_call(
        first_kernel,
        out_shape=(
            shape(4, HD, 4 * LANES),
            shape(TILES, 2 * HD, KT),
            shape(*w_out.shape),
            shape(*wg.shape),
            shape(*wu.shape),
            shape(*w_down.shape),
            shape(OWNERS * PAIR, 2, MAXLEN * HD),
        ),
        in_specs=[VMEM_SPEC] * 4 + [SMEM_SPEC] * 3 + [HBM_SPEC] * 7,
        out_specs=(HBM_SPEC,) * 7,
        scratch_shapes=[
            VM((8, ROWS, D), BF),
            VM((6 * HD, D), BF),
            VM((D, 2 * LANES), BF),
            VM((D, 2 * LANES), BF),
            VM((OWNERS * PAIR, 2, MAXLEN * HD), BF),
            VM((4, HD, 4 * LANES), BF),
            VM((2, 2 * HD, 2 * LANES), BF),
            DMA((7, NP)),
            DMA((7, NP)),
            DMA((3,)),
            DMA((5,)),
            DMA((5,)),
            DMA((7,)),
            DMA((7,)),
            DMA,
            DMA((3, 2)),
            DMA((3, 2)),
            DMA((2,)),
            DMA((2,)),
            DMA((3, 2)),
            DMA((3, 2)),
            DMA((2,)),
            DMA((2,)),
        ],
        compiler_params=pltpu.CompilerParams(
            collective_id=0, has_side_effects=True, vmem_limit_bytes=GRANT
        ),
        name="gather_project",
    )(
        own_rows, attn_gain, positions.reshape(1, 1024), cache_pool.reshape(NB, 2, BT * HD),
        req_len.reshape(RQ), req_owner.reshape(RQ), block_list.reshape(NB),
        wq, w_key, w_value, w_out, wg, wu, w_down,
    )

    layer_out = pl.pallas_call(
        last_kernel,
        out_shape=shape(ROWS, D),
        in_specs=[HBM_SPEC] * 2 + [VMEM_SPEC] * 3 + [HBM_SPEC] * 8,
        out_specs=VMEM_SPEC,
        scratch_shapes=[
            VM((8, ROWS, D), BF),
            VM((ROWS, D), F32),
            VM((4, 2, ROWS, D), F32),
            VM((LANES, 4 * LANES), BF),
            VM((4, LANES, 4 * LANES), BF),
            VM((TILES, 2 * HD + 16, KT), BF),
            VM((TILES, KT, LANES), BF),
            VM((2, KT, LANES), jnp.int32),
            VM((2, KT, 4 * LANES), F32),
            VM((2, KT, 4 * LANES), F32),
            VM((8, 4 * LANES), F32),
            VM((LANES, 4 * LANES), F32),
            VM((4 * LANES, D), BF),
            VM((2, WIDE, D), BF),
            VM((D, 2 * WIDE), BF),
            VM((WIDE, D), BF),
            VM((7, ROWS, D), BF),
            VM((7, ROWS, D), BF),
            VM((7, ROWS, D), BF),
            DMA((12,)),
        ]
        + [DMA((7, NP))] * 6,
        compiler_params=pltpu.CompilerParams(
            collective_id=1, has_side_effects=True, vmem_limit_bytes=GRANT
        ),
        name="mix_feed_forward",
    )(
        q, kv, window_lo.reshape(1, 1024), own_rows, mlp_gain, w_out, wo_s, wg, wg_s, wu, wu_s, w_down, wd_s,
    )
    return (
        layer_out.reshape(1, 1, ROWS, D),
        dc.reshape(OWNERS * PAIR, 2, 1, MAXLEN * HD),
    )


def solution(mesh):
    in_specs = (
        P("dec", "seq", "tensor", None),
        P(),
        P(None, "tensor"),
        P(),
        P(),
        P("tensor", None),
        P(),
        P(None, "tensor"),
        P(None, "tensor"),
        P("tensor", None),
        P("dec", "seq", None),
        P("dec", "seq", None),
        P(("seq", "dec"), None, "tensor", None),
        P(("seq", "dec"), None),
        P(("seq", "dec"), None),
        P(("seq", "dec"), None),
    )
    out_specs = (P("dec", "seq", "tensor", None), P(("seq", "dec"), None, "tensor", None))
    return jax.shard_map(shards, mesh=mesh, in_specs=in_specs, out_specs=out_specs, check_vma=False)
```

```python
import functools

import jax
import jax.numpy as jnp
from jax import lax
from jax.experimental import pallas as pl
from jax.experimental.pallas import tpu as pltpu
from jax.sharding import PartitionSpec as P

HD = 80
D = 2560
BT = 16
MAXLEN = 128
PAIR = 2
RQ = 8
NB = 40
UN = 432
WIDE = 896
ROWS = 64
NP = 4
PIECE = ROWS // NP
LANES = 128
KT = 512
TILES = 8
GRANT = 60 << 20
OWNERS = 8

MESH = pl.DeviceIdType.MESH
VM = pltpu.VMEM
norm_eps = 1e-05
LOG_BASE = 9.210340371976184
SCALE = HD**-0.5 * 1.4426950408889634
F32 = jnp.float32
BF = jnp.bfloat16


def place():
    t = lax.axis_index("tensor")
    return lax.div(t, 4), lax.rem(lax.div(t, 2), 2), lax.rem(t, 2)


def at_chip(x, yh, c):
    return {"tensor": (lax.rem(x + 4, 4) * 2 + yh) * 2 + c}


def col4(x):
    return lax.rem(x + 4, 4)


def batch(r, own, ca, cb, co, m):
    c0 = jnp.where(r == 0, own, jnp.where(r == 3, co, cb))
    c1 = jnp.where(r == 0, own, jnp.where(r == 3, co, ca))
    r0 = jnp.where(r == 2, 1 - m, m)
    r1 = jnp.where(r == 1, m, 1 - m)
    return c0 * 2 + r0, c1 * 2 + r1


def normed(values, gain):
    mean_square = jnp.mean(values * values, axis=-1, keepdims=True)
    return (values * lax.rsqrt(mean_square + norm_eps) * gain).astype(BF)


class Gather:
    def __init__(self, buf, send, recv):
        self.x, self.yh, self.c = place()
        self.buf, self.send, self.recv = buf, send, recv
        x, m, c, p = self.x, self.yh, self.c, 1 - self.yh
        self.a, self.b, self.o = at_chip(x + 1, m, c), at_chip(x - 1, m, c), at_chip(x, p, c)
        own, ca, cb, co = col4(x), col4(x + 1), col4(x - 1), col4(x + 2)
        self.plan = [
            (own * 2 + m, self.o, own * 2 + p),
            (own * 2 + m, self.a, cb * 2 + m),
            (own * 2 + m, self.b, ca * 2 + m),
            (own * 2 + p, self.a, cb * 2 + p),
            (own * 2 + p, self.b, ca * 2 + p),
            (cb * 2 + m, self.a, co * 2 + m),
            (co * 2 + m, self.o, co * 2 + p),
            (ca * 2 + m, self.b, co * 2 + m),
        ]

    def copy(self, k, i, got):
        plan = self.plan[7 if k == 5 and i >= NP // 2 else k]
        part = self.buf.at[plan[2] if got else plan[0], pl.ds(i * PIECE, PIECE)]
        return pltpu.make_async_remote_copy(
            src_ref=part,
            dst_ref=part,
            send_sem=self.send.at[k, i],
            recv_sem=self.recv.at[k, i],
            device_id=plan[1],
            device_id_type=MESH,
        )

    def start(self, k, i):
        self.copy(k, i, False).start()

    def got(self, k, i):
        self.copy(k, i, True).wait_recv()

    def first(self, i):
        self.start(1, i)
        self.start(2, i)
        self.start(0, i)

    def second(self):
        for i in range(NP // 2):
            self.got(1, i)
            self.start(5, i)
            self.got(2, NP - 1 - i)
            self.start(5, NP - 1 - i)

    def third(self):
        for i in range(NP):
            self.got(0, i)
            self.start(3, i)
            self.start(4, i)

    def fourth(self):
        for i in range(NP // 2):
            for e in (i, NP - 1 - i):
                self.got(5, e)
                self.start(6, e)

    def near_own(self):
        for i in range(NP // 2):
            self.got(1, NP - 1 - i)
            self.got(2, i)

    def near_partner(self):
        for i in range(NP):
            self.got(3, i)
            self.got(4, i)

    def far(self):
        for i in range(NP):
            self.got(6, i)

    def finish(self):
        for k in range(7):
            for i in range(NP):
                self.copy(k, i, False).wait_send()


class Scatter:
    def __init__(self, part, out, inb, send, recv):
        x, yh, c = place()
        self.part, self.out, self.inb, self.send, self.recv = part, out, inb, send, recv
        self.a, self.b = at_chip(x + 1, yh, c), at_chip(x - 1, yh, c)
        o = at_chip(x, 1 - yh, c)
        self.to = [o, self.a, self.b, None, self.a, self.b, o]

    def copy(self, k, i):
        rows = pl.ds(i * PIECE, PIECE)
        to = self.to[k] if k != 3 else (self.a if i < NP // 2 else self.b)
        return pltpu.make_async_remote_copy(
            src_ref=self.out.at[k, rows],
            dst_ref=self.inb.at[k, rows],
            send_sem=self.send.at[k, i],
            recv_sem=self.recv.at[k, i],
            device_id=to,
            device_id_type=MESH,
        )

    def summed(self, part, i, adds):
        rows = pl.ds(i * PIECE, PIECE)
        total = self.part[part[0], part[1], rows, :]
        for e in adds:
            self.copy(e, i).wait_recv()
            total = total + self.inb[e, rows, :].astype(F32)
        return total

    def put(self, k, part, i, adds=()):
        self.out[k, pl.ds(i * PIECE, PIECE), :] = self.summed(part, i, adds).astype(BF)
        self.copy(k, i).start()

    def sides(self):
        for i in range(NP):
            self.put(1, (2, 1), i)
            self.put(2, (2, 0), i)

    def across(self):
        for i in range(NP // 2):
            self.put(0, (3, 1), i)
            self.put(0, (3, 1), NP - 1 - i)

    def plain(self):
        for i in range(NP // 2):
            self.put(4, (1, 1), NP - 1 - i)
            self.put(5, (1, 0), i)

    def rest(self):
        for i in range(NP // 2):
            self.put(3, (3, 0), i, (0,))
            self.put(3, (3, 0), NP - 1 - i, (0,))
        for i in range(NP):
            self.put(6, (0, 1), i, (1, 2))
        for i in range(NP // 2):
            self.put(4, (1, 1), i, (3,))
            self.put(5, (1, 0), NP - 1 - i, (3,))

    def final(self, i):
        return self.summed((0, 0), i, (6, 4, 5))

    def finish(self):
        for k in range(7):
            for i in range(NP):
                self.copy(k, i).wait_send()


def signal(where):
    pl.semaphore_signal(
        pltpu.get_barrier_semaphore(), inc=1, device_id=where, device_id_type=MESH
    )


def dot_nt(left, right):
    return lax.dot_general(left, right, (((1,), (1,)), ((), ())), preferred_element_type=F32)


def layer_kernel(
    tok, gain, gain2, pos, lo_ref, pool, lens, owners, listing, wq, wk, wv, wo, wg, wu, wd,
    out, dc,
    buf, wall, wkw, wvw, outg, res, part, hv, q_ref, kv_ref, keys, kpos, sc0, sc1, mx, acc,
    wov, raw, wt, ds, o1, i1, i2,
    ag_send, ag_recv, lsem, wsend, wrecv, hsend, hrecv, hlocal,
    zsend, zrecv, ssend, srecv, rsend, rrecv, g2s, g2r, s1, r1, s2, r2,
):
    x, yh, c = place()
    s, d = lax.axis_index("seq"), lax.axis_index("dec")
    chip = x * 2 + yh
    sib = at_chip(x, yh, 1 - c)
    start = jnp.minimum(lax.div(chip * HD, LANES), 3) * LANES
    off = chip * HD - start
    cols = pl.ds(pl.multiple_of(start, LANES), 2 * LANES)
    local = [
        pltpu.make_async_copy(wq, wall.at[pl.ds(0, 2 * HD)], lsem.at[0]),
        pltpu.make_async_copy(wk.at[:, cols], wkw, lsem.at[1]),
        pltpu.make_async_copy(wv.at[:, cols], wvw, lsem.at[2]),
        pltpu.make_async_copy(wo.at[pl.ds(0, HD)], wov.at[pl.ds(0, HD)], lsem.at[3]),
        pltpu.make_async_copy(wo.at[pl.ds(HD, HD)], wov.at[pl.ds(LANES, HD)], lsem.at[4]),
        pltpu.make_async_copy(wg, raw.at[0, pl.ds(0, UN)], lsem.at[5]),
        pltpu.make_async_copy(wu, raw.at[1, pl.ds(0, UN)], lsem.at[6]),
        pltpu.make_async_copy(wd, ds.at[pl.ds(0, UN)], lsem.at[7]),
    ]
    for copy in local:
        copy.start()
    ag = Gather(buf, ag_send, ag_recv)
    for where in (ag.a, ag.b, ag.o, sib):
        signal(where)
    others = []
    for k in range(1, OWNERS):
        others.append({"seq": lax.rem(s + k // 2, 4), "dec": lax.rem(d + k % 2, 2)})
    for where in others:
        signal(where)
    buf[chip] = normed(tok[...].astype(F32), gain[...].reshape(1, D))
    pl.semaphore_wait(pltpu.get_barrier_semaphore(), 4 + len(others))
    for i in range(NP):
        ag.first(i)
    shared = [
        pltpu.make_async_remote_copy(
            src_ref=a, dst_ref=b, send_sem=wsend.at[k], recv_sem=wrecv.at[k],
            device_id=sib, device_id_type=MESH,
        )
        for k, (a, b) in enumerate(
            (
                (wq, wall.at[pl.ds(2 * HD, 2 * HD)]),
                (wo.at[pl.ds(0, HD)], wov.at[pl.ds(2 * LANES, HD)]),
                (wo.at[pl.ds(HD, HD)], wov.at[pl.ds(3 * LANES, HD)]),
                (wg, raw.at[0, pl.ds(UN, UN)]),
                (wu, raw.at[1, pl.ds(UN, UN)]),
                (wd, ds.at[pl.ds(UN, UN)]),
            )
        )
    ]
    for copy in shared:
        copy.start()

    counts = [lax.div(lens[k] + (BT - 1), BT) for k in range(RQ)]
    firsts, so_far = [], jnp.int32(0)
    for k in range(RQ):
        firsts.append(so_far)
        so_far = so_far + counts[k]
    ranks = []
    for k in range(RQ):
        rank = jnp.int32(0)
        for e in range(k):
            rank = rank + (owners[e] == owners[k]).astype(jnp.int32)
        ranks.append(rank)
    feature = lax.broadcasted_iota(jnp.int32, (2, BT * HD), 1)

    def cut(o, _):
        for r in range(PAIR):
            at, length = jnp.int32(0), jnp.int32(0)
            for k in range(RQ):
                hit = (owners[k] == o) & (ranks[k] == r)
                at = jnp.where(hit, firsts[k], at)
                length = jnp.where(hit, lens[k], length)
            for b in range(MAXLEN // BT):
                block = pool[listing[jnp.minimum(at + b, NB - 1)]].astype(F32)
                kept = jnp.where(feature < (length - BT * b) * HD, block, 0.0)
                outg[o * PAIR + r, :, BT * HD * b : BT * HD * (b + 1)] = kept.astype(BF)
        return 0

    lax.fori_loop(0, OWNERS, cut, 0)
    me = s * 2 + d
    handed = []
    for k, where in enumerate(others):
        there = where["seq"] * 2 + where["dec"]
        handed.append(
            pltpu.make_async_remote_copy(
                src_ref=outg.at[pl.ds(there * PAIR, PAIR)],
                dst_ref=dc.at[pl.ds(me * PAIR, PAIR)],
                send_sem=hsend.at[k],
                recv_sem=hrecv.at[k],
                device_id=where,
                device_id_type=MESH,
            )
        )
    keep = pltpu.make_async_copy(
        outg.at[pl.ds(me * PAIR, PAIR)], dc.at[pl.ds(me * PAIR, PAIR)], hlocal
    )
    ag.second()
    for k in (1, 3, 5, 0, 2):
        handed[k].start()
    keep.start()

    row = lax.broadcasted_iota(jnp.int32, (HD, 2 * LANES), 0)
    col = lax.broadcasted_iota(jnp.int32, (HD, 2 * LANES), 1)
    pick = (col == row + off).astype(F32).astype(BF)
    chunk = 512

    def laid(src, begin):
        def one(i, _):
            rows = pl.ds(pl.multiple_of(i * chunk, chunk), chunk)
            wall[begin : begin + HD, rows] = dot_nt(pick, src[rows, :]).astype(BF)
            return 0

        lax.fori_loop(0, D // chunk, one, 0)

    for copy in local[:3]:
        copy.wait()
    laid(wkw, 4 * HD)
    laid(wvw, 5 * HD)
    half = HD // 2
    rate = jnp.exp(
        lax.broadcasted_iota(jnp.int32, (half, 1), 0).astype(F32) * (-2.0 / HD * LOG_BASE)
    )
    low_lanes = lax.broadcasted_iota(jnp.int32, (1, LANES), 1) < ROWS

    def own_half(two, one_more):
        low = jnp.where(c == 0, two, pltpu.roll(two, ROWS, 1))
        high = jnp.where(c == 0, pltpu.roll(one_more, ROWS, 1), one_more)
        return jnp.where(low_lanes, low, high)

    def lanes_of(core):
        return pl.ds(pl.multiple_of(core * 256, 256), 256)

    def moved(src, dst, send, recv, where):
        return pltpu.make_async_remote_copy(
            src_ref=src, dst_ref=dst, send_sem=send, recv_sem=recv, device_id=where, device_id_type=MESH
        )

    def piece(sq, k, core):
        return kv_ref.at[sq * 2 + k, pl.ds(0, 2 * HD), lanes_of(core)]

    def to_later(e, k):
        own = piece(s, k, c)
        return moved(own, own, zsend.at[e - 1, k], zrecv.at[e - 1, k], {"seq": lax.rem(s + e, 4)})

    def to_sibling(k, core):
        own = piece(s, k, core)
        return moved(own, own, ssend.at[k], srecv.at[k], sib)

    def from_earlier(e, k, core, send, recv):
        there = piece(lax.rem(s - e + 4, 4), k, core)
        return moved(there, there, send.at[e - 1, k], recv.at[e - 1, k], sib)

    def relay(k):
        for e in (1, 2, 3):

            @pl.when(s >= e)
            def _():
                from_earlier(e, k, c, zsend, zrecv).wait_recv()
                from_earlier(e, k, c, rsend, rrecv).start()

    def rotated(v, cosine, sine):
        a, b = v[:half], v[half:]
        return jnp.concatenate([a * cosine - b * sine, b * cosine + a * sine], axis=0)

    def chip_lanes(ref, n):
        return ref[:, pl.ds(pl.multiple_of(n * LANES, LANES), LANES)].astype(F32)

    def make(k, _):
        @pl.when(k == 0)
        def _():
            ag.third()
            shared[0].wait_recv()
            ag.near_own()

        @pl.when(k == 1)
        def _():
            ag.fourth()
            for e in (4, 6):
                handed[e].start()
            ag.near_partner()
            ag.far()
            relay(0)

        four = []
        for r in (2 * k, 2 * k + 1):
            four += list(batch(r, x, col4(x + 1), col4(x - 1), col4(x + 2), yh))
        shards_in = jnp.concatenate([buf[n] for n in four], axis=0)
        made = dot_nt(wall[...], shards_in)
        places = jnp.concatenate(
            [
                own_half(chip_lanes(pos, four[0]), chip_lanes(pos, four[1])),
                own_half(chip_lanes(pos, four[2]), chip_lanes(pos, four[3])),
            ],
            axis=1,
        )
        angles = rate * places
        cosine, sine = jnp.cos(angles), jnp.sin(angles)
        kv_ref[s * 2 + k, 0:HD, lanes_of(c)] = rotated(made[4 * HD : 5 * HD], cosine, sine).astype(BF)
        kv_ref[s * 2 + k, HD : 2 * HD, lanes_of(c)] = made[5 * HD :].astype(BF)
        for e in (1, 2, 3):

            @pl.when(s + e < 4)
            def _():
                to_later(e, k).start()

        to_sibling(k, c).start()
        for h in range(4):
            v = (rotated(made[h * HD : (h + 1) * HD], cosine, sine) * SCALE).astype(BF)
            for n in range(2):
                q_ref[2 * k + n, 0:HD, h * LANES : (h + 1) * LANES] = v[:, n * LANES : (n + 1) * LANES]
        return 0

    for h in range(4):
        wov[h * LANES + HD : (h + 1) * LANES, :] = jnp.zeros((LANES - HD, D), BF)
    raw[:, 2 * UN :, :] = jnp.zeros((2, WIDE - 2 * UN, D), BF)
    ds[2 * UN :, :] = jnp.zeros((WIDE - 2 * UN, D), BF)
    sc = (sc0, sc1)
    m = yh
    ring = (x, col4(x + 1), col4(x - 1), col4(x + 2), m)
    row = lax.broadcasted_iota(jnp.int32, (2 * LANES, LANES), 0)
    quarter, spot = lax.div(row, ROWS), lax.rem(row, ROWS)
    for e in range(2):
        chips = batch(2 * e, *ring) + batch(2 * e + 1, *ring)
        which = jnp.where(
            quarter < 2, jnp.where(quarter == 0, chips[0], chips[1]), jnp.where(quarter == 2, chips[2], chips[3])
        )
        for core in range(2):
            kpos[e, core * 256 : core * 256 + 256] = which * LANES + core * ROWS + spot
    ones = lax.broadcasted_iota(jnp.int32, (TILES, 16, KT), 1) == 0
    kv_ref[:, 2 * HD :, :] = ones.astype(F32).astype(BF)
    q_ref[:, HD:, :] = jnp.zeros((4, LANES - HD, 4 * LANES), BF)
    lane = lax.broadcasted_iota(jnp.int32, (1, LANES), 1)

    lax.fori_loop(0, 2, make, 0)
    def upright(t, _):
        k = kv_ref[t, 0:HD].astype(F32)
        k = jnp.concatenate([k, jnp.zeros((LANES - HD, KT), F32)], axis=0)
        keys[t] = k.T.astype(BF)
        return 0

    for k in range(2):
        to_sibling(k, 1 - c).wait_recv()
    lax.fori_loop(2 * s, 2 * s + 2, upright, 0)
    ag.finish()

    def attend(n, r):
        n0, n1 = batch(r, *ring)
        one = lo_ref[:, pl.ds(pl.multiple_of(n0 * LANES, LANES), LANES)].astype(F32)
        two = lo_ref[:, pl.ds(pl.multiple_of(n1 * LANES, LANES), LANES)].astype(F32)
        low = jnp.where(c == 0, one, pltpu.roll(one, ROWS, 1))
        high = jnp.where(c == 0, pltpu.roll(two, ROWS, 1), two)
        lows = jnp.where(low_lanes, low, high).astype(jnp.int32)
        places = c * ROWS + jnp.where(low_lanes, n0 * LANES + lane, n1 * LANES + lane - ROWS)
        acc[...] = jnp.zeros_like(acc)

        def score(b, slot, seen):
            top = None
            for e in range(2):
                v = jnp.dot(keys[2 * b + e], q_ref[r], preferred_element_type=F32)
                v = jnp.concatenate(
                    [jnp.where(seen[e], v[:, h * LANES : (h + 1) * LANES], -jnp.inf) for h in range(4)],
                    axis=1,
                )
                sc[slot][e] = v
                peak = jnp.max(v.reshape(KT // 8, 8, 4 * LANES), axis=0)
                top = peak if top is None else jnp.maximum(top, peak)
            return jnp.max(top, axis=0, keepdims=True)

        def mix(b, slot):
            now = mx[0:1, :]
            total = acc[0 : HD + 16, :] * jnp.exp2(mx[1:2, :] - now)
            for e in range(2):
                p = jnp.exp2(sc[slot][e] - now).astype(BF)
                total = total + jnp.dot(kv_ref[2 * b + e, HD:], p, preferred_element_type=F32)
            acc[0 : HD + 16, :] = total

        low = [kpos[e] for e in range(2)]
        top = score(s, 0, [(k >= lows - s * 1024) & (k <= places) for k in low])
        mx[0:1, :] = top
        mx[1:2, :] = top

        @pl.when(n == 0)
        def _():
            relay(1)
            for k in range(2):
                for e in (1, 2, 3):

                    @pl.when(s >= e)
                    def _():
                        from_earlier(e, k, 1 - c, rsend, rrecv).wait_recv()

            lax.fori_loop(0, 2 * s, upright, 0)

        for i in range(3):

            @pl.when(s > i)
            def _():
                b = s - 1 - i
                mix(b + 1, i % 2)
                top = score(b, 1 - i % 2, [kpos[e] >= lows - b * 1024 for e in range(2)])
                now = mx[0:1, :]
                mx[1:2, :] = now
                mx[0:1, :] = jnp.maximum(now, top)

        for i in range(2):

            @pl.when(lax.rem(s, 2) == i)
            def _():
                mix(0, i)

        heads = acc[...] / acc[HD : HD + 1, :]
        for h in range(4):
            hv[:, h * LANES : (h + 1) * LANES] = heads[:, h * LANES : (h + 1) * LANES].T.astype(BF)

    rs = Scatter(part, o1, i1, s1, r1)

    def project(n, _):
        r = jnp.where(n < 2, n + 2, 3 - n)
        attend(n, r)

        @pl.when(n == 0)
        def _():
            for copy in local[3:5]:
                copy.wait()
            for copy in shared[1:3]:
                copy.wait_recv()

        part[r] = jnp.dot(hv[...], wov[...], preferred_element_type=F32).reshape(2, ROWS, D)

        @pl.when(n == 0)
        def _():
            rs.sides()

        @pl.when(n == 1)
        def _():
            rs.across()

        @pl.when(n == 2)
        def _():
            rs.plain()

        return 0

    lax.fori_loop(0, 4, project, 0)
    rs.rest()
    ag = Gather(buf, g2s, g2r)
    for i in range(NP):
        rows = pl.ds(i * PIECE, PIECE)
        total = tok[rows, :].astype(F32) + rs.final(i)
        res[rows, :] = total
        buf[chip, rows, :] = normed(total, gain2[...].reshape(1, D))
        ag.first(i)
    for copy in local[5:]:
        copy.wait()
    for copy in shared[3:]:
        copy.wait_recv()

    def turn(n, _):
        cols = pl.ds(pl.multiple_of(n * 256, 256), 256)
        for e in range(2):
            wt[cols, e * WIDE : (e + 1) * WIDE] = raw[e, :, cols].astype(F32).T.astype(BF)
        return 0

    lax.fori_loop(0, D // 256, turn, 0)
    rs.finish()

    rs2 = Scatter(part, o1, i2, s2, r2)
    ag.second()
    ag.third()

    def feed(r, _):
        @pl.when(r == 1)
        def _():
            ag.near_own()

        @pl.when(r == 2)
        def _():
            ag.fourth()
            ag.near_partner()

        @pl.when(r == 3)
        def _():
            rs2.sides()
            ag.far()

        n0, n1 = batch(r, *ring)
        both = jnp.concatenate([buf[n0], buf[n1]], axis=0)
        wide = jnp.dot(both, wt[...], preferred_element_type=F32)
        gate, up = wide[:, :WIDE], wide[:, WIDE:]
        hid = (gate / (1.0 + jnp.exp(-gate)) * up).astype(BF)
        part[r] = jnp.dot(hid, ds[...], preferred_element_type=F32).reshape(2, ROWS, D)
        return 0

    lax.fori_loop(0, 4, feed, 0)
    rs2.across()
    rs2.plain()
    rs2.rest()
    for i in range(NP):
        rows = pl.ds(i * PIECE, PIECE)
        out[rows, :] = (res[rows, :] + rs2.final(i)).astype(BF)
    ag.finish()
    rs2.finish()
    for k in range(2):
        to_sibling(k, c).wait_send()
        for e in (1, 2, 3):

            @pl.when(s + e < 4)
            def _():
                to_later(e, k).wait_send()

            @pl.when(s >= e)
            def _():
                from_earlier(e, k, c, rsend, rrecv).wait_send()

    for k, where in enumerate(others):
        handed[k].wait_send()
        back = lax.rem(s - (k + 1) // 2 + 4, 4) * 2 + lax.rem(d - (k + 1) % 2 + 2, 2)
        pltpu.make_async_remote_copy(
            src_ref=outg.at[pl.ds(back * PAIR, PAIR)],
            dst_ref=dc.at[pl.ds(back * PAIR, PAIR)],
            send_sem=hsend.at[k],
            recv_sem=hrecv.at[k],
            device_id=where,
            device_id_type=MESH,
        ).wait_recv()
    keep.wait()
    for copy in shared:
        copy.wait_send()


def hand_on(a_in, b_in, a_out, b_out, a_vm, b_vm, sems):
    first = [
        pltpu.make_async_copy(a_in, a_vm, sems.at[0]),
        pltpu.make_async_copy(b_in, b_vm, sems.at[1]),
    ]
    second = [
        pltpu.make_async_copy(a_vm, a_out, sems.at[2]),
        pltpu.make_async_copy(b_vm, b_out, sems.at[3]),
    ]
    for copy in first:
        copy.start()
    for one, two in zip(first, second):
        one.wait()
        two.start()
    for copy in second:
        copy.wait()


VMEM_SPEC = pl.BlockSpec(memory_space=pltpu.VMEM)
SMEM_SPEC = pl.BlockSpec(memory_space=pltpu.SMEM)
HBM_SPEC = pl.BlockSpec(memory_space=pltpu.HBM)
DMA = pltpu.SemaphoreType.DMA


def shape(*dims, dtype=BF):
    return jax.ShapeDtypeStruct(dims, dtype)


def shards(
    tokens, attn_gain, w_query, w_key, w_value, w_out, mlp_gain, w_gate, w_up, w_down,
    positions, window_lo, cache_pool, req_len, req_owner, block_list,
):
    own_rows = tokens[0, 0]
    wq, wg, wu = w_query.T, w_gate.T, w_up.T

    layer_out, dc = pl.pallas_call(
        layer_kernel,
        out_shape=(shape(ROWS, D), shape(OWNERS * PAIR, 2, MAXLEN * HD)),
        in_specs=[VMEM_SPEC] * 6 + [SMEM_SPEC] * 3 + [HBM_SPEC] * 7,
        out_specs=(VMEM_SPEC, HBM_SPEC),
        scratch_shapes=[
            VM((8, ROWS, D), BF),
            VM((6 * HD, D), BF),
            VM((D, 2 * LANES), BF),
            VM((D, 2 * LANES), BF),
            VM((OWNERS * PAIR, 2, MAXLEN * HD), BF),
            VM((ROWS, D), F32),
            VM((4, 2, ROWS, D), F32),
            VM((LANES, 4 * LANES), BF),
            VM((4, LANES, 4 * LANES), BF),
            VM((TILES, 2 * HD + 16, KT), BF),
            VM((TILES, KT, LANES), BF),
            VM((2, KT, LANES), jnp.int32),
            VM((2, KT, 4 * LANES), F32),
            VM((2, KT, 4 * LANES), F32),
            VM((8, 4 * LANES), F32),
            VM((LANES, 4 * LANES), F32),
            VM((4 * LANES, D), BF),
            VM((2, WIDE, D), BF),
            VM((D, 2 * WIDE), BF),
            VM((WIDE, D), BF),
            VM((7, ROWS, D), BF),
            VM((7, ROWS, D), BF),
            VM((7, ROWS, D), BF),
            DMA((7, NP)),
            DMA((7, NP)),
            DMA((8,)),
            DMA((6,)),
            DMA((6,)),
            DMA((7,)),
            DMA((7,)),
            DMA,
            DMA((3, 2)),
            DMA((3, 2)),
            DMA((2,)),
            DMA((2,)),
            DMA((3, 2)),
            DMA((3, 2)),
        ]
        + [DMA((7, NP))] * 6,
        compiler_params=pltpu.CompilerParams(
            collective_id=0, has_side_effects=True, vmem_limit_bytes=GRANT
        ),
        name="layer",
    )(
        own_rows, attn_gain, mlp_gain, positions.reshape(1, 1024), window_lo.reshape(1, 1024),
        cache_pool.reshape(NB, 2, BT * HD), req_len.reshape(RQ), req_owner.reshape(RQ),
        block_list.reshape(NB), wq, w_key, w_value, w_out, wg, wu, w_down,
    )
    layer_out, dc = pl.pallas_call(
        hand_on,
        out_shape=(shape(*layer_out.shape), shape(*dc.shape)),
        in_specs=[HBM_SPEC] * 2,
        out_specs=(HBM_SPEC,) * 2,
        scratch_shapes=[VM(layer_out.shape, BF), VM(dc.shape, BF), DMA((4,))],
        compiler_params=pltpu.CompilerParams(vmem_limit_bytes=GRANT),
        name="hand_on",
    )(layer_out, dc)
    return (
        layer_out.reshape(1, 1, ROWS, D),
        dc.reshape(OWNERS * PAIR, 2, 1, MAXLEN * HD),
    )


def solution(mesh):
    in_specs = (
        P("dec", "seq", "tensor", None),
        P(),
        P(None, "tensor"),
        P(),
        P(),
        P("tensor", None),
        P(),
        P(None, "tensor"),
        P(None, "tensor"),
        P("tensor", None),
        P("dec", "seq", None),
        P("dec", "seq", None),
        P(("seq", "dec"), None, "tensor", None),
        P(("seq", "dec"), None),
        P(("seq", "dec"), None),
        P(("seq", "dec"), None),
    )
    out_specs = (P("dec", "seq", "tensor", None), P(("seq", "dec"), None, "tensor", None))
    return jax.shard_map(shards, mesh=mesh, in_specs=in_specs, out_specs=out_specs, check_vma=False)
```

```python
import functools

import jax
import jax.numpy as jnp
from jax import lax
from jax.experimental import pallas as pl
from jax.experimental.pallas import tpu as pltpu
from jax.sharding import PartitionSpec as P

HD = 80
D = 2560
BT = 16
MAXLEN = 128
PAIR = 2
RQ = 8
NB = 40
UN = 432
WIDE = 896
ROWS = 64
NP = 4
PIECE = ROWS // NP
LANES = 128
KT = 512
TILES = 8
GRANT = 60 << 20
OWNERS = 8

MESH = pl.DeviceIdType.MESH
VM = pltpu.VMEM
norm_eps = 1e-05
LOG_BASE = 9.210340371976184
SCALE = HD**-0.5 * 1.4426950408889634
F32 = jnp.float32
BF = jnp.bfloat16


def place():
    t = lax.axis_index("tensor")
    return lax.div(t, 4), lax.rem(lax.div(t, 2), 2), lax.rem(t, 2)


def at_chip(x, yh, c):
    return {"tensor": (lax.rem(x + 4, 4) * 2 + yh) * 2 + c}


def col4(x):
    return lax.rem(x + 4, 4)


def batch(r, own, ca, cb, co, m):
    c0 = jnp.where(r == 0, own, jnp.where(r == 3, co, cb))
    c1 = jnp.where(r == 0, own, jnp.where(r == 3, co, ca))
    r0 = jnp.where(r == 2, 1 - m, m)
    r1 = jnp.where(r == 1, m, 1 - m)
    return c0 * 2 + r0, c1 * 2 + r1


def normed(values, gain):
    mean_square = jnp.mean(values * values, axis=-1, keepdims=True)
    return (values * lax.rsqrt(mean_square + norm_eps) * gain).astype(BF)


class Gather:
    def __init__(self, buf, send, recv):
        self.x, self.yh, self.c = place()
        self.buf, self.send, self.recv = buf, send, recv
        x, m, c, p = self.x, self.yh, self.c, 1 - self.yh
        self.a, self.b, self.o = at_chip(x + 1, m, c), at_chip(x - 1, m, c), at_chip(x, p, c)
        own, ca, cb, co = col4(x), col4(x + 1), col4(x - 1), col4(x + 2)
        self.plan = [
            (own * 2 + m, self.o, own * 2 + p),
            (own * 2 + m, self.a, cb * 2 + m),
            (own * 2 + m, self.b, ca * 2 + m),
            (own * 2 + p, self.a, cb * 2 + p),
            (own * 2 + p, self.b, ca * 2 + p),
            (cb * 2 + m, self.a, co * 2 + m),
            (co * 2 + m, self.o, co * 2 + p),
            (ca * 2 + m, self.b, co * 2 + m),
        ]

    def copy(self, k, i, got):
        plan = self.plan[7 if k == 5 and i >= NP // 2 else k]
        part = self.buf.at[plan[2] if got else plan[0], pl.ds(i * PIECE, PIECE)]
        return pltpu.make_async_remote_copy(
            src_ref=part,
            dst_ref=part,
            send_sem=self.send.at[k, i],
            recv_sem=self.recv.at[k, i],
            device_id=plan[1],
            device_id_type=MESH,
        )

    def start(self, k, i):
        self.copy(k, i, False).start()

    def got(self, k, i):
        self.copy(k, i, True).wait_recv()

    def first(self, i):
        self.start(1, i)
        self.start(2, i)
        self.start(0, i)

    def second(self):
        for i in range(NP // 2):
            self.got(1, i)
            self.start(5, i)
            self.got(2, NP - 1 - i)
            self.start(5, NP - 1 - i)

    def third(self):
        for i in range(NP):
            self.got(0, i)
            self.start(3, i)
            self.start(4, i)

    def fourth(self):
        for i in range(NP // 2):
            for e in (i, NP - 1 - i):
                self.got(5, e)
                self.start(6, e)

    def near_own(self):
        for i in range(NP // 2):
            self.got(1, NP - 1 - i)
            self.got(2, i)

    def near_partner(self):
        for i in range(NP):
            self.got(3, i)
            self.got(4, i)

    def far(self):
        for i in range(NP):
            self.got(6, i)

    def finish(self):
        for k in range(7):
            for i in range(NP):
                self.copy(k, i, False).wait_send()


class Scatter:
    def __init__(self, part, out, inb, send, recv):
        x, yh, c = place()
        self.part, self.out, self.inb, self.send, self.recv = part, out, inb, send, recv
        self.a, self.b = at_chip(x + 1, yh, c), at_chip(x - 1, yh, c)
        o = at_chip(x, 1 - yh, c)
        self.to = [o, self.a, self.b, None, self.a, self.b, o]

    def copy(self, k, i):
        rows = pl.ds(i * PIECE, PIECE)
        to = self.to[k] if k != 3 else (self.a if i < NP // 2 else self.b)
        return pltpu.make_async_remote_copy(
            src_ref=self.out.at[k, rows],
            dst_ref=self.inb.at[k, rows],
            send_sem=self.send.at[k, i],
            recv_sem=self.recv.at[k, i],
            device_id=to,
            device_id_type=MESH,
        )

    def summed(self, part, i, adds):
        rows = pl.ds(i * PIECE, PIECE)
        total = self.part[part[0], part[1], rows, :]
        for e in adds:
            self.copy(e, i).wait_recv()
            total = total + self.inb[e, rows, :].astype(F32)
        return total

    def put(self, k, part, i, adds=()):
        self.out[k, pl.ds(i * PIECE, PIECE), :] = self.summed(part, i, adds).astype(BF)
        self.copy(k, i).start()

    def sides(self):
        for i in range(NP):
            self.put(1, (2, 1), i)
            self.put(2, (2, 0), i)

    def across(self):
        for i in range(NP // 2):
            self.put(0, (3, 1), i)
            self.put(0, (3, 1), NP - 1 - i)

    def plain(self):
        for i in range(NP // 2):
            self.put(4, (1, 1), NP - 1 - i)
            self.put(5, (1, 0), i)

    def rest(self):
        for i in range(NP // 2):
            self.put(3, (3, 0), i, (0,))
            self.put(3, (3, 0), NP - 1 - i, (0,))
        for i in range(NP):
            self.put(6, (0, 1), i, (1, 2))
        for i in range(NP // 2):
            self.put(4, (1, 1), i, (3,))
            self.put(5, (1, 0), NP - 1 - i, (3,))

    def final(self, i):
        return self.summed((0, 0), i, (6, 4, 5))

    def finish(self):
        for k in range(7):
            for i in range(NP):
                self.copy(k, i).wait_send()


def signal(where):
    pl.semaphore_signal(
        pltpu.get_barrier_semaphore(), inc=1, device_id=where, device_id_type=MESH
    )


def dot_nt(left, right):
    return lax.dot_general(left, right, (((1,), (1,)), ((), ())), preferred_element_type=F32)


def layer_kernel(
    tok, gain, gain2, pos, lo_ref, pool, lens, owners, listing, wq, wk, wv, wo, wg, wu, wd,
    out, dc,
    buf, wall, wkw, wvw, outg, res, part, hv, q_ref, kv_ref, keys, kpos, sc0, sc1, mx, acc,
    wov, raw, wt, ds, o1, i1, i2,
    ag_send, ag_recv, lsem, wsend, wrecv, hsend, hrecv, hlocal,
    zsend, zrecv, ssend, srecv, rsend, rrecv, g2s, g2r, s1, r1, s2, r2,
):
    x, yh, c = place()
    s, d = lax.axis_index("seq"), lax.axis_index("dec")
    chip = x * 2 + yh
    sib = at_chip(x, yh, 1 - c)
    start = jnp.minimum(lax.div(chip * HD, LANES), 3) * LANES
    off = chip * HD - start
    cols = pl.ds(pl.multiple_of(start, LANES), 2 * LANES)
    local = [
        pltpu.make_async_copy(wq, wall.at[pl.ds(0, 2 * HD)], lsem.at[0]),
        pltpu.make_async_copy(wk.at[:, cols], wkw, lsem.at[1]),
        pltpu.make_async_copy(wv.at[:, cols], wvw, lsem.at[2]),
        pltpu.make_async_copy(wo.at[pl.ds(0, HD)], wov.at[pl.ds(0, HD)], lsem.at[3]),
        pltpu.make_async_copy(wo.at[pl.ds(HD, HD)], wov.at[pl.ds(LANES, HD)], lsem.at[4]),
        pltpu.make_async_copy(wg, raw.at[0, pl.ds(0, UN)], lsem.at[5]),
        pltpu.make_async_copy(wu, raw.at[1, pl.ds(0, UN)], lsem.at[6]),
        pltpu.make_async_copy(wd, ds.at[pl.ds(0, UN)], lsem.at[7]),
    ]
    for copy in local:
        copy.start()
    ag = Gather(buf, ag_send, ag_recv)
    for where in (ag.a, ag.b, ag.o, sib):
        signal(where)
    others = []
    for k in range(1, OWNERS):
        others.append({"seq": lax.rem(s + k // 2, 4), "dec": lax.rem(d + k % 2, 2)})
    for where in others:
        signal(where)
    buf[chip] = normed(tok[...].astype(F32), gain[...].reshape(1, D))
    pl.semaphore_wait(pltpu.get_barrier_semaphore(), 4 + len(others))
    for i in range(NP):
        ag.first(i)
    shared = [
        pltpu.make_async_remote_copy(
            src_ref=a, dst_ref=b, send_sem=wsend.at[k], recv_sem=wrecv.at[k],
            device_id=sib, device_id_type=MESH,
        )
        for k, (a, b) in enumerate(
            (
                (wq, wall.at[pl.ds(2 * HD, 2 * HD)]),
                (wo.at[pl.ds(0, HD)], wov.at[pl.ds(2 * LANES, HD)]),
                (wo.at[pl.ds(HD, HD)], wov.at[pl.ds(3 * LANES, HD)]),
                (wg, raw.at[0, pl.ds(UN, UN)]),
                (wu, raw.at[1, pl.ds(UN, UN)]),
                (wd, ds.at[pl.ds(UN, UN)]),
            )
        )
    ]
    for copy in shared:
        copy.start()

    counts = [lax.div(lens[k] + (BT - 1), BT) for k in range(RQ)]
    firsts, so_far = [], jnp.int32(0)
    for k in range(RQ):
        firsts.append(so_far)
        so_far = so_far + counts[k]
    ranks = []
    for k in range(RQ):
        rank = jnp.int32(0)
        for e in range(k):
            rank = rank + (owners[e] == owners[k]).astype(jnp.int32)
        ranks.append(rank)
    feature = lax.broadcasted_iota(jnp.int32, (2, BT * HD), 1)

    def cut(o, _):
        for r in range(PAIR):
            at, length = jnp.int32(0), jnp.int32(0)
            for k in range(RQ):
                hit = (owners[k] == o) & (ranks[k] == r)
                at = jnp.where(hit, firsts[k], at)
                length = jnp.where(hit, lens[k], length)
            for b in range(MAXLEN // BT):
                block = pool[listing[jnp.minimum(at + b, NB - 1)]].astype(F32)
                kept = jnp.where(feature < (length - BT * b) * HD, block, 0.0)
                outg[o * PAIR + r, :, BT * HD * b : BT * HD * (b + 1)] = kept.astype(BF)
        return 0

    lax.fori_loop(0, OWNERS, cut, 0)
    me = s * 2 + d
    handed = []
    for k, where in enumerate(others):
        there = where["seq"] * 2 + where["dec"]
        handed.append(
            pltpu.make_async_remote_copy(
                src_ref=outg.at[pl.ds(there * PAIR, PAIR)],
                dst_ref=dc.at[pl.ds(me * PAIR, PAIR)],
                send_sem=hsend.at[k],
                recv_sem=hrecv.at[k],
                device_id=where,
                device_id_type=MESH,
            )
        )
    keep = pltpu.make_async_copy(
        outg.at[pl.ds(me * PAIR, PAIR)], dc.at[pl.ds(me * PAIR, PAIR)], hlocal
    )
    ag.second()
    for k in (1, 3, 5, 0, 2):
        handed[k].start()
    keep.start()

    row = lax.broadcasted_iota(jnp.int32, (HD, 2 * LANES), 0)
    col = lax.broadcasted_iota(jnp.int32, (HD, 2 * LANES), 1)
    pick = (col == row + off).astype(F32).astype(BF)
    chunk = 512

    def laid(src, begin):
        def one(i, _):
            rows = pl.ds(pl.multiple_of(i * chunk, chunk), chunk)
            wall[begin : begin + HD, rows] = dot_nt(pick, src[rows, :]).astype(BF)
            return 0

        lax.fori_loop(0, D // chunk, one, 0)

    for copy in local[:3]:
        copy.wait()
    laid(wkw, 4 * HD)
    laid(wvw, 5 * HD)
    half = HD // 2
    rate = jnp.exp(
        lax.broadcasted_iota(jnp.int32, (half, 1), 0).astype(F32) * (-2.0 / HD * LOG_BASE)
    )
    low_lanes = lax.broadcasted_iota(jnp.int32, (1, LANES), 1) < ROWS

    def own_half(two, one_more):
        low = jnp.where(c == 0, two, pltpu.roll(two, ROWS, 1))
        high = jnp.where(c == 0, pltpu.roll(one_more, ROWS, 1), one_more)
        return jnp.where(low_lanes, low, high)

    def lanes_of(core):
        return pl.ds(pl.multiple_of(core * 256, 256), 256)

    def moved(src, dst, send, recv, where):
        return pltpu.make_async_remote_copy(
            src_ref=src, dst_ref=dst, send_sem=send, recv_sem=recv, device_id=where, device_id_type=MESH
        )

    def piece(sq, k, core):
        return kv_ref.at[sq * 2 + k, pl.ds(0, 2 * HD), lanes_of(core)]

    def to_later(e, k):
        own = piece(s, k, c)
        return moved(own, own, zsend.at[e - 1, k], zrecv.at[e - 1, k], {"seq": lax.rem(s + e, 4)})

    def to_sibling(k, core):
        own = piece(s, k, core)
        return moved(own, own, ssend.at[k], srecv.at[k], sib)

    def from_earlier(e, k, core, send, recv):
        there = piece(lax.rem(s - e + 4, 4), k, core)
        return moved(there, there, send.at[e - 1, k], recv.at[e - 1, k], sib)

    def relay(k):
        for e in (1, 2, 3):

            @pl.when(s >= e)
            def _():
                from_earlier(e, k, c, zsend, zrecv).wait_recv()
                from_earlier(e, k, c, rsend, rrecv).start()

    def rotated(v, cosine, sine):
        a, b = v[:half], v[half:]
        return jnp.concatenate([a * cosine - b * sine, b * cosine + a * sine], axis=0)

    def chip_lanes(ref, n):
        return ref[:, pl.ds(pl.multiple_of(n * LANES, LANES), LANES)].astype(F32)

    def make(k, _):
        @pl.when(k == 0)
        def _():
            ag.third()
            shared[0].wait_recv()
            ag.near_own()

        @pl.when(k == 1)
        def _():
            ag.fourth()
            for e in (4, 6):
                handed[e].start()
            ag.near_partner()
            ag.far()
            relay(0)

        four = []
        for r in (2 * k, 2 * k + 1):
            four += list(batch(r, x, col4(x + 1), col4(x - 1), col4(x + 2), yh))
        shards_in = jnp.concatenate([buf[n] for n in four], axis=0)
        made = dot_nt(wall[...], shards_in)
        places = jnp.concatenate(
            [
                own_half(chip_lanes(pos, four[0]), chip_lanes(pos, four[1])),
                own_half(chip_lanes(pos, four[2]), chip_lanes(pos, four[3])),
            ],
            axis=1,
        )
        angles = rate * places
        cosine, sine = jnp.cos(angles), jnp.sin(angles)
        kv_ref[s * 2 + k, 0:HD, lanes_of(c)] = rotated(made[4 * HD : 5 * HD], cosine, sine).astype(BF)
        kv_ref[s * 2 + k, HD : 2 * HD, lanes_of(c)] = made[5 * HD :].astype(BF)
        for e in (1, 2, 3):

            @pl.when(s + e < 4)
            def _():
                to_later(e, k).start()

        to_sibling(k, c).start()
        for h in range(4):
            v = (rotated(made[h * HD : (h + 1) * HD], cosine, sine) * SCALE).astype(BF)
            for n in range(2):
                q_ref[2 * k + n, 0:HD, h * LANES : (h + 1) * LANES] = v[:, n * LANES : (n + 1) * LANES]
        return 0

    for h in range(4):
        wov[h * LANES + HD : (h + 1) * LANES, :] = jnp.zeros((LANES - HD, D), BF)
    raw[:, 2 * UN :, :] = jnp.zeros((2, WIDE - 2 * UN, D), BF)
    ds[2 * UN :, :] = jnp.zeros((WIDE - 2 * UN, D), BF)
    sc = (sc0, sc1)
    m = yh
    ring = (x, col4(x + 1), col4(x - 1), col4(x + 2), m)
    row = lax.broadcasted_iota(jnp.int32, (2 * LANES, LANES), 0)
    quarter, spot = lax.div(row, ROWS), lax.rem(row, ROWS)
    for e in range(2):
        chips = batch(2 * e, *ring) + batch(2 * e + 1, *ring)
        which = jnp.where(
            quarter < 2, jnp.where(quarter == 0, chips[0], chips[1]), jnp.where(quarter == 2, chips[2], chips[3])
        )
        for core in range(2):
            kpos[e, core * 256 : core * 256 + 256] = which * LANES + core * ROWS + spot
    ones = lax.broadcasted_iota(jnp.int32, (TILES, 16, KT), 1) == 0
    kv_ref[:, 2 * HD :, :] = ones.astype(F32).astype(BF)
    q_ref[:, HD:, :] = jnp.zeros((4, LANES - HD, 4 * LANES), BF)
    lane = lax.broadcasted_iota(jnp.int32, (1, LANES), 1)

    lax.fori_loop(0, 2, make, 0)
    def upright(t, _):
        k = kv_ref[t, 0:HD].astype(F32)
        k = jnp.concatenate([k, jnp.zeros((LANES - HD, KT), F32)], axis=0)
        keys[t] = k.T.astype(BF)
        return 0

    for k in range(2):
        to_sibling(k, 1 - c).wait_recv()
    lax.fori_loop(2 * s, 2 * s + 2, upright, 0)
    ag.finish()

    def attend(n, r):
        n0, n1 = batch(r, *ring)
        one = lo_ref[:, pl.ds(pl.multiple_of(n0 * LANES, LANES), LANES)].astype(F32)
        two = lo_ref[:, pl.ds(pl.multiple_of(n1 * LANES, LANES), LANES)].astype(F32)
        low = jnp.where(c == 0, one, pltpu.roll(one, ROWS, 1))
        high = jnp.where(c == 0, pltpu.roll(two, ROWS, 1), two)
        lows = jnp.where(low_lanes, low, high).astype(jnp.int32)
        places = c * ROWS + jnp.where(low_lanes, n0 * LANES + lane, n1 * LANES + lane - ROWS)
        acc[...] = jnp.zeros_like(acc)

        def score(b, slot, seen):
            top = None
            for e in range(2):
                v = jnp.dot(keys[2 * b + e], q_ref[r], preferred_element_type=F32)
                v = jnp.concatenate(
                    [jnp.where(seen[e], v[:, h * LANES : (h + 1) * LANES], -jnp.inf) for h in range(4)],
                    axis=1,
                )
                sc[slot][e] = v
                peak = jnp.max(v.reshape(KT // 8, 8, 4 * LANES), axis=0)
                top = peak if top is None else jnp.maximum(top, peak)
            return jnp.max(top, axis=0, keepdims=True)

        def mix(b, slot):
            now = mx[0:1, :]
            total = acc[0 : HD + 16, :] * jnp.exp2(mx[1:2, :] - now)
            for e in range(2):
                p = jnp.exp2(sc[slot][e] - now).astype(BF)
                total = total + jnp.dot(kv_ref[2 * b + e, HD:], p, preferred_element_type=F32)
            acc[0 : HD + 16, :] = total

        low = [kpos[e] for e in range(2)]
        top = score(s, 0, [(k >= lows - s * 1024) & (k <= places) for k in low])
        mx[0:1, :] = top
        mx[1:2, :] = top

        @pl.when(n == 0)
        def _():
            relay(1)
            for k in range(2):
                for e in (1, 2, 3):

                    @pl.when(s >= e)
                    def _():
                        from_earlier(e, k, 1 - c, rsend, rrecv).wait_recv()

            lax.fori_loop(0, 2 * s, upright, 0)

        for i in range(3):

            @pl.when(s > i)
            def _():
                b = s - 1 - i
                mix(b + 1, i % 2)
                top = score(b, 1 - i % 2, [kpos[e] >= lows - b * 1024 for e in range(2)])
                now = mx[0:1, :]
                mx[1:2, :] = now
                mx[0:1, :] = jnp.maximum(now, top)

        for i in range(2):

            @pl.when(lax.rem(s, 2) == i)
            def _():
                mix(0, i)

        heads = acc[...] / acc[HD : HD + 1, :]
        for h in range(4):
            hv[:, h * LANES : (h + 1) * LANES] = heads[:, h * LANES : (h + 1) * LANES].T.astype(BF)

    rs = Scatter(part, o1, i1, s1, r1)

    def project(n, _):
        r = jnp.where(n < 2, n + 2, 3 - n)
        attend(n, r)

        @pl.when(n == 0)
        def _():
            for copy in local[3:5]:
                copy.wait()
            for copy in shared[1:3]:
                copy.wait_recv()

        part[r] = jnp.dot(hv[...], wov[...], preferred_element_type=F32).reshape(2, ROWS, D)

        @pl.when(n == 0)
        def _():
            rs.sides()

        @pl.when(n == 1)
        def _():
            rs.across()

        @pl.when(n == 2)
        def _():
            rs.plain()

        return 0

    lax.fori_loop(0, 4, project, 0)
    rs.rest()
    ag = Gather(buf, g2s, g2r)
    for i in range(NP):
        rows = pl.ds(i * PIECE, PIECE)
        total = tok[rows, :].astype(F32) + rs.final(i)
        res[rows, :] = total
        buf[chip, rows, :] = normed(total, gain2[...].reshape(1, D))
        ag.first(i)
    for copy in local[5:]:
        copy.wait()
    for copy in shared[3:]:
        copy.wait_recv()

    def turn(n, _):
        cols = pl.ds(pl.multiple_of(n * 256, 256), 256)
        for e in range(2):
            wt[cols, e * WIDE : (e + 1) * WIDE] = raw[e, :, cols].astype(F32).T.astype(BF)
        return 0

    lax.fori_loop(0, D // 256, turn, 0)
    rs.finish()

    rs2 = Scatter(part, o1, i2, s2, r2)
    ag.second()
    ag.third()

    def feed(r, _):
        @pl.when(r == 1)
        def _():
            ag.near_own()

        @pl.when(r == 2)
        def _():
            ag.fourth()
            ag.near_partner()
            rs2.plain()

        @pl.when(r == 3)
        def _():
            rs2.sides()
            ag.far()

        n0, n1 = batch(r, *ring)
        both = jnp.concatenate([buf[n0], buf[n1]], axis=0)
        wide = jnp.dot(both, wt[...], preferred_element_type=F32)
        gate, up = wide[:, :WIDE], wide[:, WIDE:]
        hid = (gate / (1.0 + jnp.exp(-gate)) * up).astype(BF)
        part[r] = jnp.dot(hid, ds[...], preferred_element_type=F32).reshape(2, ROWS, D)
        return 0

    lax.fori_loop(0, 4, feed, 0)
    rs2.across()
    rs2.rest()
    for i in range(NP):
        rows = pl.ds(i * PIECE, PIECE)
        out[rows, :] = (res[rows, :] + rs2.final(i)).astype(BF)
    ag.finish()
    rs2.finish()
    for k in range(2):
        to_sibling(k, c).wait_send()
        for e in (1, 2, 3):

            @pl.when(s + e < 4)
            def _():
                to_later(e, k).wait_send()

            @pl.when(s >= e)
            def _():
                from_earlier(e, k, c, rsend, rrecv).wait_send()

    for k, where in enumerate(others):
        handed[k].wait_send()
        back = lax.rem(s - (k + 1) // 2 + 4, 4) * 2 + lax.rem(d - (k + 1) % 2 + 2, 2)
        pltpu.make_async_remote_copy(
            src_ref=outg.at[pl.ds(back * PAIR, PAIR)],
            dst_ref=dc.at[pl.ds(back * PAIR, PAIR)],
            send_sem=hsend.at[k],
            recv_sem=hrecv.at[k],
            device_id=where,
            device_id_type=MESH,
        ).wait_recv()
    keep.wait()
    for copy in shared:
        copy.wait_send()


def hand_on(a_in, b_in, a_out, b_out, a_vm, b_vm, sems):
    first = [
        pltpu.make_async_copy(a_in, a_vm, sems.at[0]),
        pltpu.make_async_copy(b_in, b_vm, sems.at[1]),
    ]
    second = [
        pltpu.make_async_copy(a_vm, a_out, sems.at[2]),
        pltpu.make_async_copy(b_vm, b_out, sems.at[3]),
    ]
    for copy in first:
        copy.start()
    for one, two in zip(first, second):
        one.wait()
        two.start()
    for copy in second:
        copy.wait()


VMEM_SPEC = pl.BlockSpec(memory_space=pltpu.VMEM)
SMEM_SPEC = pl.BlockSpec(memory_space=pltpu.SMEM)
HBM_SPEC = pl.BlockSpec(memory_space=pltpu.HBM)
DMA = pltpu.SemaphoreType.DMA


def shape(*dims, dtype=BF):
    return jax.ShapeDtypeStruct(dims, dtype)


def shards(
    tokens, attn_gain, w_query, w_key, w_value, w_out, mlp_gain, w_gate, w_up, w_down,
    positions, window_lo, cache_pool, req_len, req_owner, block_list,
):
    own_rows = tokens[0, 0]
    wq, wg, wu = w_query.T, w_gate.T, w_up.T

    layer_out, dc = pl.pallas_call(
        layer_kernel,
        out_shape=(shape(ROWS, D), shape(OWNERS * PAIR, 2, MAXLEN * HD)),
        in_specs=[VMEM_SPEC] * 6 + [SMEM_SPEC] * 3 + [HBM_SPEC] * 7,
        out_specs=(VMEM_SPEC, HBM_SPEC),
        scratch_shapes=[
            VM((8, ROWS, D), BF),
            VM((6 * HD, D), BF),
            VM((D, 2 * LANES), BF),
            VM((D, 2 * LANES), BF),
            VM((OWNERS * PAIR, 2, MAXLEN * HD), BF),
            VM((ROWS, D), F32),
            VM((4, 2, ROWS, D), F32),
            VM((LANES, 4 * LANES), BF),
            VM((4, LANES, 4 * LANES), BF),
            VM((TILES, 2 * HD + 16, KT), BF),
            VM((TILES, KT, LANES), BF),
            VM((2, KT, LANES), jnp.int32),
            VM((2, KT, 4 * LANES), F32),
            VM((2, KT, 4 * LANES), F32),
            VM((8, 4 * LANES), F32),
            VM((LANES, 4 * LANES), F32),
            VM((4 * LANES, D), BF),
            VM((2, WIDE, D), BF),
            VM((D, 2 * WIDE), BF),
            VM((WIDE, D), BF),
            VM((7, ROWS, D), BF),
            VM((7, ROWS, D), BF),
            VM((7, ROWS, D), BF),
            DMA((7, NP)),
            DMA((7, NP)),
            DMA((8,)),
            DMA((6,)),
            DMA((6,)),
            DMA((7,)),
            DMA((7,)),
            DMA,
            DMA((3, 2)),
            DMA((3, 2)),
            DMA((2,)),
            DMA((2,)),
            DMA((3, 2)),
            DMA((3, 2)),
        ]
        + [DMA((7, NP))] * 6,
        compiler_params=pltpu.CompilerParams(
            collective_id=0, has_side_effects=True, vmem_limit_bytes=GRANT
        ),
        name="layer",
    )(
        own_rows, attn_gain, mlp_gain, positions.reshape(1, 1024), window_lo.reshape(1, 1024),
        cache_pool.reshape(NB, 2, BT * HD), req_len.reshape(RQ), req_owner.reshape(RQ),
        block_list.reshape(NB), wq, w_key, w_value, w_out, wg, wu, w_down,
    )
    layer_out, dc = pl.pallas_call(
        hand_on,
        out_shape=(shape(*layer_out.shape), shape(*dc.shape)),
        in_specs=[HBM_SPEC] * 2,
        out_specs=(HBM_SPEC,) * 2,
        scratch_shapes=[VM(layer_out.shape, BF), VM(dc.shape, BF), DMA((4,))],
        compiler_params=pltpu.CompilerParams(vmem_limit_bytes=GRANT),
        name="hand_on",
    )(layer_out, dc)
    return (
        layer_out.reshape(1, 1, ROWS, D),
        dc.reshape(OWNERS * PAIR, 2, 1, MAXLEN * HD),
    )


def solution(mesh):
    in_specs = (
        P("dec", "seq", "tensor", None),
        P(),
        P(None, "tensor"),
        P(),
        P(),
        P("tensor", None),
        P(),
        P(None, "tensor"),
        P(None, "tensor"),
        P("tensor", None),
        P("dec", "seq", None),
        P("dec", "seq", None),
        P(("seq", "dec"), None, "tensor", None),
        P(("seq", "dec"), None),
        P(("seq", "dec"), None),
        P(("seq", "dec"), None),
    )
    out_specs = (P("dec", "seq", "tensor", None), P(("seq", "dec"), None, "tensor", None))
    return jax.shard_map(shards, mesh=mesh, in_specs=in_specs, out_specs=out_specs, check_vma=False)
```
